32 devices in a mesh: mem: 2 (over y), row: 16 (over z, x, core).
Axes of the slice: x: 2, y: 2, z: 4, core: 2. Of those that a mesh axis runs over, the one named last changes fastest.
Arguments:
- members: bfloat16 [32, 8, 2, 128, 512], P('mem', None, None, 'row'), may hold values from -6 to 6
- static_scale: float32 [8, 2, 128, 512], P('mem', None, 'row'), may hold values from 0.3 to 1.5
- observed: float32 [8, 2, 128, 512], P('mem', None, 'row'), may hold values from -5 to 5, as said below
- huber_class: int32 [8, 2, 128, 512], P('mem', None, 'row'), may hold values from 0 to 3
- scale_index: int32 [2, 128, 512], P(None, 'row'), may hold values from 0 to 3
Outputs:
- control: float32 [32, 2, 128, 512], P('mem', None, 'row')
- static_control: float32 [8, 2, 128, 512], P('mem', None, 'row')
- increment: float32 [8, 2, 128, 512], P('mem', None, 'row')
The draws below stay inside these ranges and needn't reach their ends.
Inputs may be any that keep to these rules, and one draw needn't show every extreme that they name: observed departures of order one.
All inputs are finite; a program needn't handle non-finite values.
Results may differ from the reference program's by a relative error of at most 0.0035.
Values may be sent and summed in bfloat16 or wider, within the bound.
No kernel may reach another device: no remote copies, remote signals or barrier semaphores. Data moves between devices by JAX's collectives and lax.ppermute only.
A program may use at most 64 MiB of HBM per device.

```python
import math
import jax
import jax.numpy as jnp
from jax import lax

VARS = 8
LEVELS = 2
NX = 512
SWEEPS = 4
ITERS = 2
ENSEMBLE = 32
NY = 128


def draw_observed(key, part):
    first = jax.random.fold_in(jax.random.fold_in(key, 17), 0)
    row_frac = jnp.arange(NY, dtype=jnp.float32) / max(NY - 1, 1)
    var_frac = jnp.arange(VARS, dtype=jnp.float32) / max(VARS - 1, 1)
    scale = (0.5 + row_frac)[None, None, :, None] * (0.7 + 0.6 * var_frac)[:, None, None, None]
    value = jax.random.normal(first, (VARS, LEVELS, NY, NX), jnp.float32) * scale
    return jnp.clip(value, -5.0, 5.0)


def place_ends(array, rng, least, high):
    dims = array.shape
    index_at = [jax.random.randint(jax.random.fold_in(rng, axis), (), 0, dims[axis]) for axis in range(len(dims))]
    array = array.at[tuple(index_at)].set(least)
    longest = dims.index(max(dims))
    index_at[longest] = (index_at[longest] + 1) % dims[longest]
    return array.at[tuple(index_at)].set(high)


def levels(stream_key, extent, cuts, least, top_value):
    def one(position, parts):
        heights = jax.random.uniform(jax.random.fold_in(jax.random.fold_in(stream_key, 6), position), (parts,), jnp.float32, least / len(cuts), top_value / len(cuts))
        return jnp.repeat(jnp.exp(heights), extent[position] // parts).reshape((-1,) + (1,) * (len(extent) - position - 1))

    factor_of = one(*cuts[0])
    for cut in cuts[1:]:
        factor_of = factor_of * one(*cut)
    return factor_of


def scatter_about(own_key, dims, scale, most, cuts=(), kind=jnp.bfloat16):
    level = levels(own_key, dims, cuts, -0.22, 0.18) if cuts else 1.0
    array = jax.random.normal(own_key, dims, jnp.float32) * scale * level
    return jnp.minimum(jnp.maximum(array, -most), most).astype(kind)


def setup_inputs(seed: int = 0) -> dict:
    streams_of = jax.random.split(jax.random.key(seed), 6)
    members = scatter_about(streams_of[0], (ENSEMBLE, VARS, LEVELS, NY, NX), 1.0, 6.0, ((0, 2), (3, 16)))
    static_scale = jnp.clip(jnp.exp(math.log(1.5) - 1.60943787 * jax.random.uniform(streams_of[1], (VARS, LEVELS, NY, NX), jnp.float32) ** levels(streams_of[1], (VARS, LEVELS, NY, NX), ((0, 2), (2, 16)), -0.2, 0.2)), 0.3, 1.5)
    observed = draw_observed(jax.random.fold_in(streams_of[5], 71), 0)
    huber_class = place_ends(jax.random.randint(streams_of[3], (VARS, LEVELS, NY, NX), 0, 4), jax.random.fold_in(streams_of[3], 1), 0, 3).astype(jnp.int32)
    scale_index = place_ends(jax.random.randint(streams_of[4], (LEVELS, NY, NX), 0, 4), jax.random.fold_in(streams_of[4], 1), 0, 3).astype(jnp.int32)
    return dict(members=members, static_scale=static_scale, observed=observed, huber_class=huber_class, scale_index=scale_index)


kappa_table = (0.06, 0.11, 0.17, 0.23)
huber_levels = (1.0, 0.5, 1.0, 2.0)

def kappa_field(scale_index):
    result = jnp.zeros(scale_index.shape, jnp.float32)
    for level_id in range(4):
        result = result + jnp.where(scale_index == level_id, kappa_table[level_id], 0.0).astype(jnp.float32)
    return result

def threshold_field(huber_class):
    result = jnp.zeros(huber_class.shape, jnp.float32)
    for level_id in range(4):
        result = result + jnp.where(huber_class == level_id, huber_levels[level_id], 0.0).astype(jnp.float32)
    return result

def laplace(padded):
    full = jnp.pad(padded, [(0, 0)] * (padded.ndim - 1) + [(1, 1)])
    centre = full[..., 1:-1, 1:-1]
    vertical = full[..., 2:, 1:-1] + full[..., :-2, 1:-1]
    sideways = full[..., 1:-1, 2:] + full[..., 1:-1, :-2]
    return vertical + sideways - 4.0 * centre

def pad_rows(field):
    return jnp.pad(field, [(0, 0)] * (field.ndim - 2) + [(1, 1), (0, 0)])

def forward(field, kappa):
    for sweep in range(SWEEPS):
        field = field + kappa * laplace(pad_rows(field))
    return field

def adjoint(field, kappa):
    for sweep in range(SWEEPS):
        field = field + laplace(pad_rows(kappa * field))
    return field

def reference(members, static_scale, observed, huber_class, scale_index):
    kappa = kappa_field(scale_index)
    threshold = threshold_field(huber_class)
    observed_mask = (huber_class > 0).astype(jnp.float32)
    ens_coef = math.sqrt(0.7 / (ENSEMBLE - 1))
    stat_coef = math.sqrt(0.3)
    control = jnp.zeros((ENSEMBLE, LEVELS, NY, NX), jnp.float32)
    static_control = jnp.zeros((VARS, LEVELS, NY, NX), jnp.float32)
    increment = jnp.zeros((VARS, LEVELS, NY, NX), jnp.float32)
    for turn in range(ITERS):
        misfit = increment - observed
        clipped = observed_mask * jnp.clip(misfit, -threshold, threshold)
        weight = observed_mask * threshold / jnp.maximum(jnp.abs(misfit), threshold)
        sent = clipped.astype(jnp.bfloat16)
        sent_wide = sent.astype(jnp.float32)
        back = lax.map(lambda member: ens_coef * lax.optimization_barrier(jnp.sum(member.astype(jnp.float32) * sent_wide, axis=0)), members)
        grad_ens = control + lax.map(lambda field: adjoint(field, kappa), back)
        grad_stat = static_control + adjoint(stat_coef * static_scale * sent_wide, kappa)
        norm = jnp.sum(grad_ens * grad_ens) + jnp.sum(grad_stat * grad_stat)
        spread = lax.map(lambda field: forward(field, kappa), grad_ens).astype(jnp.bfloat16)

        def accumulate(total, pair):
            member, piece = pair
            return (total + member.astype(jnp.float32) * piece.astype(jnp.float32)[None], None)
        summed, unused = lax.scan(accumulate, jnp.zeros((VARS, LEVELS, NY, NX), jnp.float32), (members, spread))
        image = ens_coef * summed + stat_coef * static_scale * forward(grad_stat, kappa)
        curvature = jnp.sum(weight * image * image)
        step = norm / (norm + curvature)
        control = control - step * grad_ens
        static_control = static_control - step * grad_stat
        increment = increment - step * image
    return (control, static_control, increment)
```

```python
import functools
import math

import jax
import jax.numpy as jnp
from jax import lax
from jax.experimental import pallas as pl
from jax.experimental.pallas import tpu as pltpu
from jax.sharding import PartitionSpec as P

SWEEPS = 4
ITERS = 2
SUB = 8
LANES = 128
kappa_table = (0.06, 0.11, 0.17, 0.23)
huber_levels = (1.0, 0.5, 1.0, 2.0)
f32 = jnp.float32
bf16 = jnp.bfloat16


def table(index, values):
    result = jnp.full(index.shape, values[3], f32)
    for entry in range(3):
        result = jnp.where(index == entry, f32(values[entry]), result)
    return result


class Plan:
    def __init__(self, members, static_scale, mem, row):
        self.K, self.V, self.L, self.R, self.X = members.shape
        self.S = static_scale.shape[0]
        self.mem, self.row = mem, row
        self.devices = mem * row
        self.KT = -(-self.K // SUB)
        self.ST = -(-(self.S * self.L) // SUB)
        self.PM = self.L * self.KT
        self.PN = self.PM + self.ST
        self.F = self.K + self.S
        self.C = self.X // LANES
        self.RE = self.R + 4 * SWEEPS
        self.RG = self.R + 2 * SWEEPS
        self.pads = self.K % SUB != 0 or (self.S * self.L) % SUB != 0
        self.ens = math.sqrt(0.7 / (self.K * mem - 1))
        self.stat = math.sqrt(0.3)

    def slot(self, field, level):
        if field < self.K:
            return level * self.KT + field // SUB, field % SUB
        at = (field - self.K) * self.L + level
        return self.PM + at // SUB, at % SUB


def strided(start, count):
    return pl.ds(start, count, stride=SUB)


def scatter(ref, tile, where, value):
    for c in range(value.shape[1] // LANES):
        ref[tile, c, where, :] = value[:, c * LANES : (c + 1) * LANES]


def gather(ref, tile, where):
    return jnp.concatenate([ref[tile, c, where, :] for c in range(ref.shape[1])], axis=1)


def back_kernel(p, first, *refs):
    if first:
        members, static_scale, scale_index, obs, cls, obs_in, cls_in, back, msg, sent = refs
    else:
        members, static_scale, obs, cls, obs_in, cls_in, image, got, back, msg, step_out, sent = refs
    me = lax.axis_index("mem")
    if p.pads:
        back[...] = jnp.zeros(back.shape, f32)
    if not first:
        total = jnp.sum(got[...], axis=0, keepdims=True)
        norm = jnp.sum(total[:, :LANES], axis=1, keepdims=True)
        curvature = jnp.sum(total[:, LANES:], axis=1, keepdims=True)
        step = norm / (norm + curvature)
        step_out[...] = jnp.broadcast_to(step, step_out.shape)
    for shift in range(p.mem):
        base = lax.rem(me + (p.mem - shift), p.mem) * p.S
        for s in range(p.S):
            for l in range(p.L):
                if shift == 0:
                    seen, index = obs[s, l], cls[s, l]
                else:
                    seen, index = obs_in[shift - 1, s, l], cls_in[shift - 1, s, l]
                threshold = table(index, huber_levels)
                if first:
                    misfit = -seen
                else:
                    misfit = -(step * image[base + s, l]) - seen
                clipped = jnp.where(index > 0, jnp.clip(misfit, -threshold, threshold), 0.0)
                rounded = clipped.astype(bf16).astype(f32)
                sent[base + s, l] = rounded
                if shift == 0:
                    tile, lane = p.slot(p.K + s, l)
                    value = p.stat * static_scale[s, l] * rounded
                    scatter(back, tile, strided(lane, p.R), value)
                    msg[p.K + s, l] = value.astype(bf16)
    if first:
        for l in range(p.L):
            msg[p.F, l] = scale_index[l].astype(f32).astype(bf16)
    for l in range(p.L):
        for k in range(p.K):
            value = members[k, 0, l].astype(f32) * sent[0, l]
            for v in range(1, p.V):
                value = value + members[k, v, l].astype(f32) * sent[v, l]
            value = p.ens * value
            tile, lane = p.slot(k, l)
            scatter(back, tile, strided(lane, p.R), value)
            msg[k, l] = value.astype(bf16)


def sideways(u, first_lane, last_lane):
    right = [pltpu.roll(part, 1, 1) for part in u]
    left = [pltpu.roll(part, LANES - 1, 1) for part in u]
    zero = jnp.zeros_like(u[0])
    before, after = [zero] + right[:-1], left[1:] + [zero]
    return [
        jnp.where(first_lane, before[i], right[i]) + jnp.where(last_lane, after[i], left[i])
        for i in range(len(u))
    ]


def stencil(above, here, below, side):
    across = side(here)
    return [(above[c] + below[c]) + across[c] - 4.0 * here[c] for c in range(len(here))]


def sweep_kernel(p, first, *refs):
    if first:
        members, static_scale, scale_index, back, low, high, grad, kap, norm, part, lo, hi, a, b, out = refs
    else:
        members, static_scale, kap, before, step, back, low, high, grad, norm, part, lo, hi, a, b, out = refs
    me, at = lax.axis_index("mem"), lax.axis_index("row")
    low_ok = jnp.where(at > 0, 1.0, 0.0).astype(f32)
    high_ok = jnp.where(at < p.row - 1, 1.0, 0.0).astype(f32)
    R, RE, RG, W = p.R, p.RE, p.RG, SWEEPS
    H = 2 * W
    for ref, dst in ((low, lo), (high, hi)):
        if p.pads:
            dst[...] = jnp.zeros(dst.shape, f32)
        skip = R - H if ref is low else 0
        for field in range(p.F):
            for l in range(p.L):
                tile, lane = p.slot(field, l)
                scatter(dst, tile, strided(lane, H), ref[field, l].astype(f32)[skip : skip + H])
    if first:
        for l in range(p.L):
            pieces = (
                (table(low[p.F, l].astype(f32)[R - H :], kappa_table) * low_ok, 0),
                (table(scale_index[l].astype(f32), kappa_table), H),
                (table(high[p.F, l].astype(f32)[:H], kappa_table) * high_ok, H + R),
            )
            for value, offset in pieces:
                for r in range(value.shape[0]):
                    scatter(kap, l, pl.ds((offset + r) * SUB, SUB), jnp.broadcast_to(value[r : r + 1], (SUB, p.X)))
                for j in range(p.ST * SUB):
                    if (j % p.L) == l:
                        scatter(kap, p.L + j // SUB, strided(offset * SUB + j % SUB, value.shape[0]), value)
    lane = lax.broadcasted_iota(jnp.int32, (SUB, LANES), 1)
    first_lane, last_lane = lane == 0, lane == LANES - 1
    side = functools.partial(sideways, first_lane=first_lane, last_lane=last_lane)
    cols = range(p.C)

    def tiles(ref, r, *lead):
        return [ref[(*lead, c, pl.ds(r * SUB, SUB), slice(None))] for c in cols]

    def keep(value, ref, r, *lead):
        for c in cols:
            ref[(*lead, c, pl.ds(r * SUB, SUB), slice(None))] = value[c]

    if not first:
        step_tile = jnp.broadcast_to(step[0:1, 0:1], (SUB, LANES))

    def problem(t, total):
        which = jnp.where(t < p.PM, t // p.KT, t - p.PM + p.L)
        source = None
        for sweep in range(W):
            target = (a, b)[sweep % 2]
            held = []
            for r in range(sweep, RE - sweep):
                if sweep:
                    u = tiles(source, r)
                elif r < H:
                    u = tiles(lo, r, t)
                elif r < H + R:
                    u = tiles(back, r - H, t)
                else:
                    u = tiles(hi, r - H - R, t)
                factor = tiles(kap, r, which)
                w = [factor[c] * u[c] for c in cols]
                held = (held + [(u, w)])[-3:]
                if len(held) < 3:
                    continue
                (_, w0), (u1, w1), (_, w2) = held
                change = stencil(w0, w1, w2, side)
                value = [u1[c] + change[c] for c in cols]
                if sweep < W - 1:
                    keep(value, target, r - 1)
                    continue
                if not first:
                    earlier = tiles(before, r - 1 - W, t)
                    value = [value[c] - step_tile * earlier[c] for c in cols]
                if r - 1 < H:
                    value = [one * low_ok for one in value]
                elif r - 1 >= H + R:
                    value = [one * high_ok for one in value]
                else:
                    for one in value:
                        total = total + one * one
                keep(value, grad, r - 1 - W, t)
            source = target
        for sweep in range(W):
            target = (a, b)[sweep % 2]
            held = []
            for r in range(W + sweep, RE - W - sweep):
                u = tiles(source, r) if sweep else tiles(grad, r - W, t)
                held = (held + [u])[-3:]
                if len(held) < 3:
                    continue
                change = stencil(*held, side)
                factor = tiles(kap, r - 1, which)
                value = [held[1][c] + factor[c] * change[c] for c in cols]
                if sweep < W - 1:
                    keep(value, target, r - 1)
                else:
                    keep(value, out, r - 1 - H, t)
            source = target
        return total

    total = lax.fori_loop(0, p.PN, problem, jnp.zeros((SUB, LANES), f32))
    norm[...] = jnp.sum(total, axis=0, keepdims=True)
    for l in range(p.L):
        sums = [None] * p.V
        for k in range(p.K):
            tile, j = p.slot(k, l)
            spread = gather(out, tile, strided(j, R)).astype(bf16).astype(f32)
            for v in range(p.V):
                term = members[k, v, l].astype(f32) * spread
                sums[v] = term if k == 0 else sums[v] + term
        for v in range(p.V):
            part[v, l] = p.ens * sums[v]
    for s in range(p.S):
        for l in range(p.L):
            tile, j = p.slot(p.K + s, l)
            own = me * p.S + s
            part[own, l] = part[own, l] + p.stat * static_scale[s, l] * gather(out, tile, strided(j, R))


def curvature_kernel(p, first, *refs):
    if first:
        part, got, norm, obs, cls, image, send = refs
    else:
        part, got, norm, obs, cls, image_before, step, image, send = refs
    me = lax.axis_index("mem")
    if first:
        for v in range(p.V):
            for l in range(p.L):
                value = part[v, l]
                for other in range(p.mem - 1):
                    value = value + got[other, v, l].astype(f32)
                image[v, l] = value
    total = jnp.zeros((p.R, p.X), f32)
    for s in range(p.S):
        for l in range(p.L):
            own = me * p.S + s
            if first:
                value = image[own, l]
                misfit = -obs[s, l]
            else:
                value = part[own, l]
                for other in range(p.mem - 1):
                    value = value + got[other, s, l].astype(f32)
                image[s, l] = value
                misfit = -(step[0:1, 0:1] * image_before[own, l]) - obs[s, l]
            index = cls[s, l]
            threshold = table(index, huber_levels)
            weight = jnp.where(index > 0, threshold / jnp.maximum(jnp.abs(misfit), threshold), 0.0)
            total = total + weight * value * value
    total = jnp.sum(total, axis=0, keepdims=True)
    total = sum(total[:, i * LANES : (i + 1) * LANES] for i in range(p.X // LANES))
    both = jnp.concatenate([norm[...], total], axis=1)
    send[...] = jnp.broadcast_to(both, send.shape)


def final_kernel(p, got, step, grad0, grad1, image0, image1, control, static_control, increment):
    me = lax.axis_index("mem")
    total = jnp.sum(got[...], axis=0, keepdims=True)
    norm = jnp.sum(total[:, :LANES], axis=1, keepdims=True)
    curvature = jnp.sum(total[:, LANES:], axis=1, keepdims=True)
    second = norm / (norm + curvature)
    first = step[0:1, 0:1]
    for field in range(p.F):
        for l in range(p.L):
            tile, lane = p.slot(field, l)
            where = strided(SWEEPS * SUB + lane, p.R)
            value = -(first * gather(grad0, tile, where)) - second * gather(grad1, tile, where)
            if field < p.K:
                control[field, l] = value
            else:
                static_control[field - p.K, l] = value
    for s in range(p.S):
        for l in range(p.L):
            increment[s, l] = -(first * image0[me * p.S + s, l]) - second * image1[s, l]


def call(kernel, p, outs, scratch, name):
    vmem = pl.BlockSpec(memory_space=pltpu.VMEM)

    def run(*args):
        return pl.pallas_call(
            kernel,
            out_shape=tuple(jax.ShapeDtypeStruct(shape, dtype) for shape, dtype in outs),
            in_specs=[vmem] * len(args),
            out_specs=tuple(vmem for _ in outs),
            scratch_shapes=[pltpu.VMEM(shape, dtype) for shape, dtype in scratch],
            name=name,
        )(*args)

    return run


def local(members, static_scale, observed, huber_class, scale_index):
    p = Plan(members, static_scale, lax.axis_size("mem"), lax.axis_size("row"))
    K, V, L, R, X, S = p.K, p.V, p.L, p.R, p.X, p.S
    assert R >= 2 * SWEEPS

    def round_mem(block, shift):
        return lax.ppermute(block, "mem", [(i, (i + shift) % p.mem) for i in range(p.mem)])

    def round_row(block, shift):
        return lax.ppermute(block, "row", [(i, (i + shift) % p.row) for i in range(p.row)])

    me = lax.axis_index("mem")
    shifts = range(1, p.mem)
    obs_in = jnp.stack([round_mem(observed, shift) for shift in shifts])
    cls_in = jnp.stack([round_mem(huber_class, shift) for shift in shifts])
    C = p.C
    back_shape = ((p.PN, C, R * SUB, LANES), f32)
    sent_shape = ((V, L, R, X), f32)
    halo = (p.PN, C, 2 * SWEEPS * SUB, LANES)
    work = [(halo, f32), (halo, f32), ((C, p.RE * SUB, LANES), f32), ((C, p.RE * SUB, LANES), f32), back_shape]
    grad_shape = ((p.PN, C, p.RG * SUB, LANES), f32)
    norm_shape = ((1, LANES), f32)
    step_shape = ((1, LANES), f32)
    send_shape = ((p.devices, 2 * LANES), f32)

    back, msg = call(
        functools.partial(back_kernel, p, True), p,
        [back_shape, ((p.F + 1, L, R, X), bf16)], [sent_shape], "back0",
    )(members, static_scale, scale_index, observed, huber_class, obs_in, cls_in)
    low, high = round_row(msg, 1), round_row(msg, p.row - 1)
    grad0, kap, norm, part = call(
        functools.partial(sweep_kernel, p, True), p,
        [grad_shape, ((L + p.ST, C, p.RE * SUB, LANES), f32), norm_shape, sent_shape], work, "sweep0",
    )(members, static_scale, scale_index, back, low, high)
    rounded = part.astype(bf16)
    got = jnp.stack([round_mem(rounded, shift) for shift in shifts])
    image0, send = call(
        functools.partial(curvature_kernel, p, True), p, [sent_shape, send_shape], [], "curv0",
    )(part, got, norm, observed, huber_class)
    sums = lax.all_to_all(send, ("mem", "row"), 0, 0, tiled=True)

    back, msg, step = call(
        functools.partial(back_kernel, p, False), p,
        [back_shape, ((p.F, L, R, X), bf16), step_shape], [sent_shape], "back1",
    )(members, static_scale, observed, huber_class, obs_in, cls_in, image0, sums)
    low, high = round_row(msg, 1), round_row(msg, p.row - 1)
    grad1, norm, part = call(
        functools.partial(sweep_kernel, p, False), p, [grad_shape, norm_shape, sent_shape], work, "sweep1",
    )(members, static_scale, kap, grad0, step, back, low, high)
    rounded = part.astype(bf16)
    got = jnp.stack([
        round_mem(lax.dynamic_slice_in_dim(rounded, lax.rem(me + shift, p.mem) * S, S, axis=0), shift)
        for shift in shifts
    ])
    image1, send = call(
        functools.partial(curvature_kernel, p, False), p, [((S, L, R, X), f32), send_shape], [], "curv1",
    )(part, got, norm, observed, huber_class, image0, step)
    sums = lax.all_to_all(send, ("mem", "row"), 0, 0, tiled=True)
    return call(
        functools.partial(final_kernel, p), p,
        [((K, L, R, X), f32), ((S, L, R, X), f32), ((S, L, R, X), f32)], [], "final",
    )(sums, step, grad0, grad1, image0, image1)


def solution(mesh):
    placed = (
        P("mem", None, None, "row", None),
        P("mem", None, "row", None),
        P("mem", None, "row", None),
        P("mem", None, "row", None),
        P(None, "row", None),
    )
    return jax.shard_map(
        local,
        mesh=mesh,
        in_specs=placed,
        out_specs=(
            P("mem", None, "row", None),
            P("mem", None, "row", None),
            P("mem", None, "row", None),
        ),
        check_vma=False,
    )
```

```python
import functools
import math

import jax
import jax.numpy as jnp
from jax import lax
from jax.experimental import pallas as pl
from jax.experimental.pallas import tpu as pltpu
from jax.sharding import PartitionSpec as P

SWEEPS = 4
ITERS = 2
SUB = 8
LANES = 128
kappa_table = (0.06, 0.11, 0.17, 0.23)
huber_levels = (1.0, 0.5, 1.0, 2.0)
f32 = jnp.float32
bf16 = jnp.bfloat16


def table(index, values):
    result = jnp.full(index.shape, values[3], f32)
    for entry in range(3):
        result = jnp.where(index == entry, f32(values[entry]), result)
    return result


class Plan:
    def __init__(self, members, static_scale, mem, row):
        self.K, self.V, self.L, self.R, self.X = members.shape
        self.S = static_scale.shape[0]
        self.mem, self.row = mem, row
        self.devices = mem * row
        self.KT = -(-self.K // SUB)
        self.ST = -(-(self.S * self.L) // SUB)
        self.PM = self.L * self.KT
        self.PN = self.PM + self.ST
        self.F = self.K + self.S
        self.C = self.X // LANES
        self.RE = self.R + 4 * SWEEPS
        self.RG = self.R + 2 * SWEEPS
        self.pads = self.K % SUB != 0 or (self.S * self.L) % SUB != 0
        self.ens = math.sqrt(0.7 / (self.K * mem - 1))
        self.stat = math.sqrt(0.3)

    def slot(self, field, level):
        if field < self.K:
            return level * self.KT + field // SUB, field % SUB
        at = (field - self.K) * self.L + level
        return self.PM + at // SUB, at % SUB


def strided(start, count):
    return pl.ds(start, count, stride=SUB)


def scatter(ref, tile, where, value):
    for c in range(value.shape[1] // LANES):
        ref[tile, c, where, :] = value[:, c * LANES : (c + 1) * LANES]


def gather(ref, tile, where):
    return jnp.concatenate([ref[tile, c, where, :] for c in range(ref.shape[1])], axis=1)


def back_kernel(p, first, *refs):
    if first:
        members, static_scale, scale_index, obs, cls, obs_in, cls_in, back, msg, sent = refs
    else:
        members, static_scale, obs, cls, obs_in, cls_in, image, got, back, msg, step_out, sent = refs
    me = lax.axis_index("mem")
    if p.pads:
        back[...] = jnp.zeros(back.shape, f32)
    if not first:
        total = jnp.sum(got[...], axis=0)
        norm = jnp.sum(total[:, :LANES], axis=1, keepdims=True)
        curvature = jnp.sum(total[:, LANES:], axis=1, keepdims=True)
        step = norm / (norm + curvature)
        step_out[...] = jnp.broadcast_to(step, step_out.shape)
    for shift in range(p.mem):
        base = lax.rem(me + (p.mem - shift), p.mem) * p.S
        for s in range(p.S):
            for l in range(p.L):
                if shift == 0:
                    seen, index = obs[s, l], cls[s, l]
                else:
                    seen, index = obs_in[shift - 1, s, l], cls_in[shift - 1, s, l]
                threshold = table(index, huber_levels)
                if first:
                    misfit = -seen
                else:
                    misfit = -(step * image[base + s, l]) - seen
                clipped = jnp.where(index > 0, jnp.clip(misfit, -threshold, threshold), 0.0)
                rounded = clipped.astype(bf16).astype(f32)
                sent[base + s, l] = rounded
                if shift == 0:
                    tile, lane = p.slot(p.K + s, l)
                    value = p.stat * static_scale[s, l] * rounded
                    scatter(back, tile, strided(lane, p.R), value)
                    msg[p.K + s, l] = value.astype(bf16)
    if first:
        for l in range(p.L):
            msg[p.F, l] = scale_index[l].astype(f32).astype(bf16)
    for l in range(p.L):
        for k in range(p.K):
            value = members[k, 0, l].astype(f32) * sent[0, l]
            for v in range(1, p.V):
                value = value + members[k, v, l].astype(f32) * sent[v, l]
            value = p.ens * value
            tile, lane = p.slot(k, l)
            scatter(back, tile, strided(lane, p.R), value)
            msg[k, l] = value.astype(bf16)


def sideways(u, first_lane, last_lane):
    right = [pltpu.roll(part, 1, 1) for part in u]
    left = [pltpu.roll(part, LANES - 1, 1) for part in u]
    zero = jnp.zeros_like(u[0])
    before, after = [zero] + right[:-1], left[1:] + [zero]
    return [
        jnp.where(first_lane, before[i], right[i]) + jnp.where(last_lane, after[i], left[i])
        for i in range(len(u))
    ]


def stencil(above, here, below, side):
    across = side(here)
    return [(above[c] + below[c]) + across[c] - 4.0 * here[c] for c in range(len(here))]


def sweep_kernel(p, first, *refs):
    if first:
        members, static_scale, scale_index, back, low, high, grad, kap, norm, part, ship, lo, hi, a, b, out = refs
    else:
        members, static_scale, kap, before, step, back, low, high, grad, norm, part, ship, lo, hi, a, b, out = refs
    me, at = lax.axis_index("mem"), lax.axis_index("row")
    low_ok = jnp.where(at > 0, 1.0, 0.0).astype(f32)
    high_ok = jnp.where(at < p.row - 1, 1.0, 0.0).astype(f32)
    R, RE, RG, W = p.R, p.RE, p.RG, SWEEPS
    H = 2 * W
    for ref, dst in ((low, lo), (high, hi)):
        if p.pads:
            dst[...] = jnp.zeros(dst.shape, f32)
        skip = R - H if ref is low else 0
        for field in range(p.F):
            for l in range(p.L):
                tile, lane = p.slot(field, l)
                scatter(dst, tile, strided(lane, H), ref[field, l].astype(f32)[skip : skip + H])
    if first:
        for l in range(p.L):
            pieces = (
                (table(low[p.F, l].astype(f32)[R - H :], kappa_table) * low_ok, 0),
                (table(scale_index[l].astype(f32), kappa_table), H),
                (table(high[p.F, l].astype(f32)[:H], kappa_table) * high_ok, H + R),
            )
            for value, offset in pieces:
                for r in range(value.shape[0]):
                    scatter(kap, l, pl.ds((offset + r) * SUB, SUB), jnp.broadcast_to(value[r : r + 1], (SUB, p.X)))
                for j in range(p.ST * SUB):
                    if (j % p.L) == l:
                        scatter(kap, p.L + j // SUB, strided(offset * SUB + j % SUB, value.shape[0]), value)
    lane = lax.broadcasted_iota(jnp.int32, (SUB, LANES), 1)
    first_lane, last_lane = lane == 0, lane == LANES - 1
    side = functools.partial(sideways, first_lane=first_lane, last_lane=last_lane)
    cols = range(p.C)

    def tiles(ref, r, *lead):
        return [ref[(*lead, c, pl.ds(r * SUB, SUB), slice(None))] for c in cols]

    def keep(value, ref, r, *lead):
        for c in cols:
            ref[(*lead, c, pl.ds(r * SUB, SUB), slice(None))] = value[c]

    if not first:
        step_tile = jnp.broadcast_to(step[0:1, 0:1], (SUB, LANES))

    def problem(t, total):
        which = jnp.where(t < p.PM, t // p.KT, t - p.PM + p.L)
        source = None
        for sweep in range(W):
            target = (a, b)[sweep % 2]
            held = []
            for r in range(sweep, RE - sweep):
                if sweep:
                    u = tiles(source, r)
                elif r < H:
                    u = tiles(lo, r, t)
                elif r < H + R:
                    u = tiles(back, r - H, t)
                else:
                    u = tiles(hi, r - H - R, t)
                factor = tiles(kap, r, which)
                w = [factor[c] * u[c] for c in cols]
                held = (held + [(u, w)])[-3:]
                if len(held) < 3:
                    continue
                (_, w0), (u1, w1), (_, w2) = held
                change = stencil(w0, w1, w2, side)
                value = [u1[c] + change[c] for c in cols]
                if sweep < W - 1:
                    keep(value, target, r - 1)
                    continue
                if not first:
                    earlier = tiles(before, r - 1 - W, t)
                    value = [value[c] - step_tile * earlier[c] for c in cols]
                if r - 1 < H:
                    value = [one * low_ok for one in value]
                elif r - 1 >= H + R:
                    value = [one * high_ok for one in value]
                else:
                    for one in value:
                        total = total + one * one
                keep(value, grad, r - 1 - W, t)
            source = target
        for sweep in range(W):
            target = (a, b)[sweep % 2]
            held = []
            for r in range(W + sweep, RE - W - sweep):
                u = tiles(source, r) if sweep else tiles(grad, r - W, t)
                held = (held + [u])[-3:]
                if len(held) < 3:
                    continue
                change = stencil(*held, side)
                factor = tiles(kap, r - 1, which)
                value = [held[1][c] + factor[c] * change[c] for c in cols]
                if sweep < W - 1:
                    keep(value, target, r - 1)
                else:
                    keep(value, out, r - 1 - H, t)
            source = target
        return total

    total = lax.fori_loop(0, p.PN, problem, jnp.zeros((SUB, LANES), f32))
    norm[...] = jnp.sum(total, axis=0, keepdims=True)
    for l in range(p.L):
        sums = [None] * p.V
        for k in range(p.K):
            tile, j = p.slot(k, l)
            spread = gather(out, tile, strided(j, R)).astype(bf16).astype(f32)
            for v in range(p.V):
                term = members[k, v, l].astype(f32) * spread
                sums[v] = term if k == 0 else sums[v] + term
        for v in range(p.V):
            part[v, l] = p.ens * sums[v]
    for s in range(p.S):
        for l in range(p.L):
            tile, j = p.slot(p.K + s, l)
            own = me * p.S + s
            part[own, l] = part[own, l] + p.stat * static_scale[s, l] * gather(out, tile, strided(j, R))
    for l in range(p.L):
        if first:
            for v in range(p.V):
                ship[v, l] = part[v, l].astype(bf16)
            continue
        for shift in range(1, p.mem):
            base = lax.rem(me + shift, p.mem) * p.S
            for s in range(p.S):
                ship[shift - 1, s, l] = part[base + s, l].astype(bf16)


def curvature_kernel(p, first, *refs):
    if first:
        part, got, norm, obs, cls, image, send = refs
    else:
        part, got, norm, obs, cls, image_before, step, image, send = refs
    me = lax.axis_index("mem")
    if first:
        for v in range(p.V):
            for l in range(p.L):
                value = part[v, l]
                for other in range(p.mem - 1):
                    value = value + got[other, v, l].astype(f32)
                image[v, l] = value
    total = jnp.zeros((p.R, p.X), f32)
    for s in range(p.S):
        for l in range(p.L):
            own = me * p.S + s
            if first:
                value = image[own, l]
                misfit = -obs[s, l]
            else:
                value = part[own, l]
                for other in range(p.mem - 1):
                    value = value + got[other, s, l].astype(f32)
                image[s, l] = value
                misfit = -(step[0:1, 0:1] * image_before[own, l]) - obs[s, l]
            index = cls[s, l]
            threshold = table(index, huber_levels)
            weight = jnp.where(index > 0, threshold / jnp.maximum(jnp.abs(misfit), threshold), 0.0)
            total = total + weight * value * value
    total = jnp.sum(total, axis=0, keepdims=True)
    total = sum(total[:, i * LANES : (i + 1) * LANES] for i in range(p.X // LANES))
    both = jnp.concatenate([norm[...], total], axis=1)
    send[...] = jnp.broadcast_to(both[None], send.shape)


def final_kernel(p, got, step, grad0, grad1, image0, image1, control, static_control, increment):
    me = lax.axis_index("mem")
    total = jnp.sum(got[...], axis=0)
    norm = jnp.sum(total[:, :LANES], axis=1, keepdims=True)
    curvature = jnp.sum(total[:, LANES:], axis=1, keepdims=True)
    second = norm / (norm + curvature)
    first = step[0:1, 0:1]
    for field in range(p.F):
        for l in range(p.L):
            tile, lane = p.slot(field, l)
            where = strided(SWEEPS * SUB + lane, p.R)
            value = -(first * gather(grad0, tile, where)) - second * gather(grad1, tile, where)
            if field < p.K:
                control[field, l] = value
            else:
                static_control[field - p.K, l] = value
    for s in range(p.S):
        for l in range(p.L):
            increment[s, l] = -(first * image0[me * p.S + s, l]) - second * image1[s, l]


def call(kernel, p, outs, scratch, name):
    vmem = pl.BlockSpec(memory_space=pltpu.VMEM)

    def run(*args):
        return pl.pallas_call(
            kernel,
            out_shape=tuple(jax.ShapeDtypeStruct(shape, dtype) for shape, dtype in outs),
            in_specs=[vmem] * len(args),
            out_specs=tuple(vmem for _ in outs),
            scratch_shapes=[pltpu.VMEM(shape, dtype) for shape, dtype in scratch],
            compiler_params=pltpu.CompilerParams(vmem_limit_bytes=16 << 20),
            name=name,
        )(*args)

    return run


def local(members, static_scale, observed, huber_class, scale_index):
    p = Plan(members, static_scale, lax.axis_size("mem"), lax.axis_size("row"))
    K, V, L, R, X, S = p.K, p.V, p.L, p.R, p.X, p.S
    assert R >= 2 * SWEEPS

    def round_mem(block, shift):
        return lax.ppermute(block, "mem", [(i, (i + shift) % p.mem) for i in range(p.mem)])

    def round_row(block, shift):
        return lax.ppermute(block, "row", [(i, (i + shift) % p.row) for i in range(p.row)])

    shifts = range(1, p.mem)
    obs_in = jnp.stack([round_mem(observed, shift) for shift in shifts])
    cls_in = jnp.stack([round_mem(huber_class, shift) for shift in shifts])
    C = p.C
    back_shape = ((p.PN, C, R * SUB, LANES), f32)
    sent_shape = ((V, L, R, X), f32)
    halo = (p.PN, C, 2 * SWEEPS * SUB, LANES)
    work = [(halo, f32), (halo, f32), ((C, p.RE * SUB, LANES), f32), ((C, p.RE * SUB, LANES), f32), back_shape]
    grad_shape = ((p.PN, C, p.RG * SUB, LANES), f32)
    norm_shape = ((1, LANES), f32)
    step_shape = ((1, LANES), f32)
    send_shape = ((p.devices, 1, 2 * LANES), f32)

    back, msg = call(
        functools.partial(back_kernel, p, True), p,
        [back_shape, ((p.F + 1, L, R, X), bf16)], [sent_shape], "back0",
    )(members, static_scale, scale_index, observed, huber_class, obs_in, cls_in)
    low, high = round_row(msg, 1), round_row(msg, p.row - 1)
    grad0, kap, norm, part, ship = call(
        functools.partial(sweep_kernel, p, True), p,
        [grad_shape, ((L + p.ST, C, p.RE * SUB, LANES), f32), norm_shape, sent_shape, ((V, L, R, X), bf16)],
        work, "sweep0",
    )(members, static_scale, scale_index, back, low, high)
    got = jnp.stack([round_mem(ship, shift) for shift in shifts])
    image0, send = call(
        functools.partial(curvature_kernel, p, True), p, [sent_shape, send_shape], [], "curv0",
    )(part, got, norm, observed, huber_class)
    sums = lax.all_to_all(send, ("mem", "row"), 0, 0)

    back, msg, step = call(
        functools.partial(back_kernel, p, False), p,
        [back_shape, ((p.F, L, R, X), bf16), step_shape], [sent_shape], "back1",
    )(members, static_scale, observed, huber_class, obs_in, cls_in, image0, sums)
    low, high = round_row(msg, 1), round_row(msg, p.row - 1)
    grad1, norm, part, ship = call(
        functools.partial(sweep_kernel, p, False), p,
        [grad_shape, norm_shape, sent_shape, ((p.mem - 1, S, L, R, X), bf16)], work, "sweep1",
    )(members, static_scale, kap, grad0, step, back, low, high)
    got = jnp.stack([round_mem(ship[shift - 1], shift) for shift in shifts])
    image1, send = call(
        functools.partial(curvature_kernel, p, False), p, [((S, L, R, X), f32), send_shape], [], "curv1",
    )(part, got, norm, observed, huber_class, image0, step)
    sums = lax.all_to_all(send, ("mem", "row"), 0, 0)
    return call(
        functools.partial(final_kernel, p), p,
        [((K, L, R, X), f32), ((S, L, R, X), f32), ((S, L, R, X), f32)], [], "final",
    )(sums, step, grad0, grad1, image0, image1)


def solution(mesh):
    placed = (
        P("mem", None, None, "row", None),
        P("mem", None, "row", None),
        P("mem", None, "row", None),
        P("mem", None, "row", None),
        P(None, "row", None),
    )
    return jax.shard_map(
        local,
        mesh=mesh,
        in_specs=placed,
        out_specs=(
            P("mem", None, "row", None),
            P("mem", None, "row", None),
            P("mem", None, "row", None),
        ),
        check_vma=False,
    )
```

```python
import functools
import math

import jax
import jax.numpy as jnp
from jax import lax
from jax.experimental import pallas as pl
from jax.experimental.pallas import tpu as pltpu
from jax.sharding import PartitionSpec as P

SWEEPS = 4
ITERS = 2
SUB = 8
LANES = 128
kappa_table = (0.06, 0.11, 0.17, 0.23)
huber_levels = (1.0, 0.5, 1.0, 2.0)
f32 = jnp.float32
bf16 = jnp.bfloat16


def table(index, values):
    result = jnp.full(index.shape, values[3], f32)
    for entry in range(3):
        result = jnp.where(index == entry, f32(values[entry]), result)
    return result


class Plan:
    def __init__(self, members, static_scale, mem, row):
        self.K, self.V, self.L, self.R, self.X = members.shape
        self.S = static_scale.shape[0]
        self.mem, self.row = mem, row
        self.devices = mem * row
        self.KT = -(-self.K // SUB)
        self.ST = -(-(self.S * self.L) // SUB)
        self.PM = self.L * self.KT
        self.PN = self.PM + self.ST
        self.F = self.K + self.S
        self.C = self.X // LANES
        self.RE = self.R + 4 * SWEEPS
        self.RG = self.R + 2 * SWEEPS
        self.pads = self.K % SUB != 0 or (self.S * self.L) % SUB != 0
        self.ens = math.sqrt(0.7 / (self.K * mem - 1))
        self.stat = math.sqrt(0.3)

    def fields(self, level):
        own = [(k, level) for k in range(self.K)]
        return own + [(self.K + s, l) for s in range(self.S) for l in range(self.L)] if level == 0 else own

    def tiles(self, level):
        return self.KT + self.ST if level == 0 else self.KT

    def inner(self, field, level):
        if field < self.K:
            return field // SUB, field % SUB
        at = (field - self.K) * self.L + level
        return self.KT + at // SUB, at % SUB

    def slot(self, field, level):
        if field < self.K:
            return level * self.KT + field // SUB, field % SUB
        at = (field - self.K) * self.L + level
        return self.PM + at // SUB, at % SUB


def strided(start, count):
    return pl.ds(start, count, stride=SUB)


def scatter(ref, tile, where, value):
    for c in range(value.shape[1] // LANES):
        ref[tile, c, where, :] = value[:, c * LANES : (c + 1) * LANES]


def gather(ref, tile, where):
    return jnp.concatenate([ref[tile, c, where, :] for c in range(ref.shape[1])], axis=1)


def load_kernel(p, obs, cls, obs_out, cls_out, sent, code, sems):
    pairs = ((obs, obs_out), (cls, cls_out))
    copies = [pltpu.make_async_copy(src, dst, sems.at[i]) for i, (src, dst) in enumerate(pairs)]
    for copy in copies:
        copy.start()
    for copy in copies:
        copy.wait()
    for s in range(p.S):
        for l in range(p.L):
            index = cls_out[s, l]
            threshold = table(index, huber_levels)
            clipped = jnp.where(index > 0, jnp.clip(-obs_out[s, l], -threshold, threshold), 0.0)
            sent[s, l] = clipped.astype(bf16)
            code[s, l] = index.astype(f32).astype(bf16)


def fetch_kernel(p, members, static_scale, scale_index, after, members_out, static_out, scale_out, sems):
    pairs = ((members, members_out), (static_scale, static_out), (scale_index, scale_out))
    copies = [pltpu.make_async_copy(src, dst, sems.at[i]) for i, (src, dst) in enumerate(pairs)]
    for copy in copies:
        copy.start()
    for copy in copies:
        copy.wait()


def back_kernel(p, first, *refs):
    if first:
        members, static_scale, scale_index, own, others, back, *msgs, sent = refs
    else:
        members, static_scale, obs, cls, obs_in, code_in, image, got, back, step_out, *msgs, sent = refs
    me = lax.axis_index("mem")
    if p.pads:
        back[...] = jnp.zeros(back.shape, f32)
    if not first:
        total = jnp.sum(got[...], axis=0)
        norm = jnp.sum(total[:, :LANES], axis=1, keepdims=True)
        curvature = jnp.sum(total[:, LANES:], axis=1, keepdims=True)
        step = norm / (norm + curvature)
        step_out[...] = jnp.broadcast_to(step, step_out.shape)
    for shift in range(p.mem):
        base = lax.rem(me + (p.mem - shift), p.mem) * p.S
        for s in range(p.S):
            for l in range(p.L):
                if first:
                    rounded = (own[s, l] if shift == 0 else others[shift - 1, s, l]).astype(f32)
                else:
                    if shift == 0:
                        seen, index = obs[s, l], cls[s, l]
                    else:
                        seen, index = obs_in[shift - 1, s, l], code_in[shift - 1, s, l].astype(f32)
                    threshold = table(index, huber_levels)
                    misfit = -(step * image[base + s, l]) - seen
                    clipped = jnp.where(index > 0, jnp.clip(misfit, -threshold, threshold), 0.0)
                    rounded = clipped.astype(bf16).astype(f32)
                sent[base + s, l] = rounded
                if shift == 0:
                    tile, lane = p.slot(p.K + s, l)
                    value = p.stat * static_scale[s, l] * rounded
                    scatter(back, tile, strided(lane, p.R), value)
                    msgs[0][p.K + s * p.L + l] = value.astype(bf16)
    if first:
        for l in range(p.L):
            msgs[0][p.K + p.S * p.L + l] = scale_index[l].astype(f32).astype(bf16)
    for l in range(p.L):
        for k in range(p.K):
            value = members[k, 0, l].astype(f32) * sent[0, l]
            for v in range(1, p.V):
                value = value + members[k, v, l].astype(f32) * sent[v, l]
            value = p.ens * value
            tile, lane = p.slot(k, l)
            scatter(back, tile, strided(lane, p.R), value)
            msgs[l][k] = value.astype(bf16)


def sideways(u, first_lane, last_lane):
    right = [pltpu.roll(part, 1, 1) for part in u]
    left = [pltpu.roll(part, LANES - 1, 1) for part in u]
    zero = jnp.zeros_like(u[0])
    before, after = [zero] + right[:-1], left[1:] + [zero]
    return [
        jnp.where(first_lane, before[i], right[i]) + jnp.where(last_lane, after[i], left[i])
        for i in range(len(u))
    ]


def stencil(above, here, below, side):
    across = side(here)
    return [(above[c] + below[c]) + across[c] - 4.0 * here[c] for c in range(len(here))]


def sweep_kernel(p, first, level, *refs):
    refs = list(refs)
    members, static_scale, back, low, high = refs[:5]
    refs = refs[5:]
    if first and level == 0:
        scale_index, *refs = refs
    else:
        kap, *refs = refs
    if level:
        rest, *refs = refs
    if not first:
        before, step, *refs = refs
    grad, norm, part, ship, *refs = refs
    if level == 0 and p.L > 1:
        rest, *refs = refs
    if first and level == 0:
        kap, *refs = refs
    lo, hi, a, b, out = refs
    me, at = lax.axis_index("mem"), lax.axis_index("row")
    low_ok = jnp.where(at > 0, 1.0, 0.0).astype(f32)
    high_ok = jnp.where(at < p.row - 1, 1.0, 0.0).astype(f32)
    R, RE, RG, W = p.R, p.RE, p.RG, SWEEPS
    H = 2 * W
    fields = p.fields(level)
    count = p.tiles(level)
    for ref, dst in ((low, lo), (high, hi)):
        if p.pads:
            dst[...] = jnp.zeros(dst.shape, f32)
        skip = R - H if ref is low else 0
        for i, (field, l) in enumerate(fields):
            tile, lane = p.inner(field, l)
            scatter(dst, tile, strided(lane, H), ref[i].astype(f32)[skip : skip + H])
    if first and level == 0:
        for l in range(p.L):
            pieces = (
                (table(low[len(fields) + l].astype(f32)[R - H :], kappa_table) * low_ok, 0),
                (table(scale_index[l].astype(f32), kappa_table), H),
                (table(high[len(fields) + l].astype(f32)[:H], kappa_table) * high_ok, H + R),
            )
            for value, offset in pieces:
                for r in range(value.shape[0]):
                    scatter(kap, l, pl.ds((offset + r) * SUB, SUB), jnp.broadcast_to(value[r : r + 1], (SUB, p.X)))
                for j in range(p.ST * SUB):
                    if (j % p.L) == l:
                        scatter(kap, p.L + j // SUB, strided(offset * SUB + j % SUB, value.shape[0]), value)
    lane = lax.broadcasted_iota(jnp.int32, (SUB, LANES), 1)
    first_lane, last_lane = lane == 0, lane == LANES - 1
    side = functools.partial(sideways, first_lane=first_lane, last_lane=last_lane)
    cols = range(p.C)

    def tiles(ref, r, *lead):
        return [ref[(*lead, c, pl.ds(r * SUB, SUB), slice(None))] for c in cols]

    def keep(value, ref, r, *lead):
        for c in cols:
            ref[(*lead, c, pl.ds(r * SUB, SUB), slice(None))] = value[c]

    if not first:
        step_tile = jnp.broadcast_to(step[0:1, 0:1], (SUB, LANES))

    def problem(t, total):
        if level == 0:
            which = jnp.where(t < p.KT, 0, t - p.KT + p.L)
            whole = jnp.where(t < p.KT, t, t - p.KT + p.PM)
        else:
            which, whole = level, t + level * p.KT
        source = None
        for sweep in range(W):
            target = (a, b)[sweep % 2]
            held = []
            for r in range(sweep, RE - sweep):
                if sweep:
                    u = tiles(source, r)
                elif r < H:
                    u = tiles(lo, r, t)
                elif r < H + R:
                    u = tiles(back, r - H, whole)
                else:
                    u = tiles(hi, r - H - R, t)
                factor = tiles(kap, r, which)
                w = [factor[c] * u[c] for c in cols]
                held = (held + [(u, w)])[-3:]
                if len(held) < 3:
                    continue
                (_, w0), (u1, w1), (_, w2) = held
                change = stencil(w0, w1, w2, side)
                value = [u1[c] + change[c] for c in cols]
                if sweep < W - 1:
                    keep(value, target, r - 1)
                    continue
                if not first:
                    earlier = tiles(before, r - 1 - W, t)
                    value = [value[c] - step_tile * earlier[c] for c in cols]
                if r - 1 < H:
                    value = [one * low_ok for one in value]
                elif r - 1 >= H + R:
                    value = [one * high_ok for one in value]
                else:
                    for one in value:
                        total = total + one * one
                keep(value, grad, r - 1 - W, t)
            source = target
        for sweep in range(W):
            target = (a, b)[sweep % 2]
            held = []
            for r in range(W + sweep, RE - W - sweep):
                u = tiles(source, r) if sweep else tiles(grad, r - W, t)
                held = (held + [u])[-3:]
                if len(held) < 3:
                    continue
                change = stencil(*held, side)
                factor = tiles(kap, r - 1, which)
                value = [held[1][c] + factor[c] * change[c] for c in cols]
                if sweep < W - 1:
                    keep(value, target, r - 1)
                else:
                    keep(value, out, r - 1 - H, t)
            source = target
        return total

    total = lax.fori_loop(0, count, problem, jnp.zeros((SUB, LANES), f32))
    norm[...] = jnp.sum(total, axis=0, keepdims=True)
    sums = [None] * p.V
    for k in range(p.K):
        tile, j = p.inner(k, level)
        spread = gather(out, tile, strided(j, R)).astype(bf16).astype(f32)
        for v in range(p.V):
            term = members[k, v, level].astype(f32) * spread
            sums[v] = term if k == 0 else sums[v] + term
    for v in range(p.V):
        part[v] = p.ens * sums[v]
    for s in range(p.S):
        own = me * p.S + s
        if level:
            part[own] = part[own] + rest[level - 1, s]
            continue
        for l in range(p.L):
            tile, j = p.inner(p.K + s, l)
            value = p.stat * static_scale[s, l] * gather(out, tile, strided(j, R))
            if l:
                rest[l - 1, s] = value
            else:
                part[own] = part[own] + value
    if first:
        ship[...] = part[...].astype(bf16)
        return
    for shift in range(1, p.mem):
        base = lax.rem(me + shift, p.mem) * p.S
        for s in range(p.S):
            ship[shift - 1, s] = part[base + s].astype(bf16)


def curvature_kernel(p, first, *refs):
    parts, gots, norms, refs = refs[: p.L], refs[p.L : 2 * p.L], refs[2 * p.L : 3 * p.L], refs[3 * p.L :]
    if first:
        obs, cls, image, send = refs
    else:
        obs, cls, image_before, step, image, send = refs
    me = lax.axis_index("mem")
    total = jnp.zeros((p.R, p.X), f32)
    for l in range(p.L):
        if first:
            for v in range(p.V):
                value = parts[l][v]
                for other in range(p.mem - 1):
                    value = value + gots[l][other, v].astype(f32)
                image[v, l] = value
        for s in range(p.S):
            own = me * p.S + s
            if first:
                value = image[own, l]
                misfit = -obs[s, l]
            else:
                value = parts[l][own]
                for other in range(p.mem - 1):
                    value = value + gots[l][other, s].astype(f32)
                image[s, l] = value
                misfit = -(step[0:1, 0:1] * image_before[own, l]) - obs[s, l]
            index = cls[s, l]
            threshold = table(index, huber_levels)
            weight = jnp.where(index > 0, threshold / jnp.maximum(jnp.abs(misfit), threshold), 0.0)
            total = total + weight * value * value
    total = jnp.sum(total, axis=0, keepdims=True)
    total = sum(total[:, i * LANES : (i + 1) * LANES] for i in range(p.X // LANES))
    norm = sum(one[...] for one in norms)
    send[...] = jnp.broadcast_to(jnp.concatenate([norm, total], axis=1)[None], send.shape)


def final_kernel(p, got, step, image0, image1, *refs):
    before, after, outs = refs[: p.L], refs[p.L : 2 * p.L], refs[2 * p.L :]
    control, static_control, increment = outs
    me = lax.axis_index("mem")
    total = jnp.sum(got[...], axis=0)
    norm = jnp.sum(total[:, :LANES], axis=1, keepdims=True)
    curvature = jnp.sum(total[:, LANES:], axis=1, keepdims=True)
    second = norm / (norm + curvature)
    first = step[0:1, 0:1]
    for level in range(p.L):
        for field, l in p.fields(level):
            tile, lane = p.inner(field, l)
            where = strided(SWEEPS * SUB + lane, p.R)
            value = -(first * gather(before[level], tile, where)) - second * gather(after[level], tile, where)
            if field < p.K:
                control[field, l] = value
            else:
                static_control[field - p.K, l] = value
    for s in range(p.S):
        for l in range(p.L):
            increment[s, l] = -(first * image0[me * p.S + s, l]) - second * image1[s, l]


def call(kernel, p, outs, scratch, name, far=0, cost=0):
    vmem = pl.BlockSpec(memory_space=pltpu.VMEM)
    anywhere = pl.BlockSpec(memory_space=pl.ANY)

    def run(*args):
        return pl.pallas_call(
            kernel,
            out_shape=tuple(jax.ShapeDtypeStruct(shape, dtype) for shape, dtype in outs),
            in_specs=[anywhere] * far + [vmem] * (len(args) - far),
            out_specs=tuple(vmem for _ in outs),
            scratch_shapes=scratch,
            compiler_params=pltpu.CompilerParams(vmem_limit_bytes=16 << 20),
            cost_estimate=pl.CostEstimate(flops=cost, bytes_accessed=cost, transcendentals=0),
            name=name,
        )(*args)

    return run


def local(members, static_scale, observed, huber_class, scale_index):
    p = Plan(members, static_scale, lax.axis_size("mem"), lax.axis_size("row"))
    K, V, L, R, X, S, C = p.K, p.V, p.L, p.R, p.X, p.S, p.C
    assert R >= 2 * SWEEPS

    def round_mem(block, shift):
        return lax.ppermute(block, "mem", [(i, (i + shift) % p.mem) for i in range(p.mem)])

    def round_row(block, shift):
        return lax.ppermute(block, "row", [(i, (i + shift) % p.row) for i in range(p.row)])

    vmem = lambda shape: pltpu.VMEM(shape, f32)
    part = functools.partial
    shifts = range(1, p.mem)
    own_shape = (S, L, R, X)
    full_shape = (V, L, R, X)
    back_shape = (p.PN, C, R * SUB, LANES)
    send_shape = ((p.devices, 1, 2 * LANES), f32)
    line = ((1, LANES), f32)

    obs, cls, own, code = call(
        part(load_kernel, p), p,
        [(own_shape, f32), (own_shape, jnp.int32), (own_shape, bf16), (own_shape, bf16)],
        [pltpu.SemaphoreType.DMA((2,))], "load", far=2,
    )(observed, huber_class)
    others = jnp.stack([round_mem(own, shift) for shift in shifts])
    members, static_scale, scale_index = call(
        part(fetch_kernel, p), p,
        [(x.shape, x.dtype) for x in (members, static_scale, scale_index)],
        [pltpu.SemaphoreType.DMA((3,))], "fetch", far=3, cost=4 << 20,
    )(members, static_scale, scale_index, own)
    obs_in = jnp.stack([round_mem(obs, shift) for shift in shifts])
    code_in = jnp.stack([round_mem(code, shift) for shift in shifts])

    grads, image, step, kap, sums = [], None, None, None, None
    for turn in range(ITERS):
        first = turn == 0
        sizes = [len(p.fields(level)) for level in range(L)]
        if first:
            sizes[0] += L
        msg_shapes = [((size, R, X), bf16) for size in sizes]
        if first:
            back, *msgs = call(
                part(back_kernel, p, True), p, [(back_shape, f32)] + msg_shapes, [vmem(full_shape)], "back0",
            )(members, static_scale, scale_index, own, others)
        else:
            back, step, *msgs = call(
                part(back_kernel, p, False), p, [(back_shape, f32), line] + msg_shapes, [vmem(full_shape)], "back1",
            )(members, static_scale, obs, cls, obs_in, code_in, image, sums)
        halos = [(round_row(msg, 1), round_row(msg, p.row - 1)) for msg in msgs]
        grad, norms, partial_images, gots, rest = [], [], [], [], None
        for level in range(L):
            count = p.tiles(level)
            args = [members, static_scale, back, *halos[level]]
            args += [scale_index] if first and level == 0 else [kap]
            args += [rest] if level else []
            args += [] if first else [grads[0][level], step]
            ship_shape = (V, R, X) if first else (p.mem - 1, S, R, X)
            outs = [((count, C, p.RG * SUB, LANES), f32), line, ((V, R, X), f32), (ship_shape, bf16)]
            if level == 0 and L > 1:
                outs.append(((L - 1, S, R, X), f32))
            if first and level == 0:
                outs.append(((L + p.ST, C, p.RE * SUB, LANES), f32))
            halo = vmem((count, C, 2 * SWEEPS * SUB, LANES))
            work = [halo, halo, vmem((C, p.RE * SUB, LANES)), vmem((C, p.RE * SUB, LANES))]
            g, norm, partial_image, ship, *more = call(
                part(sweep_kernel, p, first, level), p, outs, work + [vmem((count, C, R * SUB, LANES))],
                f"sweep{turn}_{level}", cost=8 << 20,
            )(*args)
            if level == 0 and L > 1:
                rest, *more = more
            if first and level == 0:
                kap = more[0]
            grad.append(g)
            norms.append(norm)
            partial_images.append(partial_image)
            gots.append(jnp.stack([round_mem(ship if first else ship[shift - 1], shift) for shift in shifts]))
        grads.append(grad)
        if first:
            image, send = call(
                part(curvature_kernel, p, True), p, [(full_shape, f32), send_shape], [], "curv0",
            )(*partial_images, *gots, *norms, obs, cls)
        else:
            last, send = call(
                part(curvature_kernel, p, False), p, [(own_shape, f32), send_shape], [], "curv1",
            )(*partial_images, *gots, *norms, obs, cls, image, step)
        sums = lax.all_to_all(send, ("mem", "row"), 0, 0)
    return call(
        part(final_kernel, p), p,
        [((K, L, R, X), f32), (own_shape, f32), (own_shape, f32)], [], "final",
    )(sums, step, image, last, *grads[0], *grads[1])


def solution(mesh):
    placed = (
        P("mem", None, None, "row", None),
        P("mem", None, "row", None),
        P("mem", None, "row", None),
        P("mem", None, "row", None),
        P(None, "row", None),
    )
    return jax.shard_map(
        local,
        mesh=mesh,
        in_specs=placed,
        out_specs=(
            P("mem", None, "row", None),
            P("mem", None, "row", None),
            P("mem", None, "row", None),
        ),
        check_vma=False,
    )
```

```python
import functools
import math

import jax
import jax.numpy as jnp
from jax import lax
from jax.experimental import pallas as pl
from jax.experimental.pallas import tpu as pltpu
from jax.sharding import PartitionSpec as P


SWEEPS = 4
ITERS = 2
SUB = 8
LANES = 128
kappa_table = (0.06, 0.11, 0.17, 0.23)
huber_levels = (1.0, 0.5, 1.0, 2.0)
f32 = jnp.float32
bf16 = jnp.bfloat16


def table(index, values):
    result = jnp.full(index.shape, values[3], f32)
    for entry in range(3):
        result = jnp.where(index == entry, f32(values[entry]), result)
    return result


class Plan:
    def __init__(self, members, static_scale, mem, row):
        self.K, self.V, self.L, self.R, self.X = members.shape
        self.S = static_scale.shape[0]
        self.mem, self.row = mem, row
        self.devices = mem * row
        self.KT = -(-self.K // SUB)
        self.ST = -(-(self.S * self.L) // SUB)
        self.PM = self.L * self.KT
        self.PN = self.PM + self.ST
        self.C = self.X // LANES
        self.RE = self.R + 4 * SWEEPS
        self.RG = self.R + 2 * SWEEPS
        self.pads = self.K % SUB != 0 or (self.S * self.L) % SUB != 0
        self.ens = math.sqrt(0.7 / (self.K * mem - 1))
        self.stat = math.sqrt(0.3)

    def fields(self, level):
        own = [(k, level) for k in range(self.K)]
        return own + [(self.K + s, l) for s in range(self.S) for l in range(self.L)] if level == 0 else own

    def tiles(self, level):
        return self.KT + self.ST if level == 0 else self.KT

    def inner(self, field, level):
        if field < self.K:
            return field // SUB, field % SUB
        at = (field - self.K) * self.L + level
        return self.KT + at // SUB, at % SUB

    def slot(self, field, level):
        if field < self.K:
            return level * self.KT + field // SUB, field % SUB
        at = (field - self.K) * self.L + level
        return self.PM + at // SUB, at % SUB


def strided(start, count):
    return pl.ds(start, count, stride=SUB)


def scatter(ref, tile, where, value):
    for c in range(value.shape[1] // LANES):
        ref[tile, c, where, :] = value[:, c * LANES : (c + 1) * LANES]


def gather(ref, tile, where):
    return jnp.concatenate([ref[tile, c, where, :] for c in range(ref.shape[1])], axis=1)


def load_kernel(p, obs, cls, obs_out, cls_out, sent, code, sems):
    pairs = ((obs, obs_out), (cls, cls_out))
    copies = [pltpu.make_async_copy(src, dst, sems.at[i]) for i, (src, dst) in enumerate(pairs)]
    for copy in copies:
        copy.start()
    for copy in copies:
        copy.wait()
    for s in range(p.S):
        for l in range(p.L):
            index = cls_out[s, l]
            threshold = table(index, huber_levels)
            clipped = jnp.where(index > 0, jnp.clip(-obs_out[s, l], -threshold, threshold), 0.0)
            sent[s, l] = clipped.astype(bf16)
            code[s, l] = index.astype(f32).astype(bf16)


def fetch_kernel(members, static_scale, scale_index, after, members_out, static_out, scale_out, sems):
    pairs = ((members, members_out), (static_scale, static_out), (scale_index, scale_out))
    copies = [pltpu.make_async_copy(src, dst, sems.at[i]) for i, (src, dst) in enumerate(pairs)]
    for copy in copies:
        copy.start()
    for copy in copies:
        copy.wait()


def back_kernel(p, first, *refs):
    if first:
        members, static_scale, scale_index, own, others, back, *msgs, sent = refs
    else:
        members, static_scale, obs, cls, obs_in, code_in, image, got, back, step_out, *msgs, sent = refs
    me = lax.axis_index("mem")
    if p.pads:
        back[...] = jnp.zeros(back.shape, f32)
    if not first:
        total = jnp.sum(got[...], axis=0)
        norm = jnp.sum(total[:, :LANES], axis=1, keepdims=True)
        curvature = jnp.sum(total[:, LANES:], axis=1, keepdims=True)
        step = norm / (norm + curvature)
        step_out[...] = jnp.broadcast_to(step, step_out.shape)
    for shift in range(p.mem):
        base = lax.rem(me + (p.mem - shift), p.mem) * p.S
        for s in range(p.S):
            for l in range(p.L):
                if first:
                    rounded = (own[s, l] if shift == 0 else others[shift - 1, s, l]).astype(f32)
                else:
                    if shift == 0:
                        seen, index = obs[s, l], cls[s, l]
                    else:
                        seen, index = obs_in[shift - 1, s, l], code_in[shift - 1, s, l].astype(f32)
                    threshold = table(index, huber_levels)
                    misfit = -(step * image[base + s, l]) - seen
                    clipped = jnp.where(index > 0, jnp.clip(misfit, -threshold, threshold), 0.0)
                    rounded = clipped.astype(bf16).astype(f32)
                sent[base + s, l] = rounded
                if shift == 0:
                    tile, lane = p.slot(p.K + s, l)
                    value = p.stat * static_scale[s, l] * rounded
                    scatter(back, tile, strided(lane, p.R), value)
                    msgs[0][p.K + s * p.L + l] = value.astype(bf16)
    if first:
        for l in range(p.L):
            msgs[0][p.K + p.S * p.L + l] = scale_index[l].astype(f32).astype(bf16)
    for l in range(p.L):
        for k in range(p.K):
            value = members[k, 0, l].astype(f32) * sent[0, l]
            for v in range(1, p.V):
                value = value + members[k, v, l].astype(f32) * sent[v, l]
            value = p.ens * value
            tile, lane = p.slot(k, l)
            scatter(back, tile, strided(lane, p.R), value)
            msgs[l][k] = value.astype(bf16)


def sideways(u, first_lane, last_lane):
    right = [pltpu.roll(part, 1, 1) for part in u]
    left = [pltpu.roll(part, LANES - 1, 1) for part in u]
    zero = jnp.zeros_like(u[0])
    before, after = [zero] + right[:-1], left[1:] + [zero]
    return [
        jnp.where(first_lane, before[i], right[i]) + jnp.where(last_lane, after[i], left[i])
        for i in range(len(u))
    ]


def stencil(above, here, below, side):
    across = side(here)
    return [(above[c] + below[c]) + across[c] - 4.0 * here[c] for c in range(len(here))]


def sweep_kernel(p, first, level, *refs):
    refs = list(refs)
    members, static_scale, back, low, high = refs[:5]
    refs = refs[5:]
    if first and level == 0:
        scale_index, *refs = refs
    else:
        kap, *refs = refs
    if level:
        rest, *refs = refs
    if not first:
        before, step, *refs = refs
    grad, norm, part, ship, *refs = refs
    if level == 0 and p.L > 1:
        rest, *refs = refs
    if first and level == 0:
        kap, *refs = refs
    lo, hi, a, b, out = refs
    me, at = lax.axis_index("mem"), lax.axis_index("row")
    low_ok = jnp.where(at > 0, 1.0, 0.0).astype(f32)
    high_ok = jnp.where(at < p.row - 1, 1.0, 0.0).astype(f32)
    R, RE, W = p.R, p.RE, SWEEPS
    H = 2 * W
    fields = p.fields(level)
    count = p.tiles(level)
    for ref, dst in ((low, lo), (high, hi)):
        if p.pads:
            dst[...] = jnp.zeros(dst.shape, f32)
        skip = R - H if ref is low else 0
        for i, (field, l) in enumerate(fields):
            tile, lane = p.inner(field, l)
            scatter(dst, tile, strided(lane, H), ref[i].astype(f32)[skip : skip + H])
    if first and level == 0:
        for l in range(p.L):
            pieces = (
                (table(low[len(fields) + l].astype(f32)[R - H :], kappa_table) * low_ok, 0),
                (table(scale_index[l].astype(f32), kappa_table), H),
                (table(high[len(fields) + l].astype(f32)[:H], kappa_table) * high_ok, H + R),
            )
            for value, offset in pieces:
                for r in range(value.shape[0]):
                    scatter(kap, l, pl.ds((offset + r) * SUB, SUB), jnp.broadcast_to(value[r : r + 1], (SUB, p.X)))
                for j in range(p.ST * SUB):
                    if (j % p.L) == l:
                        scatter(kap, p.L + j // SUB, strided(offset * SUB + j % SUB, value.shape[0]), value)
    lane = lax.broadcasted_iota(jnp.int32, (SUB, LANES), 1)
    first_lane, last_lane = lane == 0, lane == LANES - 1
    side = functools.partial(sideways, first_lane=first_lane, last_lane=last_lane)
    cols = range(p.C)

    def tiles(ref, r, *lead):
        return [ref[(*lead, c, pl.ds(r * SUB, SUB), slice(None))] for c in cols]

    def keep(value, ref, r, *lead):
        for c in cols:
            ref[(*lead, c, pl.ds(r * SUB, SUB), slice(None))] = value[c]

    if not first:
        step_tile = jnp.broadcast_to(step[0:1, 0:1], (SUB, LANES))

    def problem(t, total):
        if level == 0:
            which = jnp.where(t < p.KT, 0, t - p.KT + p.L)
            whole = jnp.where(t < p.KT, t, t - p.KT + p.PM)
        else:
            which, whole = level, t + level * p.KT
        source = None
        for sweep in range(W):
            target = (a, b)[sweep % 2]
            held = []
            for r in range(sweep, RE - sweep):
                if sweep:
                    u = tiles(source, r)
                elif r < H:
                    u = tiles(lo, r, t)
                elif r < H + R:
                    u = tiles(back, r - H, whole)
                else:
                    u = tiles(hi, r - H - R, t)
                factor = tiles(kap, r, which)
                w = [factor[c] * u[c] for c in cols]
                held = (held + [(u, w)])[-3:]
                if len(held) < 3:
                    continue
                (_, w0), (u1, w1), (_, w2) = held
                change = stencil(w0, w1, w2, side)
                value = [u1[c] + change[c] for c in cols]
                if sweep < W - 1:
                    keep(value, target, r - 1)
                    continue
                if not first:
                    earlier = tiles(before, r - 1 - W, t)
                    value = [value[c] - step_tile * earlier[c] for c in cols]
                if r - 1 < H:
                    value = [one * low_ok for one in value]
                elif r - 1 >= H + R:
                    value = [one * high_ok for one in value]
                else:
                    for one in value:
                        total = total + one * one
                keep(value, grad, r - 1 - W, t)
            source = target
        for sweep in range(W):
            target = (a, b)[sweep % 2]
            held = []
            for r in range(W + sweep, RE - W - sweep):
                u = tiles(source, r) if sweep else tiles(grad, r - W, t)
                held = (held + [u])[-3:]
                if len(held) < 3:
                    continue
                change = stencil(*held, side)
                factor = tiles(kap, r - 1, which)
                value = [held[1][c] + factor[c] * change[c] for c in cols]
                if sweep < W - 1:
                    keep(value, target, r - 1)
                else:
                    keep(value, out, r - 1 - H, t)
            source = target
        return total

    total = lax.fori_loop(0, count, problem, jnp.zeros((SUB, LANES), f32))
    norm[...] = jnp.sum(total, axis=0, keepdims=True)
    sums = [None] * p.V
    for k in range(p.K):
        tile, j = p.inner(k, level)
        spread = gather(out, tile, strided(j, R)).astype(bf16).astype(f32)
        for v in range(p.V):
            term = members[k, v, level].astype(f32) * spread
            sums[v] = term if k == 0 else sums[v] + term
    for v in range(p.V):
        part[v] = p.ens * sums[v]
    for s in range(p.S):
        own = me * p.S + s
        if level:
            part[own] = part[own] + rest[level - 1, s]
            continue
        for l in range(p.L):
            tile, j = p.inner(p.K + s, l)
            value = p.stat * static_scale[s, l] * gather(out, tile, strided(j, R))
            if l:
                rest[l - 1, s] = value
            else:
                part[own] = part[own] + value
    if first:
        ship[...] = part[...].astype(bf16)
        return
    for shift in range(1, p.mem):
        base = lax.rem(me + shift, p.mem) * p.S
        for s in range(p.S):
            ship[shift - 1, s] = part[base + s].astype(bf16)


def curvature_kernel(p, first, *refs):
    parts, gots, norms, refs = refs[: p.L], refs[p.L : 2 * p.L], refs[2 * p.L : 3 * p.L], refs[3 * p.L :]
    if first:
        obs, cls, _, _, image, send = refs
    else:
        obs, cls, image_before, step, image, send = refs
    me = lax.axis_index("mem")
    total = jnp.zeros((p.R, p.X), f32)
    for l in range(p.L):
        if first:
            for v in range(p.V):
                value = parts[l][v]
                for other in range(p.mem - 1):
                    value = value + gots[l][other, v].astype(f32)
                image[v, l] = value
        for s in range(p.S):
            own = me * p.S + s
            if first:
                value = image[own, l]
                misfit = -obs[s, l]
            else:
                value = parts[l][own]
                for other in range(p.mem - 1):
                    value = value + gots[l][other, s].astype(f32)
                image[s, l] = value
                misfit = -(step[0:1, 0:1] * image_before[own, l]) - obs[s, l]
            index = cls[s, l]
            threshold = table(index, huber_levels)
            weight = jnp.where(index > 0, threshold / jnp.maximum(jnp.abs(misfit), threshold), 0.0)
            total = total + weight * value * value
    total = jnp.sum(total, axis=0, keepdims=True)
    total = sum(total[:, i * LANES : (i + 1) * LANES] for i in range(p.X // LANES))
    norm = sum(one[...] for one in norms)
    send[...] = jnp.broadcast_to(jnp.concatenate([norm, total], axis=1)[None], send.shape)


def final_kernel(p, got, step, image0, image1, *refs):
    before, after, outs = refs[: p.L], refs[p.L : 2 * p.L], refs[2 * p.L :]
    control, static_control, increment = outs
    me = lax.axis_index("mem")
    total = jnp.sum(got[...], axis=0)
    norm = jnp.sum(total[:, :LANES], axis=1, keepdims=True)
    curvature = jnp.sum(total[:, LANES:], axis=1, keepdims=True)
    second = norm / (norm + curvature)
    first = step[0:1, 0:1]
    for level in range(p.L):
        for field, l in p.fields(level):
            tile, lane = p.inner(field, l)
            where = strided(SWEEPS * SUB + lane, p.R)
            value = -(first * gather(before[level], tile, where)) - second * gather(after[level], tile, where)
            if field < p.K:
                control[field, l] = value
            else:
                static_control[field - p.K, l] = value
    for s in range(p.S):
        for l in range(p.L):
            increment[s, l] = -(first * image0[me * p.S + s, l]) - second * image1[s, l]


def call(kernel, outs, scratch, far=0, cost=0):
    vmem = pl.BlockSpec(memory_space=pltpu.VMEM)
    anywhere = pl.BlockSpec(memory_space=pltpu.MemorySpace.HBM)

    def run(*args):
        return pl.pallas_call(
            kernel,
            out_shape=tuple(jax.ShapeDtypeStruct(shape, dtype) for shape, dtype in outs),
            in_specs=[anywhere] * far + [vmem] * (len(args) - far),
            out_specs=tuple(vmem for _ in outs),
            scratch_shapes=scratch,
            compiler_params=pltpu.CompilerParams(vmem_limit_bytes=8 << 20),
            cost_estimate=pl.CostEstimate(flops=cost, bytes_accessed=cost, transcendentals=0),
        )(*[pltpu.with_memory_space_constraint(x, pltpu.MemorySpace.HBM) for x in args[:far]], *args[far:])

    return run


def local(members, static_scale, observed, huber_class, scale_index):
    p = Plan(members, static_scale, lax.axis_size("mem"), lax.axis_size("row"))
    K, V, L, R, X, S, C = p.K, p.V, p.L, p.R, p.X, p.S, p.C
    assert R >= 2 * SWEEPS

    def round_mem(block, shift):
        return lax.ppermute(block, "mem", [(i, (i + shift) % p.mem) for i in range(p.mem)])

    def round_row(block, shift):
        return lax.ppermute(block, "row", [(i, (i + shift) % p.row) for i in range(p.row)])

    vmem = lambda shape: pltpu.VMEM(shape, f32)
    part = functools.partial
    shifts = range(1, p.mem)
    own_shape = (S, L, R, X)
    full_shape = (V, L, R, X)
    back_shape = (p.PN, C, R * SUB, LANES)
    send_shape = ((p.devices, 1, 2 * LANES), f32)
    line = ((1, LANES), f32)

    obs, cls, own, code = call(
        part(load_kernel, p),
        [(own_shape, f32), (own_shape, jnp.int32), (own_shape, bf16), (own_shape, bf16)],
        [pltpu.SemaphoreType.DMA((2,))], far=2,
    )(observed, huber_class)
    others = jnp.stack([round_mem(own, shift) for shift in shifts])
    members, static_scale, scale_index = call(
        fetch_kernel,
        [(x.shape, x.dtype) for x in (members, static_scale, scale_index)],
        [pltpu.SemaphoreType.DMA((3,))], far=3, cost=4 << 20,
    )(members, static_scale, scale_index, own)
    obs_in = jnp.stack([round_mem(obs, shift) for shift in shifts])
    code_in = jnp.stack([round_mem(code, shift) for shift in shifts])

    grads, image, step, kap, sums = [], None, None, None, None
    for turn in range(ITERS):
        first = turn == 0
        sizes = [len(p.fields(level)) for level in range(L)]
        if first:
            sizes[0] += L
        msg_shapes = [((size, R, X), bf16) for size in sizes]
        if first:
            back, *msgs = call(
                part(back_kernel, p, True), [(back_shape, f32)] + msg_shapes, [vmem(full_shape)],
            )(members, static_scale, scale_index, own, others)
        else:
            back, step, *msgs = call(
                part(back_kernel, p, False), [(back_shape, f32), line] + msg_shapes, [vmem(full_shape)],
            )(members, static_scale, obs, cls, obs_in, code_in, image, sums)
        halos = [(round_row(msg, 1), round_row(msg, p.row - 1)) for msg in msgs]
        grad, norms, partial_images, gots, rest = [], [], [], [], None
        for level in range(L):
            count = p.tiles(level)
            args = [members, static_scale, back, *halos[level]]
            args += [scale_index] if first and level == 0 else [kap]
            args += [rest] if level else []
            args += [] if first else [grads[0][level], step]
            ship_shape = (V, R, X) if first else (p.mem - 1, S, R, X)
            outs = [((count, C, p.RG * SUB, LANES), f32), line, ((V, R, X), f32), (ship_shape, bf16)]
            if level == 0 and L > 1:
                outs.append(((L - 1, S, R, X), f32))
            if first and level == 0:
                outs.append(((L + p.ST, C, p.RE * SUB, LANES), f32))
            halo = vmem((count, C, 2 * SWEEPS * SUB, LANES))
            work = [halo, halo, vmem((C, p.RE * SUB, LANES)), vmem((C, p.RE * SUB, LANES))]
            g, norm, partial_image, ship, *more = call(
                part(sweep_kernel, p, first, level), outs, work + [vmem((count, C, R * SUB, LANES))],
                cost=8 << 20,
            )(*args)
            if level == 0 and L > 1:
                rest, *more = more
            if first and level == 0:
                kap = more[0]
            grad.append(g)
            norms.append(norm)
            partial_images.append(partial_image)
            gots.append(jnp.stack([round_mem(ship if first else ship[shift - 1], shift) for shift in shifts]))
        grads.append(grad)
        if first:
            image, send = call(
                part(curvature_kernel, p, True), [(full_shape, f32), send_shape], [],
            )(*partial_images, *gots, *norms, obs, cls, obs_in, code_in)
        else:
            last, send = call(
                part(curvature_kernel, p, False), [(own_shape, f32), send_shape], [],
            )(*partial_images, *gots, *norms, obs, cls, image, step)
        sums = lax.all_to_all(send, ("mem", "row"), 0, 0)
    return call(
        part(final_kernel, p),
        [((K, L, R, X), f32), (own_shape, f32), (own_shape, f32)], [],
    )(sums, step, image, last, *grads[0], *grads[1])


def solution(mesh):
    placed = (
        P("mem", None, None, "row", None),
        P("mem", None, "row", None),
        P("mem", None, "row", None),
        P("mem", None, "row", None),
        P(None, "row", None),
    )
    return jax.shard_map(
        local,
        mesh=mesh,
        in_specs=placed,
        out_specs=(
            P("mem", None, "row", None),
            P("mem", None, "row", None),
            P("mem", None, "row", None),
        ),
        check_vma=False,
    )
```

```python
import functools
import math

import jax
import jax.numpy as jnp
from jax import lax
from jax.experimental import pallas as pl
from jax.experimental.pallas import tpu as pltpu
from jax.sharding import PartitionSpec as P


SWEEPS = 4
ITERS = 2
SUB = 8
LANES = 128
kappa_table = (0.06, 0.11, 0.17, 0.23)
huber_levels = (1.0, 0.5, 1.0, 2.0)
f32 = jnp.float32
bf16 = jnp.bfloat16


def table(index, values):
    result = jnp.full(index.shape, values[3], f32)
    for entry in range(3):
        result = jnp.where(index == entry, f32(values[entry]), result)
    return result


class Plan:
    def __init__(self, members, static_scale, mem, row):
        self.K, self.V, self.L, self.R, self.X = members.shape
        self.S = static_scale.shape[0]
        self.mem, self.row = mem, row
        self.devices = mem * row
        self.KT = -(-self.K // SUB)
        self.ST = -(-(self.S * self.L) // SUB)
        self.PM = self.L * self.KT
        self.PN = self.PM + self.ST
        self.C = self.X // LANES
        self.RE = self.R + 4 * SWEEPS
        self.RG = self.R + 2 * SWEEPS
        self.pads = self.K % SUB != 0 or (self.S * self.L) % SUB != 0
        self.ens = math.sqrt(0.7 / (self.K * mem - 1))
        self.stat = math.sqrt(0.3)

    def fields(self, level):
        own = [(k, level) for k in range(self.K)]
        return own + [(self.K + s, l) for s in range(self.S) for l in range(self.L)] if level == self.L - 1 else own

    def tiles(self, level):
        return self.KT + self.ST if level == self.L - 1 else self.KT

    def inner(self, field, level):
        if field < self.K:
            return field // SUB, field % SUB
        at = (field - self.K) * self.L + level
        return self.KT + at // SUB, at % SUB

    def slot(self, field, level):
        if field < self.K:
            return level * self.KT + field // SUB, field % SUB
        at = (field - self.K) * self.L + level
        return self.PM + at // SUB, at % SUB


def strided(start, count):
    return pl.ds(start, count, stride=SUB)


def scatter(ref, tile, where, value):
    for c in range(value.shape[1] // LANES):
        ref[tile, c, where, :] = value[:, c * LANES : (c + 1) * LANES]


def gather(ref, tile, where):
    return jnp.concatenate([ref[tile, c, where, :] for c in range(ref.shape[1])], axis=1)


def onehot(p):
    source = lax.broadcasted_iota(jnp.int32, (p.X, p.X), 0)
    target = lax.broadcasted_iota(jnp.int32, (p.X, p.X), 1)
    return jnp.where(source == (target % LANES) * p.C + target // LANES, 1.0, 0.0).astype(bf16)


def product(block, matrix, back=False):
    dims = (((1,), (1 if back else 0,)), ((), ()))
    return lax.dot_general(block, matrix, dims, preferred_element_type=f32)


def exact(block, matrix, back=False):
    first = block.astype(bf16)
    left = block - first.astype(f32)
    second = left.astype(bf16)
    third = (left - second.astype(f32)).astype(bf16)
    return product(first, matrix, back) + (product(second, matrix, back) + product(third, matrix, back))


def load_kernel(p, obs, cls, obs_out, cls_out, sent, sems):
    pairs = ((obs, obs_out), (cls, cls_out))
    copies = [pltpu.make_async_copy(src, dst, sems.at[i]) for i, (src, dst) in enumerate(pairs)]
    for copy in copies:
        copy.start()
    for copy in copies:
        copy.wait()
    for s in range(p.S):
        for l in range(p.L):
            index = cls_out[s, l]
            threshold = table(index, huber_levels)
            clipped = jnp.where(index > 0, jnp.clip(-obs_out[s, l], -threshold, threshold), 0.0)
            sent[s, l] = clipped.astype(bf16)


def fetch_kernel(p, members, static_scale, scale_index, obs, cls, own, members_out, static_out, scale_out, pack,
                 own_out, matrix_out, raw, static_raw, scale_raw, sems):
    copies = [pltpu.make_async_copy(members.at[k], raw.at[k], sems.at[k]) for k in range(p.K)]
    rest = [
        pltpu.make_async_copy(static_scale, static_raw, sems.at[p.K]),
        pltpu.make_async_copy(scale_index, scale_raw, sems.at[p.K + 1]),
    ]
    for copy in copies + rest:
        copy.start()
    matrix_out[...] = onehot(p)
    matrix = matrix_out[...]
    rows = p.S * p.L * p.R
    own_out[...] = product(own[...].reshape(rows, p.X), matrix).astype(bf16).reshape(own_out.shape)
    shape = (p.S, p.L, p.R, p.X)
    pack[0] = exact(obs[...].reshape(rows, p.X), matrix).reshape(shape)
    pack[1] = product(cls[...].astype(f32).astype(bf16).reshape(rows, p.X), matrix).reshape(shape)
    for copy in rest:
        copy.wait()
    static_out[...] = exact(static_raw[...].reshape(rows, p.X), matrix).reshape(shape)
    scale = scale_raw[...].astype(f32).astype(bf16).reshape(p.L * p.R, p.X)
    scale_out[...] = product(scale, matrix).reshape(scale_out.shape)
    for k in range(p.K):
        copies[k].wait()
        block = raw[k].reshape(p.V * p.L * p.R, p.X)
        members_out[k] = product(block, matrix).astype(bf16).reshape(p.V, p.L, p.R, p.X)


def back_kernel(p, first, *refs):
    if first:
        members, static_scale, scale_index, own, others, matrix, back, *msgs, sent = refs
    else:
        members, static_scale, pack, pack_in, image, got, back, step_out, *msgs, sent = refs
    me = lax.axis_index("mem")
    if p.pads:
        back[...] = jnp.zeros(back.shape, f32)
    if not first:
        total = jnp.sum(got[...], axis=0)
        norm = jnp.sum(total[:, :LANES], axis=1, keepdims=True)
        curvature = jnp.sum(total[:, LANES:], axis=1, keepdims=True)
        step = norm / (norm + curvature)
        step_out[...] = jnp.broadcast_to(step, step_out.shape)
    for shift in range(p.mem):
        base = lax.rem(me + (p.mem - shift), p.mem) * p.S
        if first and shift:
            block = product(others[shift - 1].reshape(p.S * p.L * p.R, p.X), matrix[...])
            block = block.reshape(p.S, p.L, p.R, p.X)
        for s in range(p.S):
            for l in range(p.L):
                if first:
                    rounded = block[s, l] if shift else own[s, l].astype(f32)
                else:
                    if shift == 0:
                        seen, index = pack[0, s, l], pack[1, s, l]
                    else:
                        seen, index = pack_in[shift - 1, 0, s, l], pack_in[shift - 1, 1, s, l]
                    threshold = table(index, huber_levels)
                    misfit = -(step * image[base + s, l]) - seen
                    clipped = jnp.where(index > 0, jnp.clip(misfit, -threshold, threshold), 0.0)
                    rounded = clipped.astype(bf16).astype(f32)
                sent[base + s, l] = rounded
                if shift == 0:
                    tile, lane = p.slot(p.K + s, l)
                    value = p.stat * static_scale[s, l] * rounded
                    scatter(back, tile, strided(lane, p.R), value)
                    msgs[p.L - 1][p.K + s * p.L + l] = value.astype(bf16)
    if first:
        for l in range(p.L):
            msgs[0][len(p.fields(0)) + l] = scale_index[l].astype(bf16)
    for l in range(p.L):
        for k in range(p.K):
            value = members[k, 0, l].astype(f32) * sent[0, l]
            for v in range(1, p.V):
                value = value + members[k, v, l].astype(f32) * sent[v, l]
            value = p.ens * value
            tile, lane = p.slot(k, l)
            scatter(back, tile, strided(lane, p.R), value)
            msgs[l][k] = value.astype(bf16)


def sideways(u, first_lane, last_lane):
    zero = jnp.zeros_like(u[0])
    before = jnp.where(first_lane, zero, pltpu.roll(u[-1], 1, 1))
    after = jnp.where(last_lane, zero, pltpu.roll(u[0], LANES - 1, 1))
    around = [before] + list(u) + [after]
    return [around[i] + around[i + 2] for i in range(len(u))]


def stencil(above, here, below, side):
    across = side(here)
    return [(above[c] + below[c]) + across[c] - 4.0 * here[c] for c in range(len(here))]


def sweep_kernel(p, first, level, *refs):
    refs = list(refs)
    members, static_scale, back, low, high = refs[:5]
    refs = refs[5:]
    if first and level == 0:
        scale_index, *refs = refs
    else:
        kap, *refs = refs
    if not first:
        before, step, *refs = refs
    grad, norm, part, ship, *refs = refs
    last = level == p.L - 1
    if last and p.L > 1:
        rest, *refs = refs
    if first and level == 0:
        kap, *refs = refs
    lo, hi, a, b, out = refs
    me, at = lax.axis_index("mem"), lax.axis_index("row")
    low_ok = jnp.where(at > 0, 1.0, 0.0).astype(f32)
    high_ok = jnp.where(at < p.row - 1, 1.0, 0.0).astype(f32)
    R, RE, W = p.R, p.RE, SWEEPS
    H = 2 * W
    fields = p.fields(level)
    count = p.tiles(level)
    for ref, dst in ((low, lo), (high, hi)):
        if p.pads:
            dst[...] = jnp.zeros(dst.shape, f32)
        skip = R - H if ref is low else 0
        for i, (field, l) in enumerate(fields):
            tile, lane = p.inner(field, l)
            scatter(dst, tile, strided(lane, H), ref[i].astype(f32)[skip : skip + H])
    if first and level == 0:
        for l in range(p.L):
            pieces = (
                (table(low[len(fields) + l].astype(f32)[R - H :], kappa_table) * low_ok, 0),
                (table(scale_index[l], kappa_table), H),
                (table(high[len(fields) + l].astype(f32)[:H], kappa_table) * high_ok, H + R),
            )
            for value, offset in pieces:
                for r in range(value.shape[0]):
                    scatter(kap, l, pl.ds((offset + r) * SUB, SUB), jnp.broadcast_to(value[r : r + 1], (SUB, p.X)))
                for j in range(p.ST * SUB):
                    if (j % p.L) == l:
                        scatter(kap, p.L + j // SUB, strided(offset * SUB + j % SUB, value.shape[0]), value)
    lane = lax.broadcasted_iota(jnp.int32, (SUB, LANES), 1)
    first_lane, last_lane = lane == 0, lane == LANES - 1
    side = functools.partial(sideways, first_lane=first_lane, last_lane=last_lane)
    cols = range(p.C)

    def tiles(ref, r, *lead):
        return [ref[(*lead, c, pl.ds(r * SUB, SUB), slice(None))] for c in cols]

    def keep(value, ref, r, *lead):
        for c in cols:
            ref[(*lead, c, pl.ds(r * SUB, SUB), slice(None))] = value[c]

    if not first:
        step_tile = jnp.broadcast_to(step[0:1, 0:1], (SUB, LANES))

    def problem(t, total):
        which, whole = level, t + level * p.KT
        if last:
            which = jnp.where(t < p.KT, level, t - p.KT + p.L)
            whole = jnp.where(t < p.KT, whole, t - p.KT + p.PM)
        source = None
        for sweep in range(W):
            target = (a, b)[sweep % 2]
            held = []
            for r in range(sweep, RE - sweep):
                if sweep:
                    u = tiles(source, r)
                elif r < H:
                    u = tiles(lo, r, t)
                elif r < H + R:
                    u = tiles(back, r - H, whole)
                else:
                    u = tiles(hi, r - H - R, t)
                factor = tiles(kap, r, which)
                w = [factor[c] * u[c] for c in cols]
                held = (held + [(u, w)])[-3:]
                if len(held) < 3:
                    continue
                (_, w0), (u1, w1), (_, w2) = held
                change = stencil(w0, w1, w2, side)
                value = [u1[c] + change[c] for c in cols]
                if sweep < W - 1:
                    keep(value, target, r - 1)
                    continue
                if not first:
                    earlier = tiles(before, r - 1 - W, t)
                    value = [value[c] - step_tile * earlier[c] for c in cols]
                if r - 1 < H:
                    value = [one * low_ok for one in value]
                elif r - 1 >= H + R:
                    value = [one * high_ok for one in value]
                else:
                    for one in value:
                        total = total + one * one
                keep(value, grad, r - 1 - W, t)
            source = target
        for sweep in range(W):
            target = (a, b)[sweep % 2]
            held = []
            for r in range(W + sweep, RE - W - sweep):
                u = tiles(source, r) if sweep else tiles(grad, r - W, t)
                held = (held + [u])[-3:]
                if len(held) < 3:
                    continue
                change = stencil(*held, side)
                factor = tiles(kap, r - 1, which)
                value = [held[1][c] + factor[c] * change[c] for c in cols]
                if sweep < W - 1:
                    keep(value, target, r - 1)
                else:
                    keep(value, out, r - 1 - H, t)
            source = target
        return total

    total = lax.fori_loop(0, count, problem, jnp.zeros((SUB, LANES), f32))
    norm[...] = jnp.sum(total, axis=0, keepdims=True)
    sums = [None] * p.V
    for k in range(p.K):
        tile, j = p.inner(k, level)
        spread = gather(out, tile, strided(j, R)).astype(bf16).astype(f32)
        for v in range(p.V):
            term = members[k, v, level].astype(f32) * spread
            sums[v] = term if k == 0 else sums[v] + term
    for v in range(p.V):
        part[v] = p.ens * sums[v]
    if last:
        for s in range(p.S):
            own = me * p.S + s
            for l in range(p.L):
                tile, j = p.inner(p.K + s, l)
                value = p.stat * static_scale[s, l] * gather(out, tile, strided(j, R))
                if l == level:
                    part[own] = part[own] + value
                else:
                    rest[l, s] = value
    if first:
        for v in range(p.V):
            ship[v] = part[v].astype(bf16)
        if last:
            for l in range(p.L - 1):
                for s in range(p.S):
                    ship[p.V + l * p.S + s] = rest[l, s].astype(bf16)
        return
    for shift in range(1, p.mem):
        base = lax.rem(me + shift, p.mem) * p.S
        for s in range(p.S):
            ship[shift - 1, s] = part[base + s].astype(bf16)


def curvature_kernel(p, first, *refs):
    parts, gots, norms, refs = refs[: p.L], refs[p.L : 2 * p.L], refs[2 * p.L : 3 * p.L], refs[3 * p.L :]
    if p.L > 1:
        rest, *refs = refs
    if first:
        pack, _, image, send = refs
    else:
        pack, image_before, step, image, send = refs
    me = lax.axis_index("mem")
    total = jnp.zeros((p.R, p.X), f32)
    for l in range(p.L):
        if first:
            for v in range(p.V):
                value = parts[l][v]
                for other in range(p.mem - 1):
                    value = value + gots[l][other, v].astype(f32)
                image[v, l] = value
            if l < p.L - 1:
                for s in range(p.S):
                    own = me * p.S + s
                    image[own, l] = image[own, l] + rest[l, s]
                    for other in range(p.mem - 1):
                        theirs = lax.rem(me + (p.mem - 1 - other), p.mem) * p.S + s
                        value = gots[p.L - 1][other, p.V + l * p.S + s].astype(f32)
                        image[theirs, l] = image[theirs, l] + value
        for s in range(p.S):
            own = me * p.S + s
            if first:
                value = image[own, l]
                misfit = -pack[0, s, l]
            else:
                value = parts[l][own]
                if l < p.L - 1:
                    value = value + rest[l, s]
                for other in range(p.mem - 1):
                    value = value + gots[l][other, s].astype(f32)
                image[s, l] = value
                misfit = -(step[0:1, 0:1] * image_before[own, l]) - pack[0, s, l]
            index = pack[1, s, l]
            threshold = table(index, huber_levels)
            weight = jnp.where(index > 0, threshold / jnp.maximum(jnp.abs(misfit), threshold), 0.0)
            total = total + weight * value * value
    total = jnp.sum(total, axis=0, keepdims=True)
    total = sum(total[:, i * LANES : (i + 1) * LANES] for i in range(p.X // LANES))
    norm = sum(one[...] for one in norms)
    send[...] = jnp.broadcast_to(jnp.concatenate([norm, total], axis=1)[None], send.shape)


def final_kernel(p, got, step, image0, image1, matrix_ref, *refs):
    before, after, outs = refs[: p.L], refs[p.L : 2 * p.L], refs[2 * p.L :]
    control, static_control, increment = outs
    me = lax.axis_index("mem")
    total = jnp.sum(got[...], axis=0)
    norm = jnp.sum(total[:, :LANES], axis=1, keepdims=True)
    curvature = jnp.sum(total[:, LANES:], axis=1, keepdims=True)
    second = norm / (norm + curvature)
    first = step[0:1, 0:1]
    matrix = matrix_ref[...]

    def natural(blocks):
        whole = exact(jnp.concatenate(blocks, axis=0), matrix, True)
        return [whole[i * p.R : (i + 1) * p.R] for i in range(len(blocks))]

    for level in range(p.L):
        fields = p.fields(level)
        for begin in range(0, len(fields), 8):
            some = fields[begin : begin + 8]
            blocks = []
            for field, l in some:
                tile, lane = p.inner(field, l)
                where = strided(SWEEPS * SUB + lane, p.R)
                blocks.append(-(first * gather(before[level], tile, where)) - second * gather(after[level], tile, where))
            for (field, l), value in zip(some, natural(blocks)):
                if field < p.K:
                    control[field, l] = value
                else:
                    static_control[field - p.K, l] = value
    some = [(s, l) for s in range(p.S) for l in range(p.L)]
    blocks = [-(first * image0[me * p.S + s, l]) - second * image1[s, l] for s, l in some]
    for (s, l), value in zip(some, natural(blocks)):
        increment[s, l] = value


def call(kernel, outs, scratch, far=0, cost=0):
    vmem = pl.BlockSpec(memory_space=pltpu.VMEM)
    anywhere = pl.BlockSpec(memory_space=pltpu.MemorySpace.HBM)

    def run(*args):
        return pl.pallas_call(
            kernel,
            out_shape=tuple(jax.ShapeDtypeStruct(shape, dtype) for shape, dtype in outs),
            in_specs=[anywhere] * far + [vmem] * (len(args) - far),
            out_specs=tuple(vmem for _ in outs),
            scratch_shapes=scratch,
            compiler_params=pltpu.CompilerParams(vmem_limit_bytes=8 << 20),
            cost_estimate=pl.CostEstimate(flops=cost, bytes_accessed=cost, transcendentals=0),
        )(*[pltpu.with_memory_space_constraint(x, pltpu.MemorySpace.HBM) for x in args[:far]], *args[far:])

    return run


def local(members, static_scale, observed, huber_class, scale_index):
    p = Plan(members, static_scale, lax.axis_size("mem"), lax.axis_size("row"))
    K, V, L, R, X, S, C = p.K, p.V, p.L, p.R, p.X, p.S, p.C
    assert R >= 2 * SWEEPS

    def round_mem(block, shift):
        return lax.ppermute(block, "mem", [(i, (i + shift) % p.mem) for i in range(p.mem)])

    def round_row(block, shift):
        return lax.ppermute(block, "row", [(i, (i + shift) % p.row) for i in range(p.row)])

    vmem = lambda shape: pltpu.VMEM(shape, f32)
    part = functools.partial
    shifts = range(1, p.mem)
    own_shape = (S, L, R, X)
    full_shape = (V, L, R, X)
    back_shape = (p.PN, C, R * SUB, LANES)
    send_shape = ((p.devices, 1, 2 * LANES), f32)
    line = ((1, LANES), f32)

    obs, cls, own = call(
        part(load_kernel, p), [(own_shape, f32), (own_shape, jnp.int32), (own_shape, bf16)],
        [pltpu.SemaphoreType.DMA((2,))], far=2,
    )(observed, huber_class)
    others = jnp.stack([round_mem(own, shift) for shift in shifts])
    scratch = [pltpu.VMEM(x.shape, x.dtype) for x in (members, static_scale, scale_index)]
    members, static_scale, scale_index, pack, own, matrix = call(
        part(fetch_kernel, p),
        [(members.shape, bf16), (own_shape, f32), ((L, R, X), f32), ((2,) + own_shape, f32), (own_shape, bf16), ((X, X), bf16)],
        scratch + [pltpu.SemaphoreType.DMA((K + 2,))], far=3, cost=4 << 20,
    )(members, static_scale, scale_index, obs, cls, own)
    pack_in = jnp.stack([round_mem(pack, shift) for shift in shifts])

    grads, image, step, kap, sums = [], None, None, None, None
    for turn in range(ITERS):
        first = turn == 0
        sizes = [len(p.fields(level)) for level in range(L)]
        if first:
            sizes[0] += L
        msg_shapes = [((size, R, X), bf16) for size in sizes]
        if first:
            back, *msgs = call(
                part(back_kernel, p, True), [(back_shape, f32)] + msg_shapes, [vmem(full_shape)],
            )(members, static_scale, scale_index, own, others, matrix)
        else:
            back, step, *msgs = call(
                part(back_kernel, p, False), [(back_shape, f32), line] + msg_shapes, [vmem(full_shape)],
            )(members, static_scale, pack, pack_in, image, sums)
        halos = []
        for msg in msgs:
            low = round_row(msg, 1)
            high = round_row(msg, p.row - 1)
            halos.append((low, high))
        grad, norms, partial_images, gots, rest = [], [], [], [], None
        for level in range(L):
            count = p.tiles(level)
            args = [members, static_scale, back, *halos[level]]
            args += [scale_index] if first and level == 0 else [kap]
            args += [] if first else [grads[0][level], step]
            last = level == L - 1
            ship_shape = (V + (L - 1) * S if last else V, R, X) if first else (p.mem - 1, S, R, X)
            outs = [((count, C, p.RG * SUB, LANES), f32), line, ((V, R, X), f32), (ship_shape, bf16)]
            if last and L > 1:
                outs.append(((L - 1, S, R, X), f32))
            if first and level == 0:
                outs.append(((L + p.ST, C, p.RE * SUB, LANES), f32))
            halo = vmem((count, C, 2 * SWEEPS * SUB, LANES))
            work = [halo, halo, vmem((C, p.RE * SUB, LANES)), vmem((C, p.RE * SUB, LANES))]
            g, norm, partial_image, ship, *more = call(
                part(sweep_kernel, p, first, level), outs, work + [vmem((count, C, R * SUB, LANES))],
                cost=8 << 20,
            )(*args)
            if last and L > 1:
                rest, *more = more
            if first and level == 0:
                kap = more[0]
            grad.append(g)
            norms.append(norm)
            partial_images.append(partial_image)
            gots.append(jnp.stack([round_mem(ship if first else ship[shift - 1], shift) for shift in shifts]))
        grads.append(grad)
        extra = [rest] if L > 1 else []
        if first:
            image, send = call(
                part(curvature_kernel, p, True), [(full_shape, f32), send_shape], [],
            )(*partial_images, *gots, *norms, *extra, pack, pack_in)
        else:
            final_image, send = call(
                part(curvature_kernel, p, False), [(own_shape, f32), send_shape], [],
            )(*partial_images, *gots, *norms, *extra, pack, image, step)
        sums = lax.all_to_all(send, ("mem", "row"), 0, 0)
    return call(
        part(final_kernel, p),
        [((K, L, R, X), f32), (own_shape, f32), (own_shape, f32)], [],
    )(sums, step, image, final_image, matrix, *grads[0], *grads[1])


def solution(mesh):
    placed = (
        P("mem", None, None, "row", None),
        P("mem", None, "row", None),
        P("mem", None, "row", None),
        P("mem", None, "row", None),
        P(None, "row", None),
    )
    return jax.shard_map(
        local,
        mesh=mesh,
        in_specs=placed,
        out_specs=(
            P("mem", None, "row", None),
            P("mem", None, "row", None),
            P("mem", None, "row", None),
        ),
        check_vma=False,
    )
```

```python
import functools
import math

import jax
import jax.numpy as jnp
from jax import lax
from jax.experimental import pallas as pl
from jax.experimental.pallas import tpu as pltpu
from jax.sharding import PartitionSpec as P


SWEEPS = 4
ITERS = 2
SUB = 8
LANES = 128
kappa_table = (0.06, 0.11, 0.17, 0.23)
huber_levels = (1.0, 0.5, 1.0, 2.0)
f32 = jnp.float32
bf16 = jnp.bfloat16


def table(index, values):
    result = jnp.full(index.shape, values[3], f32)
    for entry in range(3):
        result = jnp.where(index == entry, f32(values[entry]), result)
    return result


class Plan:
    def __init__(self, members, static_scale, mem, row):
        self.K, self.V, self.L, self.R, self.X = members.shape
        self.S = static_scale.shape[0]
        self.mem, self.row = mem, row
        self.devices = mem * row
        self.KT = -(-self.K // SUB)
        self.ST = -(-(self.S * self.L) // SUB)
        self.PM = self.L * self.KT
        self.PN = self.PM + self.ST
        self.C = self.X // LANES
        self.RE = self.R + 4 * SWEEPS
        self.RG = self.R + 2 * SWEEPS
        self.pads = self.K % SUB != 0 or (self.S * self.L) % SUB != 0
        self.ens = math.sqrt(0.7 / (self.K * mem - 1))
        self.stat = math.sqrt(0.3)

    def fields(self, level):
        own = [(k, level) for k in range(self.K)]
        return own + [(self.K + s, l) for s in range(self.S) for l in range(self.L)] if level == self.L - 1 else own

    def tiles(self, level):
        return self.KT + self.ST if level == self.L - 1 else self.KT

    def inner(self, field, level):
        if field < self.K:
            return field // SUB, field % SUB
        at = (field - self.K) * self.L + level
        return self.KT + at // SUB, at % SUB

    def slot(self, field, level):
        if field < self.K:
            return level * self.KT + field // SUB, field % SUB
        at = (field - self.K) * self.L + level
        return self.PM + at // SUB, at % SUB


def strided(start, count):
    return pl.ds(start, count, stride=SUB)


def scatter(ref, tile, where, value):
    for c in range(value.shape[1] // LANES):
        ref[tile, c, where, :] = value[:, c * LANES : (c + 1) * LANES]


def gather(ref, tile, where):
    return jnp.concatenate([ref[tile, c, where, :] for c in range(ref.shape[1])], axis=1)


def onehot(p):
    source = lax.broadcasted_iota(jnp.int32, (p.X, p.X), 0)
    target = lax.broadcasted_iota(jnp.int32, (p.X, p.X), 1)
    return jnp.where(source == (target % LANES) * p.C + target // LANES, 1.0, 0.0).astype(bf16)


def product(block, matrix, back=False):
    dims = (((1,), (1 if back else 0,)), ((), ()))
    return lax.dot_general(block, matrix, dims, preferred_element_type=f32)


def pieces(block):
    first = block.astype(bf16)
    left = block - first.astype(f32)
    second = left.astype(bf16)
    return [first, second, (left - second.astype(f32)).astype(bf16)]


def products(blocks, matrix, back=False):
    parts = [pieces(block) if block.dtype == f32 else [block] for block in blocks]
    flat = [one for part in parts for one in part]
    whole = product(jnp.concatenate(flat, axis=0), matrix, back)
    out, at = [], 0
    for part in parts:
        rows = part[0].shape[0]
        cut = [whole[at + i * rows : at + (i + 1) * rows] for i in range(len(part))]
        out.append(cut[0] if len(cut) == 1 else cut[0] + (cut[1] + cut[2]))
        at += rows * len(part)
    return out


def load_kernel(p, obs, cls, obs_out, cls_out, sent, sems):
    pairs = ((obs, obs_out), (cls, cls_out))
    copies = [pltpu.make_async_copy(src, dst, sems.at[i]) for i, (src, dst) in enumerate(pairs)]
    for copy in copies:
        copy.start()
    for copy in copies:
        copy.wait()
    for s in range(p.S):
        for l in range(p.L):
            index = cls_out[s, l]
            threshold = table(index, huber_levels)
            clipped = jnp.where(index > 0, jnp.clip(-obs_out[s, l], -threshold, threshold), 0.0)
            sent[s, l] = clipped.astype(bf16)


def fetch_kernel(p, members, static_scale, scale_index, obs, cls, own, members_out, static_out, scale_out, pack,
                 own_out, matrix_out, raw, static_raw, scale_raw, sems):
    copies = [pltpu.make_async_copy(members.at[k], raw.at[k], sems.at[k]) for k in range(p.K)]
    rest = [
        pltpu.make_async_copy(static_scale, static_raw, sems.at[p.K]),
        pltpu.make_async_copy(scale_index, scale_raw, sems.at[p.K + 1]),
    ]
    for copy in copies + rest:
        copy.start()
    matrix_out[...] = onehot(p)
    matrix = matrix_out[...]
    rows = p.S * p.L * p.R
    shape = (p.S, p.L, p.R, p.X)
    flat = lambda x: x.reshape(rows, p.X)
    for copy in rest:
        copy.wait()
    scale = scale_raw[...].astype(f32).astype(bf16).reshape(p.L * p.R, p.X)
    blocks = [flat(own[...]), flat(obs[...]), flat(cls[...].astype(f32).astype(bf16)), flat(static_raw[...]), scale]
    blocks = products(blocks, matrix)
    own_out[...] = blocks[0].astype(bf16).reshape(shape)
    pack[0] = blocks[1].reshape(shape)
    pack[1] = blocks[2].reshape(shape)
    static_out[...] = blocks[3].reshape(shape)
    scale_out[...] = blocks[4].reshape(scale_out.shape)
    step = -(-p.K // 1)
    for k in range(0, p.K, step):
        some = min(step, p.K - k)
        for copy in copies[k : k + some]:
            copy.wait()
        block = raw[k : k + some].reshape(some * p.V * p.L * p.R, p.X)
        block = product(block, matrix).astype(bf16)
        members_out[k : k + some] = block.reshape(some, p.V, p.L, p.R, p.X)


def back_kernel(p, first, *refs):
    if first:
        members, static_scale, scale_index, own, others, matrix, back, *msgs, sent = refs
    else:
        members, static_scale, pack, pack_in, image, got, back, step_out, *msgs, sent = refs
    me = lax.axis_index("mem")
    if p.pads:
        back[...] = jnp.zeros(back.shape, f32)
    if not first:
        total = jnp.sum(got[...], axis=0)
        norm = jnp.sum(total[:, :LANES], axis=1, keepdims=True)
        curvature = jnp.sum(total[:, LANES:], axis=1, keepdims=True)
        step = norm / (norm + curvature)
        step_out[...] = jnp.broadcast_to(step, step_out.shape)
    for shift in range(p.mem):
        base = lax.rem(me + (p.mem - shift), p.mem) * p.S
        if first and shift:
            block = product(others[shift - 1].reshape(p.S * p.L * p.R, p.X), matrix[...])
            block = block.reshape(p.S, p.L, p.R, p.X)
        for s in range(p.S):
            for l in range(p.L):
                if first:
                    rounded = block[s, l] if shift else own[s, l].astype(f32)
                else:
                    if shift == 0:
                        seen, index = pack[0, s, l], pack[1, s, l]
                    else:
                        seen, index = pack_in[shift - 1, 0, s, l], pack_in[shift - 1, 1, s, l]
                    threshold = table(index, huber_levels)
                    misfit = -(step * image[base + s, l]) - seen
                    clipped = jnp.where(index > 0, jnp.clip(misfit, -threshold, threshold), 0.0)
                    rounded = clipped.astype(bf16).astype(f32)
                sent[base + s, l] = rounded
                if shift == 0:
                    tile, lane = p.slot(p.K + s, l)
                    value = p.stat * static_scale[s, l] * rounded
                    scatter(back, tile, strided(lane, p.R), value)
                    msgs[p.L - 1][p.K + s * p.L + l] = value.astype(bf16)
    if first:
        for l in range(p.L):
            msgs[0][len(p.fields(0)) + l] = scale_index[l].astype(bf16)
    for l in range(p.L):
        for k in range(p.K):
            value = members[k, 0, l].astype(f32) * sent[0, l]
            for v in range(1, p.V):
                value = value + members[k, v, l].astype(f32) * sent[v, l]
            value = p.ens * value
            tile, lane = p.slot(k, l)
            scatter(back, tile, strided(lane, p.R), value)
            msgs[l][k] = value.astype(bf16)


def sideways(u, first_lane, last_lane):
    zero = jnp.zeros_like(u[0])
    before = jnp.where(first_lane, zero, pltpu.roll(u[-1], 1, 1))
    after = jnp.where(last_lane, zero, pltpu.roll(u[0], LANES - 1, 1))
    around = [before] + list(u) + [after]
    return [around[i] + around[i + 2] for i in range(len(u))]


def stencil(above, here, below, side):
    across = side(here)
    return [(above[c] + below[c]) + across[c] - 4.0 * here[c] for c in range(len(here))]


def sweep_kernel(p, first, level, *refs):
    refs = list(refs)
    members, static_scale, back, near, far = refs[:5]
    refs = refs[5:]
    if first and level == 0:
        scale_index, *refs = refs
    else:
        kap, *refs = refs
    if not first:
        before, step, *refs = refs
    grad, norm, part, ship, *refs = refs
    last = level == p.L - 1
    if last and p.L > 1:
        rest, *refs = refs
    if first and level == 0:
        kap, *refs = refs
    ends, a, b, out = refs
    me, at = lax.axis_index("mem"), lax.axis_index("row")
    low_ok = jnp.where(at > 0, 1.0, 0.0).astype(f32)
    high_ok = jnp.where(at < p.row - 1, 1.0, 0.0).astype(f32)
    R, RE, W = p.R, p.RE, SWEEPS
    H = 2 * W
    fields = p.fields(level)
    count = p.tiles(level)
    odd = lax.rem(at, 2)
    if p.pads:
        ends[...] = jnp.zeros(ends.shape, f32)

    def edge(value, side):
        if R == H:
            return value
        return jnp.where(side == 0, value[R - H :], value[:H])

    for ref, side in ((near, 1 - odd), (far, odd)):
        for i, (field, l) in enumerate(fields):
            tile, lane = p.inner(field, l)
            scatter(ends.at[side], tile, strided(lane, H), edge(ref[i].astype(f32), side))
    if first and level == 0:
        for l in range(p.L):
            pieces_of = [(table(scale_index[l], kappa_table), H)]
            for ref, side in ((near, 1 - odd), (far, odd)):
                value = table(edge(ref[len(fields) + l].astype(f32), side), kappa_table)
                pieces_of.append((value * jnp.where(side == 0, low_ok, high_ok), side * (H + R)))
            for value, offset in pieces_of:
                start = offset * SUB if isinstance(offset, int) else pl.multiple_of(offset * SUB, SUB)
                for r in range(value.shape[0]):
                    scatter(kap, l, pl.ds(start + r * SUB, SUB), jnp.broadcast_to(value[r : r + 1], (SUB, p.X)))
                for j in range(p.ST * SUB):
                    if (j % p.L) == l:
                        scatter(kap, p.L + j // SUB, strided(start + j % SUB, value.shape[0]), value)
    lane = lax.broadcasted_iota(jnp.int32, (SUB, LANES), 1)
    first_lane, last_lane = lane == 0, lane == LANES - 1
    side = functools.partial(sideways, first_lane=first_lane, last_lane=last_lane)
    cols = range(p.C)

    def tiles(ref, r, *lead):
        return [ref[(*lead, c, pl.ds(r * SUB, SUB), slice(None))] for c in cols]

    def keep(value, ref, r, *lead):
        for c in cols:
            ref[(*lead, c, pl.ds(r * SUB, SUB), slice(None))] = value[c]

    if not first:
        step_tile = jnp.broadcast_to(step[0:1, 0:1], (SUB, LANES))

    def problem(t, total):
        which, whole = level, t + level * p.KT
        if last:
            which = jnp.where(t < p.KT, level, t - p.KT + p.L)
            whole = jnp.where(t < p.KT, whole, t - p.KT + p.PM)
        source = None
        for sweep in range(W):
            target = (a, b)[sweep % 2]
            held = []
            for r in range(sweep, RE - sweep):
                if sweep:
                    u = tiles(source, r)
                elif r < H:
                    u = tiles(ends, r, 0, t)
                elif r < H + R:
                    u = tiles(back, r - H, whole)
                else:
                    u = tiles(ends, r - H - R, 1, t)
                factor = tiles(kap, r, which)
                w = [factor[c] * u[c] for c in cols]
                held = (held + [(u, w)])[-3:]
                if len(held) < 3:
                    continue
                (_, w0), (u1, w1), (_, w2) = held
                change = stencil(w0, w1, w2, side)
                value = [u1[c] + change[c] for c in cols]
                if sweep < W - 1:
                    keep(value, target, r - 1)
                    continue
                if not first:
                    earlier = tiles(before, r - 1 - W, t)
                    value = [value[c] - step_tile * earlier[c] for c in cols]
                if r - 1 < H:
                    value = [one * low_ok for one in value]
                elif r - 1 >= H + R:
                    value = [one * high_ok for one in value]
                else:
                    for one in value:
                        total = total + one * one
                keep(value, grad, r - 1 - W, t)
            source = target
        for sweep in range(W):
            target = (a, b)[sweep % 2]
            held = []
            for r in range(W + sweep, RE - W - sweep):
                u = tiles(source, r) if sweep else tiles(grad, r - W, t)
                held = (held + [u])[-3:]
                if len(held) < 3:
                    continue
                change = stencil(*held, side)
                factor = tiles(kap, r - 1, which)
                value = [held[1][c] + factor[c] * change[c] for c in cols]
                if sweep < W - 1:
                    keep(value, target, r - 1)
                else:
                    keep(value, out, r - 1 - H, t)
            source = target
        return total

    total = lax.fori_loop(0, count, problem, jnp.zeros((SUB, LANES), f32))
    norm[...] = jnp.sum(total, axis=0, keepdims=True)
    sums = [None] * p.V
    for k in range(p.K):
        tile, j = p.inner(k, level)
        spread = gather(out, tile, strided(j, R)).astype(bf16).astype(f32)
        for v in range(p.V):
            term = members[k, v, level].astype(f32) * spread
            sums[v] = term if k == 0 else sums[v] + term
    for v in range(p.V):
        part[v] = p.ens * sums[v]
    if last:
        for s in range(p.S):
            own = me * p.S + s
            for l in range(p.L):
                tile, j = p.inner(p.K + s, l)
                value = p.stat * static_scale[s, l] * gather(out, tile, strided(j, R))
                if l == level:
                    part[own] = part[own] + value
                else:
                    rest[l, s] = value
    if first:
        for v in range(p.V):
            ship[v] = part[v].astype(bf16)
        if last:
            for l in range(p.L - 1):
                for s in range(p.S):
                    ship[p.V + l * p.S + s] = rest[l, s].astype(bf16)
        return
    for shift in range(1, p.mem):
        base = lax.rem(me + shift, p.mem) * p.S
        for s in range(p.S):
            ship[shift - 1, s] = part[base + s].astype(bf16)


def curvature_kernel(p, first, *refs):
    parts, gots, norms, refs = refs[: p.L], refs[p.L : 2 * p.L], refs[2 * p.L : 3 * p.L], refs[3 * p.L :]
    if p.L > 1:
        rest, *refs = refs
    if first:
        pack, _, image, send = refs
    else:
        pack, image_before, step, image, send = refs
    me = lax.axis_index("mem")
    total = jnp.zeros((p.R, p.X), f32)
    for l in range(p.L):
        if first:
            for v in range(p.V):
                value = parts[l][v]
                for other in range(p.mem - 1):
                    value = value + gots[l][other, v].astype(f32)
                image[v, l] = value
            if l < p.L - 1:
                for s in range(p.S):
                    own = me * p.S + s
                    image[own, l] = image[own, l] + rest[l, s]
                    for other in range(p.mem - 1):
                        theirs = lax.rem(me + (p.mem - 1 - other), p.mem) * p.S + s
                        value = gots[p.L - 1][other, p.V + l * p.S + s].astype(f32)
                        image[theirs, l] = image[theirs, l] + value
        for s in range(p.S):
            own = me * p.S + s
            if first:
                value = image[own, l]
                misfit = -pack[0, s, l]
            else:
                value = parts[l][own]
                if l < p.L - 1:
                    value = value + rest[l, s]
                for other in range(p.mem - 1):
                    value = value + gots[l][other, s].astype(f32)
                image[s, l] = value
                misfit = -(step[0:1, 0:1] * image_before[own, l]) - pack[0, s, l]
            index = pack[1, s, l]
            threshold = table(index, huber_levels)
            weight = jnp.where(index > 0, threshold / jnp.maximum(jnp.abs(misfit), threshold), 0.0)
            total = total + weight * value * value
    total = jnp.sum(total, axis=0, keepdims=True)
    total = sum(total[:, i * LANES : (i + 1) * LANES] for i in range(p.X // LANES))
    norm = sum(one[...] for one in norms)
    send[...] = jnp.broadcast_to(jnp.concatenate([norm, total], axis=1)[None], send.shape)


def final_kernel(p, got, step, image0, image1, matrix_ref, *refs):
    before, after, outs = refs[: p.L], refs[p.L : 2 * p.L], refs[2 * p.L :]
    control, static_control, increment = outs
    me = lax.axis_index("mem")
    total = jnp.sum(got[...], axis=0)
    norm = jnp.sum(total[:, :LANES], axis=1, keepdims=True)
    curvature = jnp.sum(total[:, LANES:], axis=1, keepdims=True)
    second = norm / (norm + curvature)
    first = step[0:1, 0:1]
    matrix = matrix_ref[...]

    targets, blocks = [], []
    for level in range(p.L):
        for field, l in p.fields(level):
            tile, lane = p.inner(field, l)
            where = strided(SWEEPS * SUB + lane, p.R)
            blocks.append(-(first * gather(before[level], tile, where)) - second * gather(after[level], tile, where))
            targets.append((control, field, l) if field < p.K else (static_control, field - p.K, l))
    for s in range(p.S):
        for l in range(p.L):
            blocks.append(-(first * image0[me * p.S + s, l]) - second * image1[s, l])
            targets.append((increment, s, l))
    (whole,) = products([jnp.concatenate(blocks, axis=0)], matrix, True)
    for i, (ref, index, l) in enumerate(targets):
        ref[index, l] = whole[i * p.R : (i + 1) * p.R]


def call(kernel, outs, scratch, far=0, cost=0, grant=8):
    vmem = pl.BlockSpec(memory_space=pltpu.VMEM)
    anywhere = pl.BlockSpec(memory_space=pltpu.MemorySpace.HBM)

    def run(*args):
        return pl.pallas_call(
            kernel,
            out_shape=tuple(jax.ShapeDtypeStruct(shape, dtype) for shape, dtype in outs),
            in_specs=[anywhere] * far + [vmem] * (len(args) - far),
            out_specs=tuple(vmem for _ in outs),
            scratch_shapes=scratch,
            compiler_params=pltpu.CompilerParams(vmem_limit_bytes=grant << 20),
            cost_estimate=pl.CostEstimate(flops=cost, bytes_accessed=cost, transcendentals=0),
        )(*[pltpu.with_memory_space_constraint(x, pltpu.MemorySpace.HBM) for x in args[:far]], *args[far:])

    return run


def local(members, static_scale, observed, huber_class, scale_index):
    p = Plan(members, static_scale, lax.axis_size("mem"), lax.axis_size("row"))
    K, V, L, R, X, S, C = p.K, p.V, p.L, p.R, p.X, p.S, p.C
    assert R >= 2 * SWEEPS and p.row % 2 == 0

    def round_mem(block, shift):
        return lax.ppermute(block, "mem", [(i, (i + shift) % p.mem) for i in range(p.mem)])

    def inside(block):
        return lax.ppermute(block, "row", [(i, i ^ 1) for i in range(p.row)])

    def across(block):
        n, pairs = p.row, []
        for m in range(p.mem):
            pairs += [(m * n + i, m * n + (i + 1 if i % 2 else i - 1)) for i in range(1, n - 1)]
            other = m ^ 1 if p.mem % 2 == 0 else m
            pairs += [(m * n + i, other * n + i) for i in (0, n - 1)]
        return lax.ppermute(block, ("mem", "row"), pairs)

    vmem = lambda shape: pltpu.VMEM(shape, f32)
    part = functools.partial
    shifts = range(1, p.mem)
    own_shape = (S, L, R, X)
    full_shape = (V, L, R, X)
    back_shape = (p.PN, C, R * SUB, LANES)
    send_shape = ((p.devices, 1, 2 * LANES), f32)
    line = ((1, LANES), f32)

    obs, cls, own = call(
        part(load_kernel, p), [(own_shape, f32), (own_shape, jnp.int32), (own_shape, bf16)],
        [pltpu.SemaphoreType.DMA((2,))], far=2,
    )(observed, huber_class)
    others = jnp.stack([round_mem(own, shift) for shift in shifts])
    scratch = [pltpu.VMEM(x.shape, x.dtype) for x in (members, static_scale, scale_index)]
    members, static_scale, scale_index, pack, own, matrix = call(
        part(fetch_kernel, p),
        [(members.shape, bf16), (own_shape, f32), ((L, R, X), f32), ((2,) + own_shape, f32), (own_shape, bf16), ((X, X), bf16)],
        scratch + [pltpu.SemaphoreType.DMA((K + 2,))], far=3, cost=4 << 20, grant=20,
    )(members, static_scale, scale_index, obs, cls, own)
    pack_in = jnp.stack([round_mem(pack, shift) for shift in shifts])

    grads, image, step, kap, sums = [], None, None, None, None
    for turn in range(ITERS):
        first = turn == 0
        sizes = [len(p.fields(level)) for level in range(L)]
        if first:
            sizes[0] += L
        msg_shapes = [((size, R, X), bf16) for size in sizes]
        if first:
            back, *msgs = call(
                part(back_kernel, p, True), [(back_shape, f32)] + msg_shapes, [vmem(full_shape)],
            )(members, static_scale, scale_index, own, others, matrix)
        else:
            back, step, *msgs = call(
                part(back_kernel, p, False), [(back_shape, f32), line] + msg_shapes, [vmem(full_shape)],
            )(members, static_scale, pack, pack_in, image, sums)
        halos = []
        for msg in msgs:
            near = inside(msg)
            far = across(msg)
            halos.append((near, far))
        grad, norms, partial_images, gots, rest = [], [], [], [], None
        for level in range(L):
            count = p.tiles(level)
            args = [members, static_scale, back, *halos[level]]
            args += [scale_index] if first and level == 0 else [kap]
            args += [] if first else [grads[0][level], step]
            last = level == L - 1
            ship_shape = (V + (L - 1) * S if last else V, R, X) if first else (p.mem - 1, S, R, X)
            outs = [((count, C, p.RG * SUB, LANES), f32), line, ((V, R, X), f32), (ship_shape, bf16)]
            if last and L > 1:
                outs.append(((L - 1, S, R, X), f32))
            if first and level == 0:
                outs.append(((L + p.ST, C, p.RE * SUB, LANES), f32))
            halo = vmem((2, count, C, 2 * SWEEPS * SUB, LANES))
            work = [halo, vmem((C, p.RE * SUB, LANES)), vmem((C, p.RE * SUB, LANES))]
            g, norm, partial_image, ship, *more = call(
                part(sweep_kernel, p, first, level), outs, work + [vmem((count, C, R * SUB, LANES))],
                cost=8 << 20,
            )(*args)
            if last and L > 1:
                rest, *more = more
            if first and level == 0:
                kap = more[0]
            grad.append(g)
            norms.append(norm)
            partial_images.append(partial_image)
            gots.append(jnp.stack([round_mem(ship if first else ship[shift - 1], shift) for shift in shifts]))
        grads.append(grad)
        extra = [rest] if L > 1 else []
        if first:
            image, send = call(
                part(curvature_kernel, p, True), [(full_shape, f32), send_shape], [],
            )(*partial_images, *gots, *norms, *extra, pack, pack_in)
        else:
            final_image, send = call(
                part(curvature_kernel, p, False), [(own_shape, f32), send_shape], [],
            )(*partial_images, *gots, *norms, *extra, pack, image, step)
        sums = lax.all_to_all(send, ("mem", "row"), 0, 0)
    return call(
        part(final_kernel, p),
        [((K, L, R, X), f32), (own_shape, f32), (own_shape, f32)], [],
    )(sums, step, image, final_image, matrix, *grads[0], *grads[1])


def solution(mesh):
    placed = (
        P("mem", None, None, "row", None),
        P("mem", None, "row", None),
        P("mem", None, "row", None),
        P("mem", None, "row", None),
        P(None, "row", None),
    )
    return jax.shard_map(
        local,
        mesh=mesh,
        in_specs=placed,
        out_specs=(
            P("mem", None, "row", None),
            P("mem", None, "row", None),
            P("mem", None, "row", None),
        ),
        check_vma=False,
    )
```

```python
import functools
import math

import jax
import jax.numpy as jnp
from jax import lax
from jax.experimental import pallas as pl
from jax.experimental.pallas import tpu as pltpu
from jax.sharding import PartitionSpec as P


SWEEPS = 4
ITERS = 2
SUB = 8
LANES = 128
kappa_table = (0.06, 0.11, 0.17, 0.23)
huber_levels = (1.0, 0.5, 1.0, 2.0)
f32 = jnp.float32
bf16 = jnp.bfloat16


def table(index, values):
    result = jnp.full(index.shape, values[3], f32)
    for entry in range(3):
        result = jnp.where(index == entry, f32(values[entry]), result)
    return result


class Plan:
    def __init__(self, members, static_scale, mem, row):
        self.K, self.V, self.L, self.R, self.X = members.shape
        self.S = static_scale.shape[0]
        self.mem, self.row = mem, row
        self.devices = mem * row
        self.KT = -(-self.K // SUB)
        self.ST = -(-(self.S * self.L) // SUB)
        self.PM = self.L * self.KT
        self.PN = self.PM + self.ST
        self.C = self.X // LANES
        self.RE = self.R + 4 * SWEEPS
        self.RG = self.R + 2 * SWEEPS
        self.pads = self.K % SUB != 0 or (self.S * self.L) % SUB != 0
        self.ens = math.sqrt(0.7 / (self.K * mem - 1))
        self.stat = math.sqrt(0.3)

    def fields(self, level):
        own = [(k, level) for k in range(self.K)]
        return own + [(self.K + s, l) for s in range(self.S) for l in range(self.L)] if level == self.L - 1 else own

    def tiles(self, level):
        return self.KT + self.ST if level == self.L - 1 else self.KT

    def inner(self, field, level):
        if field < self.K:
            return field // SUB, field % SUB
        at = (field - self.K) * self.L + level
        return self.KT + at // SUB, at % SUB

    def slot(self, field, level):
        if field < self.K:
            return level * self.KT + field // SUB, field % SUB
        at = (field - self.K) * self.L + level
        return self.PM + at // SUB, at % SUB


def strided(start, count):
    return pl.ds(start, count, stride=SUB)


def scatter(ref, tile, where, value):
    for c in range(value.shape[1] // LANES):
        ref[tile, c, where, :] = value[:, c * LANES : (c + 1) * LANES]


def gather(ref, tile, where):
    return jnp.concatenate([ref[tile, c, where, :] for c in range(ref.shape[1])], axis=1)


def onehot(p):
    source = lax.broadcasted_iota(jnp.int32, (p.X, p.X), 0)
    target = lax.broadcasted_iota(jnp.int32, (p.X, p.X), 1)
    return jnp.where(source == (target % LANES) * p.C + target // LANES, 1.0, 0.0).astype(bf16)


def product(block, matrix, back=False):
    dims = (((1,), (1 if back else 0,)), ((), ()))
    return lax.dot_general(block, matrix, dims, preferred_element_type=f32)


def pieces(block):
    first = block.astype(bf16)
    left = block - first.astype(f32)
    second = left.astype(bf16)
    return [first, second, (left - second.astype(f32)).astype(bf16)]


def products(blocks, matrix, back=False):
    parts = [pieces(block) if block.dtype == f32 else [block] for block in blocks]
    flat = [one for part in parts for one in part]
    whole = product(jnp.concatenate(flat, axis=0), matrix, back)
    out, at = [], 0
    for part in parts:
        rows = part[0].shape[0]
        cut = [whole[at + i * rows : at + (i + 1) * rows] for i in range(len(part))]
        out.append(cut[0] if len(cut) == 1 else cut[0] + (cut[1] + cut[2]))
        at += rows * len(part)
    return out


def load_kernel(p, obs, cls, obs_out, cls_out, sent, sems):
    pairs = ((obs, obs_out), (cls, cls_out))
    copies = [pltpu.make_async_copy(src, dst, sems.at[i]) for i, (src, dst) in enumerate(pairs)]
    for copy in copies:
        copy.start()
    for copy in copies:
        copy.wait()
    for s in range(p.S):
        for l in range(p.L):
            index = cls_out[s, l]
            threshold = table(index, huber_levels)
            clipped = jnp.where(index > 0, jnp.clip(-obs_out[s, l], -threshold, threshold), 0.0)
            sent[s, l] = clipped.astype(bf16)


def fetch_kernel(p, members, static_scale, scale_index, obs, cls, own, members_out, static_out, scale_out, pack,
                 own_out, matrix_out, raw, static_raw, scale_raw, sems):
    copies = [pltpu.make_async_copy(members.at[k], raw.at[k], sems.at[k]) for k in range(p.K)]
    rest = [
        pltpu.make_async_copy(static_scale, static_raw, sems.at[p.K]),
        pltpu.make_async_copy(scale_index, scale_raw, sems.at[p.K + 1]),
    ]
    for copy in copies + rest:
        copy.start()
    matrix_out[...] = onehot(p)
    matrix = matrix_out[...]
    rows = p.S * p.L * p.R
    shape = (p.S, p.L, p.R, p.X)
    flat = lambda x: x.reshape(rows, p.X)
    for copy in rest:
        copy.wait()
    scale = scale_raw[...].astype(f32).astype(bf16).reshape(p.L * p.R, p.X)
    blocks = [flat(own[...]), flat(obs[...]), flat(cls[...].astype(f32).astype(bf16)), flat(static_raw[...]), scale]
    blocks = products(blocks, matrix)
    own_out[...] = blocks[0].astype(bf16).reshape(shape)
    pack[0] = blocks[1].reshape(shape)
    pack[1] = blocks[2].reshape(shape)
    static_out[...] = blocks[3].reshape(shape)
    scale_out[...] = blocks[4].reshape(scale_out.shape)
    step = -(-p.K // 1)
    for k in range(0, p.K, step):
        some = min(step, p.K - k)
        for copy in copies[k : k + some]:
            copy.wait()
        block = raw[k : k + some].reshape(some * p.V * p.L * p.R, p.X)
        block = product(block, matrix)
        members_out[k : k + some] = block.reshape(some, p.V, p.L, p.R, p.X)


def back_kernel(p, first, *refs):
    if first:
        members, static_scale, scale_index, own, others, matrix, back, *msgs, sent = refs
    else:
        members, static_scale, pack, pack_in, image, got, back, step_out, *msgs, sent = refs
    me = lax.axis_index("mem")
    if p.pads:
        back[...] = jnp.zeros(back.shape, f32)
    if not first:
        total = jnp.sum(got[...], axis=0)
        norm = jnp.sum(total[:, :LANES], axis=1, keepdims=True)
        curvature = jnp.sum(total[:, LANES:], axis=1, keepdims=True)
        step = norm / (norm + curvature)
        step_out[...] = jnp.broadcast_to(step, step_out.shape)
    for shift in range(p.mem):
        base = lax.rem(me + (p.mem - shift), p.mem) * p.S
        if first and shift:
            block = product(others[shift - 1].reshape(p.S * p.L * p.R, p.X), matrix[...])
            block = block.reshape(p.S, p.L, p.R, p.X)
        for s in range(p.S):
            for l in range(p.L):
                if first:
                    rounded = block[s, l] if shift else own[s, l].astype(f32)
                else:
                    if shift == 0:
                        seen, index = pack[0, s, l], pack[1, s, l]
                    else:
                        seen, index = pack_in[shift - 1, 0, s, l], pack_in[shift - 1, 1, s, l]
                    threshold = table(index, huber_levels)
                    misfit = -(step * image[base + s, l]) - seen
                    clipped = jnp.where(index > 0, jnp.clip(misfit, -threshold, threshold), 0.0)
                    rounded = clipped.astype(bf16).astype(f32)
                sent[base + s, l] = rounded
                if shift == 0:
                    tile, lane = p.slot(p.K + s, l)
                    value = p.stat * static_scale[s, l] * rounded
                    scatter(back, tile, strided(lane, p.R), value)
                    msgs[p.L - 1][p.K + s * p.L + l] = value.astype(bf16)
    if first:
        for l in range(p.L):
            msgs[0][len(p.fields(0)) + l] = scale_index[l].astype(bf16)
    for l in range(p.L):
        for k in range(p.K):
            value = members[k, 0, l] * sent[0, l]
            for v in range(1, p.V):
                value = value + members[k, v, l] * sent[v, l]
            value = p.ens * value
            tile, lane = p.slot(k, l)
            scatter(back, tile, strided(lane, p.R), value)
            msgs[l][k] = value.astype(bf16)


def sideways(u, first_lane, last_lane):
    zero = jnp.zeros_like(u[0])
    before = jnp.where(first_lane, zero, pltpu.roll(u[-1], 1, 1))
    after = jnp.where(last_lane, zero, pltpu.roll(u[0], LANES - 1, 1))
    around = [before] + list(u) + [after]
    return [around[i] + around[i + 2] for i in range(len(u))]


def stencil(above, here, below, side):
    across = side(here)
    return [(above[c] + below[c]) + across[c] - 4.0 * here[c] for c in range(len(here))]


def sweep_kernel(p, first, level, *refs):
    refs = list(refs)
    members, static_scale, back, near, far = refs[:5]
    refs = refs[5:]
    if first and level == 0:
        scale_index, *refs = refs
    else:
        kap, *refs = refs
    if not first:
        before, step, *refs = refs
    grad, norm, part, ship, *refs = refs
    last = level == p.L - 1
    if last and p.L > 1:
        rest, *refs = refs
    if first and level == 0:
        kap, *refs = refs
    ends, a, b, out = refs
    me, at = lax.axis_index("mem"), lax.axis_index("row")
    low_ok = jnp.where(at > 0, 1.0, 0.0).astype(f32)
    high_ok = jnp.where(at < p.row - 1, 1.0, 0.0).astype(f32)
    R, RE, W = p.R, p.RE, SWEEPS
    H = 2 * W
    fields = p.fields(level)
    count = p.tiles(level)
    odd = lax.rem(at, 2)
    if p.pads:
        ends[...] = jnp.zeros(ends.shape, f32)

    def edge(value, side):
        if R == H:
            return value
        return jnp.where(side == 0, value[R - H :], value[:H])

    for ref, side in ((near, 1 - odd), (far, odd)):
        for i, (field, l) in enumerate(fields):
            tile, lane = p.inner(field, l)
            scatter(ends.at[side], tile, strided(lane, H), edge(ref[i].astype(f32), side))
    if first and level == 0:
        for l in range(p.L):
            pieces_of = [(table(scale_index[l], kappa_table), H)]
            for ref, side in ((near, 1 - odd), (far, odd)):
                value = table(edge(ref[len(fields) + l].astype(f32), side), kappa_table)
                pieces_of.append((value * jnp.where(side == 0, low_ok, high_ok), side * (H + R)))
            for value, offset in pieces_of:
                start = offset * SUB if isinstance(offset, int) else pl.multiple_of(offset * SUB, SUB)
                for r in range(value.shape[0]):
                    scatter(kap, l, pl.ds(start + r * SUB, SUB), jnp.broadcast_to(value[r : r + 1], (SUB, p.X)))
                for j in range(p.ST * SUB):
                    if (j % p.L) == l:
                        scatter(kap, p.L + j // SUB, strided(start + j % SUB, value.shape[0]), value)
    lane = lax.broadcasted_iota(jnp.int32, (SUB, LANES), 1)
    first_lane, last_lane = lane == 0, lane == LANES - 1
    side = functools.partial(sideways, first_lane=first_lane, last_lane=last_lane)
    cols = range(p.C)

    def tiles(ref, r, *lead):
        return [ref[(*lead, c, pl.ds(r * SUB, SUB), slice(None))] for c in cols]

    def keep(value, ref, r, *lead):
        for c in cols:
            ref[(*lead, c, pl.ds(r * SUB, SUB), slice(None))] = value[c]

    if not first:
        step_tile = jnp.broadcast_to(step[0:1, 0:1], (SUB, LANES))

    def problem(t, total):
        which, whole = level, t + level * p.KT
        if last:
            which = jnp.where(t < p.KT, level, t - p.KT + p.L)
            whole = jnp.where(t < p.KT, whole, t - p.KT + p.PM)
        source = None
        for sweep in range(W):
            target = (a, b)[sweep % 2]
            held = []
            for r in range(sweep, RE - sweep):
                if sweep:
                    u = tiles(source, r)
                elif r < H:
                    u = tiles(ends, r, 0, t)
                elif r < H + R:
                    u = tiles(back, r - H, whole)
                else:
                    u = tiles(ends, r - H - R, 1, t)
                factor = tiles(kap, r, which)
                w = [factor[c] * u[c] for c in cols]
                held = (held + [(u, w)])[-3:]
                if len(held) < 3:
                    continue
                (_, w0), (u1, w1), (_, w2) = held
                change = stencil(w0, w1, w2, side)
                value = [u1[c] + change[c] for c in cols]
                if sweep < W - 1:
                    keep(value, target, r - 1)
                    continue
                if not first:
                    earlier = tiles(before, r - 1 - W, t)
                    value = [value[c] - step_tile * earlier[c] for c in cols]
                if r - 1 < H:
                    value = [one * low_ok for one in value]
                elif r - 1 >= H + R:
                    value = [one * high_ok for one in value]
                else:
                    for one in value:
                        total = total + one * one
                keep(value, grad, r - 1 - W, t)
            source = target
        for sweep in range(W):
            target = (a, b)[sweep % 2]
            held = []
            for r in range(W + sweep, RE - W - sweep):
                u = tiles(source, r) if sweep else tiles(grad, r - W, t)
                held = (held + [u])[-3:]
                if len(held) < 3:
                    continue
                change = stencil(*held, side)
                factor = tiles(kap, r - 1, which)
                value = [held[1][c] + factor[c] * change[c] for c in cols]
                if sweep < W - 1:
                    keep(value, target, r - 1)
                else:
                    keep(value, out, r - 1 - H, t)
            source = target
        return total

    total = lax.fori_loop(0, count, problem, jnp.zeros((SUB, LANES), f32))
    norm[...] = jnp.sum(total, axis=0, keepdims=True)
    sums = [None] * p.V
    for k in range(p.K):
        tile, j = p.inner(k, level)
        spread = gather(out, tile, strided(j, R)).astype(bf16).astype(f32)
        for v in range(p.V):
            term = members[k, v, level] * spread
            sums[v] = term if k == 0 else sums[v] + term
    for v in range(p.V):
        part[v] = p.ens * sums[v]
    if last:
        for s in range(p.S):
            own = me * p.S + s
            for l in range(p.L):
                tile, j = p.inner(p.K + s, l)
                value = p.stat * static_scale[s, l] * gather(out, tile, strided(j, R))
                if l == level:
                    part[own] = part[own] + value
                else:
                    rest[l, s] = value
    if first:
        for v in range(p.V):
            ship[v] = part[v].astype(bf16)
        if last:
            for l in range(p.L - 1):
                for s in range(p.S):
                    ship[p.V + l * p.S + s] = rest[l, s].astype(bf16)
        return
    for shift in range(1, p.mem):
        base = lax.rem(me + shift, p.mem) * p.S
        for s in range(p.S):
            ship[shift - 1, s] = part[base + s].astype(bf16)


def curvature_kernel(p, first, *refs):
    parts, gots, norms, refs = refs[: p.L], refs[p.L : 2 * p.L], refs[2 * p.L : 3 * p.L], refs[3 * p.L :]
    if p.L > 1:
        rest, *refs = refs
    if first:
        pack, _, image, send = refs
    else:
        pack, image_before, step, image, send = refs
    me = lax.axis_index("mem")
    total = jnp.zeros((p.R, p.X), f32)
    for l in range(p.L):
        if first:
            for v in range(p.V):
                value = parts[l][v]
                for other in range(p.mem - 1):
                    value = value + gots[l][other, v].astype(f32)
                image[v, l] = value
            if l < p.L - 1:
                for s in range(p.S):
                    own = me * p.S + s
                    image[own, l] = image[own, l] + rest[l, s]
                    for other in range(p.mem - 1):
                        theirs = lax.rem(me + (p.mem - 1 - other), p.mem) * p.S + s
                        value = gots[p.L - 1][other, p.V + l * p.S + s].astype(f32)
                        image[theirs, l] = image[theirs, l] + value
        for s in range(p.S):
            own = me * p.S + s
            if first:
                value = image[own, l]
                misfit = -pack[0, s, l]
            else:
                value = parts[l][own]
                if l < p.L - 1:
                    value = value + rest[l, s]
                for other in range(p.mem - 1):
                    value = value + gots[l][other, s].astype(f32)
                image[s, l] = value
                misfit = -(step[0:1, 0:1] * image_before[own, l]) - pack[0, s, l]
            index = pack[1, s, l]
            threshold = table(index, huber_levels)
            weight = jnp.where(index > 0, threshold / jnp.maximum(jnp.abs(misfit), threshold), 0.0)
            total = total + weight * value * value
    total = jnp.sum(total, axis=0, keepdims=True)
    total = sum(total[:, i * LANES : (i + 1) * LANES] for i in range(p.X // LANES))
    norm = sum(one[...] for one in norms)
    send[...] = jnp.broadcast_to(jnp.concatenate([norm, total], axis=1)[None], send.shape)


def final_kernel(p, got, step, image0, image1, matrix_ref, *refs):
    before, after, outs = refs[: p.L], refs[p.L : 2 * p.L], refs[2 * p.L :]
    control, static_control, increment = outs
    me = lax.axis_index("mem")
    total = jnp.sum(got[...], axis=0)
    norm = jnp.sum(total[:, :LANES], axis=1, keepdims=True)
    curvature = jnp.sum(total[:, LANES:], axis=1, keepdims=True)
    second = norm / (norm + curvature)
    first = step[0:1, 0:1]
    matrix = matrix_ref[...]

    targets, blocks = [], []
    for level in range(p.L):
        for field, l in p.fields(level):
            tile, lane = p.inner(field, l)
            where = strided(SWEEPS * SUB + lane, p.R)
            blocks.append(-(first * gather(before[level], tile, where)) - second * gather(after[level], tile, where))
            targets.append((control, field, l) if field < p.K else (static_control, field - p.K, l))
    for s in range(p.S):
        for l in range(p.L):
            blocks.append(-(first * image0[me * p.S + s, l]) - second * image1[s, l])
            targets.append((increment, s, l))
    (whole,) = products([jnp.concatenate(blocks, axis=0)], matrix, True)
    for i, (ref, index, l) in enumerate(targets):
        ref[index, l] = whole[i * p.R : (i + 1) * p.R]


def call(kernel, outs, scratch, far=0, cost=0, grant=8):
    vmem = pl.BlockSpec(memory_space=pltpu.VMEM)
    anywhere = pl.BlockSpec(memory_space=pltpu.MemorySpace.HBM)

    def run(*args):
        return pl.pallas_call(
            kernel,
            out_shape=tuple(jax.ShapeDtypeStruct(shape, dtype) for shape, dtype in outs),
            in_specs=[anywhere] * far + [vmem] * (len(args) - far),
            out_specs=tuple(vmem for _ in outs),
            scratch_shapes=scratch,
            compiler_params=pltpu.CompilerParams(vmem_limit_bytes=grant << 20),
            cost_estimate=pl.CostEstimate(flops=cost, bytes_accessed=cost, transcendentals=0),
        )(*[pltpu.with_memory_space_constraint(x, pltpu.MemorySpace.HBM) for x in args[:far]], *args[far:])

    return run


def local(members, static_scale, observed, huber_class, scale_index):
    p = Plan(members, static_scale, lax.axis_size("mem"), lax.axis_size("row"))
    K, V, L, R, X, S, C = p.K, p.V, p.L, p.R, p.X, p.S, p.C
    assert R >= 2 * SWEEPS and p.row % 2 == 0

    def round_mem(block, shift):
        return lax.ppermute(block, "mem", [(i, (i + shift) % p.mem) for i in range(p.mem)])

    def inside(block):
        return lax.ppermute(block, "row", [(i, i ^ 1) for i in range(p.row)])

    def across(block):
        n, pairs = p.row, []
        for m in range(p.mem):
            pairs += [(m * n + i, m * n + (i + 1 if i % 2 else i - 1)) for i in range(1, n - 1)]
            other = m ^ 1 if p.mem % 2 == 0 else m
            pairs += [(m * n + i, other * n + i) for i in (0, n - 1)]
        return lax.ppermute(block, ("mem", "row"), pairs)

    vmem = lambda shape: pltpu.VMEM(shape, f32)
    part = functools.partial
    shifts = range(1, p.mem)
    own_shape = (S, L, R, X)
    full_shape = (V, L, R, X)
    back_shape = (p.PN, C, R * SUB, LANES)
    send_shape = ((p.devices, 1, 2 * LANES), f32)
    line = ((1, LANES), f32)

    obs, cls, own = call(
        part(load_kernel, p), [(own_shape, f32), (own_shape, jnp.int32), (own_shape, bf16)],
        [pltpu.SemaphoreType.DMA((2,))], far=2,
    )(observed, huber_class)
    others = jnp.stack([round_mem(own, shift) for shift in shifts])
    scratch = [pltpu.VMEM(x.shape, x.dtype) for x in (members, static_scale, scale_index)]
    members, static_scale, scale_index, pack, own, matrix = call(
        part(fetch_kernel, p),
        [(members.shape, f32), (own_shape, f32), ((L, R, X), f32), ((2,) + own_shape, f32), (own_shape, bf16), ((X, X), bf16)],
        scratch + [pltpu.SemaphoreType.DMA((K + 2,))], far=3, cost=4 << 20, grant=20,
    )(members, static_scale, scale_index, obs, cls, own)
    pack_in = jnp.stack([round_mem(pack, shift) for shift in shifts])

    grads, image, step, kap, sums = [], None, None, None, None
    for turn in range(ITERS):
        first = turn == 0
        sizes = [len(p.fields(level)) for level in range(L)]
        if first:
            sizes[0] += L
        msg_shapes = [((size, R, X), bf16) for size in sizes]
        if first:
            back, *msgs = call(
                part(back_kernel, p, True), [(back_shape, f32)] + msg_shapes, [vmem(full_shape)],
            )(members, static_scale, scale_index, own, others, matrix)
        else:
            back, step, *msgs = call(
                part(back_kernel, p, False), [(back_shape, f32), line] + msg_shapes, [vmem(full_shape)],
            )(members, static_scale, pack, pack_in, image, sums)
        halos = []
        for msg in msgs:
            near = inside(msg)
            far = across(msg)
            halos.append((near, far))
        grad, norms, partial_images, gots, rest = [], [], [], [], None
        for level in range(L):
            count = p.tiles(level)
            args = [members, static_scale, back, *halos[level]]
            args += [scale_index] if first and level == 0 else [kap]
            args += [] if first else [grads[0][level], step]
            last = level == L - 1
            ship_shape = (V + (L - 1) * S if last else V, R, X) if first else (p.mem - 1, S, R, X)
            outs = [((count, C, p.RG * SUB, LANES), f32), line, ((V, R, X), f32), (ship_shape, bf16)]
            if last and L > 1:
                outs.append(((L - 1, S, R, X), f32))
            if first and level == 0:
                outs.append(((L + p.ST, C, p.RE * SUB, LANES), f32))
            halo = vmem((2, count, C, 2 * SWEEPS * SUB, LANES))
            work = [halo, vmem((C, p.RE * SUB, LANES)), vmem((C, p.RE * SUB, LANES))]
            g, norm, partial_image, ship, *more = call(
                part(sweep_kernel, p, first, level), outs, work + [vmem((count, C, R * SUB, LANES))],
                cost=8 << 20,
            )(*args)
            if last and L > 1:
                rest, *more = more
            if first and level == 0:
                kap = more[0]
            grad.append(g)
            norms.append(norm)
            partial_images.append(partial_image)
            gots.append(jnp.stack([round_mem(ship if first else ship[shift - 1], shift) for shift in shifts]))
        grads.append(grad)
        extra = [rest] if L > 1 else []
        if first:
            image, send = call(
                part(curvature_kernel, p, True), [(full_shape, f32), send_shape], [],
            )(*partial_images, *gots, *norms, *extra, pack, pack_in)
        else:
            final_image, send = call(
                part(curvature_kernel, p, False), [(own_shape, f32), send_shape], [],
            )(*partial_images, *gots, *norms, *extra, pack, image, step)
        sums = lax.all_to_all(send, ("mem", "row"), 0, 0)
    return call(
        part(final_kernel, p),
        [((K, L, R, X), f32), (own_shape, f32), (own_shape, f32)], [],
    )(sums, step, image, final_image, matrix, *grads[0], *grads[1])


def solution(mesh):
    placed = (
        P("mem", None, None, "row", None),
        P("mem", None, "row", None),
        P("mem", None, "row", None),
        P("mem", None, "row", None),
        P(None, "row", None),
    )
    return jax.shard_map(
        local,
        mesh=mesh,
        in_specs=placed,
        out_specs=(
            P("mem", None, "row", None),
            P("mem", None, "row", None),
            P("mem", None, "row", None),
        ),
        check_vma=False,
    )
```

```python
import functools
import math

import jax
import jax.numpy as jnp
from jax import lax
from jax.experimental import pallas as pl
from jax.experimental.pallas import tpu as pltpu
from jax.sharding import PartitionSpec as P


SWEEPS = 4
ITERS = 2
SUB = 8
LANES = 128
kappa_table = (0.06, 0.11, 0.17, 0.23)
huber_levels = (1.0, 0.5, 1.0, 2.0)
f32 = jnp.float32
bf16 = jnp.bfloat16


def table(index, values):
    result = jnp.full(index.shape, values[3], f32)
    for entry in range(3):
        result = jnp.where(index == entry, f32(values[entry]), result)
    return result


class Plan:
    def __init__(self, members, static_scale, mem, row):
        self.K, self.V, self.L, self.R, self.X = members.shape
        self.S = static_scale.shape[0]
        self.mem, self.row = mem, row
        self.devices = mem * row
        self.KT = -(-self.K // SUB)
        self.ST = -(-(self.S * self.L) // SUB)
        self.PM = self.L * self.KT
        self.PN = self.PM + self.ST
        self.chunks = self.L + 1
        self.C = self.X // LANES
        self.RE = self.R + 4 * SWEEPS
        self.RG = self.R + 2 * SWEEPS
        self.pads = self.K % SUB != 0 or (self.S * self.L) % SUB != 0
        self.ens = math.sqrt(0.7 / (self.K * mem - 1))
        self.stat = math.sqrt(0.3)

    def fields(self, chunk):
        if chunk == 0:
            return [(self.K + s, l) for s in range(self.S) for l in range(self.L)]
        return [(k, chunk - 1) for k in range(self.K)]

    def tiles(self, chunk):
        return self.KT if chunk else self.ST

    def inner(self, field, level):
        at = field if field < self.K else (field - self.K) * self.L + level
        return at // SUB, at % SUB

    def slot(self, field, level):
        if field < self.K:
            return level * self.KT + field // SUB, field % SUB
        at = (field - self.K) * self.L + level
        return self.PM + at // SUB, at % SUB


def strided(start, count):
    return pl.ds(start, count, stride=SUB)


def scatter(ref, tile, where, value):
    for c in range(value.shape[1] // LANES):
        ref[tile, c, where, :] = value[:, c * LANES : (c + 1) * LANES]


def gather(ref, tile, where):
    return jnp.concatenate([ref[tile, c, where, :] for c in range(ref.shape[1])], axis=1)


def onehot(p):
    source = lax.broadcasted_iota(jnp.int32, (p.X, p.X), 0)
    target = lax.broadcasted_iota(jnp.int32, (p.X, p.X), 1)
    return jnp.where(source == (target % LANES) * p.C + target // LANES, 1.0, 0.0).astype(bf16)


def product(block, matrix, back=False):
    dims = (((1,), (1 if back else 0,)), ((), ()))
    return lax.dot_general(block, matrix, dims, preferred_element_type=f32)


def pieces(block):
    first = block.astype(bf16)
    left = block - first.astype(f32)
    second = left.astype(bf16)
    return [first, second, (left - second.astype(f32)).astype(bf16)]


def products(blocks, matrix, back=False):
    parts = [pieces(block) if block.dtype == f32 else [block] for block in blocks]
    flat = [one for part in parts for one in part]
    whole = product(jnp.concatenate(flat, axis=0), matrix, back)
    out, at = [], 0
    for part in parts:
        rows = part[0].shape[0]
        cut = [whole[at + i * rows : at + (i + 1) * rows] for i in range(len(part))]
        out.append(cut[0] if len(cut) == 1 else cut[0] + (cut[1] + cut[2]))
        at += rows * len(part)
    return out


def load_kernel(p, obs, cls, obs_out, cls_out, sent, sems):
    pairs = ((obs, obs_out), (cls, cls_out))
    copies = [pltpu.make_async_copy(src, dst, sems.at[i]) for i, (src, dst) in enumerate(pairs)]
    for copy in copies:
        copy.start()
    for copy in copies:
        copy.wait()
    for s in range(p.S):
        for l in range(p.L):
            index = cls_out[s, l]
            threshold = table(index, huber_levels)
            clipped = jnp.where(index > 0, jnp.clip(-obs_out[s, l], -threshold, threshold), 0.0)
            sent[s, l] = clipped.astype(bf16)


def fetch_kernel(p, members, static_scale, scale_index, obs, cls, own, members_out, static_out, scale_out, pack,
                 own_out, matrix_out, raw, static_raw, scale_raw, sems):
    copies = [pltpu.make_async_copy(members.at[k], raw.at[k], sems.at[k]) for k in range(p.K)]
    rest = [
        pltpu.make_async_copy(static_scale, static_raw, sems.at[p.K]),
        pltpu.make_async_copy(scale_index, scale_raw, sems.at[p.K + 1]),
    ]
    for copy in copies + rest:
        copy.start()
    matrix_out[...] = onehot(p)
    matrix = matrix_out[...]
    rows = p.S * p.L * p.R
    shape = (p.S, p.L, p.R, p.X)
    flat = lambda x: x.reshape(rows, p.X)
    for copy in rest:
        copy.wait()
    scale = scale_raw[...].astype(f32).astype(bf16).reshape(p.L * p.R, p.X)
    blocks = [flat(own[...]), flat(obs[...]), flat(cls[...].astype(f32).astype(bf16)), flat(static_raw[...]), scale]
    blocks = products(blocks, matrix)
    own_out[...] = blocks[0].astype(bf16).reshape(shape)
    pack[0] = blocks[1].reshape(shape)
    pack[1] = blocks[2].reshape(shape)
    static_out[...] = blocks[3].reshape(shape)
    scale_out[...] = blocks[4].reshape(scale_out.shape)
    step = -(-p.K // 1)
    for k in range(0, p.K, step):
        some = min(step, p.K - k)
        for copy in copies[k : k + some]:
            copy.wait()
        block = raw[k : k + some].reshape(some * p.V * p.L * p.R, p.X)
        block = product(block, matrix)
        members_out[k : k + some] = block.reshape(some, p.V, p.L, p.R, p.X)


def back_kernel(p, first, *refs):
    if first:
        members, static_scale, scale_index, own, others, matrix, back, *msgs, sent = refs
    else:
        members, static_scale, pack, pack_in, image, got, back, step_out, *msgs, sent = refs
    me = lax.axis_index("mem")
    if p.pads:
        back[...] = jnp.zeros(back.shape, f32)
    if not first:
        total = jnp.sum(got[...], axis=0)
        norm = jnp.sum(total[:, :LANES], axis=1, keepdims=True)
        curvature = jnp.sum(total[:, LANES:], axis=1, keepdims=True)
        step = norm / (norm + curvature)
        step_out[...] = jnp.broadcast_to(step, step_out.shape)
    for shift in range(p.mem):
        base = lax.rem(me + (p.mem - shift), p.mem) * p.S
        if first and shift:
            block = product(others[shift - 1].reshape(p.S * p.L * p.R, p.X), matrix[...])
            block = block.reshape(p.S, p.L, p.R, p.X)
        for s in range(p.S):
            for l in range(p.L):
                if first:
                    rounded = block[s, l] if shift else own[s, l].astype(f32)
                else:
                    if shift == 0:
                        seen, index = pack[0, s, l], pack[1, s, l]
                    else:
                        seen, index = pack_in[shift - 1, 0, s, l], pack_in[shift - 1, 1, s, l]
                    threshold = table(index, huber_levels)
                    misfit = -(step * image[base + s, l]) - seen
                    clipped = jnp.where(index > 0, jnp.clip(misfit, -threshold, threshold), 0.0)
                    rounded = clipped.astype(bf16).astype(f32)
                sent[base + s, l] = rounded
                if shift == 0:
                    tile, lane = p.slot(p.K + s, l)
                    value = p.stat * static_scale[s, l] * rounded
                    scatter(back, tile, strided(lane, p.R), value)
                    msgs[0][s * p.L + l] = value.astype(bf16)
    if first:
        for l in range(p.L):
            msgs[0][len(p.fields(0)) + l] = scale_index[l].astype(bf16)
    for l in range(p.L):
        for k in range(p.K):
            value = members[k, 0, l] * sent[0, l]
            for v in range(1, p.V):
                value = value + members[k, v, l] * sent[v, l]
            value = p.ens * value
            tile, lane = p.slot(k, l)
            scatter(back, tile, strided(lane, p.R), value)
            msgs[l + 1][k] = value.astype(bf16)


def sideways(u, first_lane, last_lane):
    zero = jnp.zeros_like(u[0])
    before = jnp.where(first_lane, zero, pltpu.roll(u[-1], 1, 1))
    after = jnp.where(last_lane, zero, pltpu.roll(u[0], LANES - 1, 1))
    around = [before] + list(u) + [after]
    return [around[i] + around[i + 2] for i in range(len(u))]


def stencil(above, here, below, side):
    across = side(here)
    return [(above[c] + below[c]) + across[c] - 4.0 * here[c] for c in range(len(here))]


def sweep_kernel(p, first, chunk, *refs):
    refs = list(refs)
    source_of, back, near, far = refs[:4]
    refs = refs[4:]
    builds = first and chunk == 0
    if builds:
        scale_index, *refs = refs
    else:
        kap, *refs = refs
    if chunk:
        members, level = source_of, chunk - 1
        rest, *refs = refs
    else:
        static_scale = source_of
    if not first:
        before, step, *refs = refs
    grad, norm, *refs = refs
    if chunk:
        part, ship, *refs = refs
    else:
        rest, *refs = refs
    if builds:
        kap, *refs = refs
    ends, a, b, out = refs
    me, at = lax.axis_index("mem"), lax.axis_index("row")
    low_ok = jnp.where(at > 0, 1.0, 0.0).astype(f32)
    high_ok = jnp.where(at < p.row - 1, 1.0, 0.0).astype(f32)
    R, RE, W = p.R, p.RE, SWEEPS
    H = 2 * W
    fields = p.fields(chunk)
    count = p.tiles(chunk)
    odd = lax.rem(at, 2)
    if p.pads:
        ends[...] = jnp.zeros(ends.shape, f32)

    def edge(value, side):
        if R == H:
            return value
        return jnp.where(side == 0, value[R - H :], value[:H])

    for ref, side in ((near, 1 - odd), (far, odd)):
        for i, (field, l) in enumerate(fields):
            tile, lane = p.inner(field, l)
            scatter(ends.at[side], tile, strided(lane, H), edge(ref[i].astype(f32), side))
    if builds:
        for l in range(p.L):
            pieces_of = [(table(scale_index[l], kappa_table), H)]
            for ref, side in ((near, 1 - odd), (far, odd)):
                value = table(edge(ref[len(fields) + l].astype(f32), side), kappa_table)
                pieces_of.append((value * jnp.where(side == 0, low_ok, high_ok), side * (H + R)))
            for value, offset in pieces_of:
                start = offset * SUB if isinstance(offset, int) else pl.multiple_of(offset * SUB, SUB)
                for r in range(value.shape[0]):
                    scatter(kap, l, pl.ds(start + r * SUB, SUB), jnp.broadcast_to(value[r : r + 1], (SUB, p.X)))
                for j in range(p.ST * SUB):
                    if (j % p.L) == l:
                        scatter(kap, p.L + j // SUB, strided(start + j % SUB, value.shape[0]), value)
    lane = lax.broadcasted_iota(jnp.int32, (SUB, LANES), 1)
    first_lane, last_lane = lane == 0, lane == LANES - 1
    side = functools.partial(sideways, first_lane=first_lane, last_lane=last_lane)
    cols = range(p.C)

    def tiles(ref, r, *lead):
        return [ref[(*lead, c, pl.ds(r * SUB, SUB), slice(None))] for c in cols]

    def keep(value, ref, r, *lead):
        for c in cols:
            ref[(*lead, c, pl.ds(r * SUB, SUB), slice(None))] = value[c]

    if not first:
        step_tile = jnp.broadcast_to(step[0:1, 0:1], (SUB, LANES))

    def problem(t, total):
        which, whole = (level, t + level * p.KT) if chunk else (t + p.L, t + p.PM)
        source = None
        for sweep in range(W):
            target = (a, b)[sweep % 2]
            held = []
            for r in range(sweep, RE - sweep):
                if sweep:
                    u = tiles(source, r)
                elif r < H:
                    u = tiles(ends, r, 0, t)
                elif r < H + R:
                    u = tiles(back, r - H, whole)
                else:
                    u = tiles(ends, r - H - R, 1, t)
                factor = tiles(kap, r, which)
                w = [factor[c] * u[c] for c in cols]
                held = (held + [(u, w)])[-3:]
                if len(held) < 3:
                    continue
                (_, w0), (u1, w1), (_, w2) = held
                change = stencil(w0, w1, w2, side)
                value = [u1[c] + change[c] for c in cols]
                if sweep < W - 1:
                    keep(value, target, r - 1)
                    continue
                if not first:
                    earlier = tiles(before, r - 1 - W, t)
                    value = [value[c] - step_tile * earlier[c] for c in cols]
                if r - 1 < H:
                    value = [one * low_ok for one in value]
                elif r - 1 >= H + R:
                    value = [one * high_ok for one in value]
                else:
                    for one in value:
                        total = total + one * one
                keep(value, grad, r - 1 - W, t)
            source = target
        for sweep in range(W):
            target = (a, b)[sweep % 2]
            held = []
            for r in range(W + sweep, RE - W - sweep):
                u = tiles(source, r) if sweep else tiles(grad, r - W, t)
                held = (held + [u])[-3:]
                if len(held) < 3:
                    continue
                change = stencil(*held, side)
                factor = tiles(kap, r - 1, which)
                value = [held[1][c] + factor[c] * change[c] for c in cols]
                if sweep < W - 1:
                    keep(value, target, r - 1)
                else:
                    keep(value, out, r - 1 - H, t)
            source = target
        return total

    total = lax.fori_loop(0, count, problem, jnp.zeros((SUB, LANES), f32))
    norm[...] = jnp.sum(total, axis=0, keepdims=True)
    if chunk == 0:
        for s in range(p.S):
            for l in range(p.L):
                tile, j = p.inner(p.K + s, l)
                rest[l, s] = p.stat * static_scale[s, l] * gather(out, tile, strided(j, R))
        return
    sums = [None] * p.V
    for k in range(p.K):
        tile, j = p.inner(k, level)
        spread = gather(out, tile, strided(j, R)).astype(bf16).astype(f32)
        for v in range(p.V):
            term = members[k, v, level] * spread
            sums[v] = term if k == 0 else sums[v] + term
    for v in range(p.V):
        part[v] = p.ens * sums[v]
    for s in range(p.S):
        own = me * p.S + s
        part[own] = part[own] + rest[level, s]
    if first:
        for v in range(p.V):
            ship[v] = part[v].astype(bf16)
        return
    for shift in range(1, p.mem):
        base = lax.rem(me + shift, p.mem) * p.S
        for s in range(p.S):
            ship[shift - 1, s] = part[base + s].astype(bf16)


def curvature_kernel(p, first, *refs):
    parts, gots, norms = refs[: p.L], refs[p.L : 2 * p.L], refs[2 * p.L : 3 * p.L + 1]
    refs = refs[3 * p.L + 1 :]
    if first:
        pack, _, image, send = refs
    else:
        pack, image_before, step, image, send = refs
    me = lax.axis_index("mem")
    total = jnp.zeros((p.R, p.X), f32)
    for l in range(p.L):
        if first:
            for v in range(p.V):
                value = parts[l][v]
                for other in range(p.mem - 1):
                    value = value + gots[l][other, v].astype(f32)
                image[v, l] = value
        for s in range(p.S):
            own = me * p.S + s
            if first:
                value = image[own, l]
                misfit = -pack[0, s, l]
            else:
                value = parts[l][own]
                for other in range(p.mem - 1):
                    value = value + gots[l][other, s].astype(f32)
                image[s, l] = value
                misfit = -(step[0:1, 0:1] * image_before[own, l]) - pack[0, s, l]
            index = pack[1, s, l]
            threshold = table(index, huber_levels)
            weight = jnp.where(index > 0, threshold / jnp.maximum(jnp.abs(misfit), threshold), 0.0)
            total = total + weight * value * value
    total = jnp.sum(total, axis=0, keepdims=True)
    total = sum(total[:, i * LANES : (i + 1) * LANES] for i in range(p.X // LANES))
    norm = sum(one[...] for one in norms)
    send[...] = jnp.broadcast_to(jnp.concatenate([norm, total], axis=1)[None], send.shape)


def final_kernel(p, got, step, image0, image1, matrix_ref, *refs):
    before, after, outs = refs[: p.chunks], refs[p.chunks : 2 * p.chunks], refs[2 * p.chunks :]
    control, static_control, increment = outs
    me = lax.axis_index("mem")
    total = jnp.sum(got[...], axis=0)
    norm = jnp.sum(total[:, :LANES], axis=1, keepdims=True)
    curvature = jnp.sum(total[:, LANES:], axis=1, keepdims=True)
    second = norm / (norm + curvature)
    first = step[0:1, 0:1]
    matrix = matrix_ref[...]

    targets, blocks = [], []
    for chunk in range(p.chunks):
        for field, l in p.fields(chunk):
            tile, lane = p.inner(field, l)
            where = strided(SWEEPS * SUB + lane, p.R)
            blocks.append(-(first * gather(before[chunk], tile, where)) - second * gather(after[chunk], tile, where))
            targets.append((control, field, l) if field < p.K else (static_control, field - p.K, l))
    for s in range(p.S):
        for l in range(p.L):
            blocks.append(-(first * image0[me * p.S + s, l]) - second * image1[s, l])
            targets.append((increment, s, l))
    (whole,) = products([jnp.concatenate(blocks, axis=0)], matrix, True)
    for i, (ref, index, l) in enumerate(targets):
        ref[index, l] = whole[i * p.R : (i + 1) * p.R]


def call(kernel, outs, scratch, far=0, cost=0, grant=8):
    vmem = pl.BlockSpec(memory_space=pltpu.VMEM)
    anywhere = pl.BlockSpec(memory_space=pltpu.MemorySpace.HBM)

    def run(*args):
        return pl.pallas_call(
            kernel,
            out_shape=tuple(jax.ShapeDtypeStruct(shape, dtype) for shape, dtype in outs),
            in_specs=[anywhere] * far + [vmem] * (len(args) - far),
            out_specs=tuple(vmem for _ in outs),
            scratch_shapes=scratch,
            compiler_params=pltpu.CompilerParams(vmem_limit_bytes=grant << 20),
            cost_estimate=pl.CostEstimate(flops=cost, bytes_accessed=cost, transcendentals=0),
        )(*[pltpu.with_memory_space_constraint(x, pltpu.MemorySpace.HBM) for x in args[:far]], *args[far:])

    return run


def local(members, static_scale, observed, huber_class, scale_index):
    p = Plan(members, static_scale, lax.axis_size("mem"), lax.axis_size("row"))
    K, V, L, R, X, S, C = p.K, p.V, p.L, p.R, p.X, p.S, p.C
    assert R >= 2 * SWEEPS and p.row % 2 == 0

    def round_mem(block, shift):
        return lax.ppermute(block, "mem", [(i, (i + shift) % p.mem) for i in range(p.mem)])

    def inside(block):
        return lax.ppermute(block, "row", [(i, i ^ 1) for i in range(p.row)])

    def across(block):
        n, pairs = p.row, []
        for m in range(p.mem):
            pairs += [(m * n + i, m * n + (i + 1 if i % 2 else i - 1)) for i in range(1, n - 1)]
            other = m ^ 1 if p.mem % 2 == 0 else m
            pairs += [(m * n + i, other * n + i) for i in (0, n - 1)]
        return lax.ppermute(block, ("mem", "row"), pairs)

    vmem = lambda shape: pltpu.VMEM(shape, f32)
    part = functools.partial
    shifts = range(1, p.mem)
    own_shape = (S, L, R, X)
    full_shape = (V, L, R, X)
    back_shape = (p.PN, C, R * SUB, LANES)
    send_shape = ((p.devices, 1, 2 * LANES), f32)
    line = ((1, LANES), f32)

    obs, cls, own = call(
        part(load_kernel, p), [(own_shape, f32), (own_shape, jnp.int32), (own_shape, bf16)],
        [pltpu.SemaphoreType.DMA((2,))], far=2,
    )(observed, huber_class)
    others = jnp.stack([round_mem(own, shift) for shift in shifts])
    scratch = [pltpu.VMEM(x.shape, x.dtype) for x in (members, static_scale, scale_index)]
    members, static_scale, scale_index, pack, own, matrix = call(
        part(fetch_kernel, p),
        [(members.shape, f32), (own_shape, f32), ((L, R, X), f32), ((2,) + own_shape, f32), (own_shape, bf16), ((X, X), bf16)],
        scratch + [pltpu.SemaphoreType.DMA((K + 2,))], far=3, cost=4 << 20, grant=20,
    )(members, static_scale, scale_index, obs, cls, own)
    pack_in = jnp.stack([round_mem(pack, shift) for shift in shifts])

    grads, image, step, kap, sums = [], None, None, None, None
    for turn in range(ITERS):
        first = turn == 0
        sizes = [len(p.fields(chunk)) for chunk in range(p.chunks)]
        if first:
            sizes[0] += L
        msg_shapes = [((size, R, X), bf16) for size in sizes]
        if first:
            back, *msgs = call(
                part(back_kernel, p, True), [(back_shape, f32)] + msg_shapes, [vmem(full_shape)],
            )(members, static_scale, scale_index, own, others, matrix)
        else:
            back, step, *msgs = call(
                part(back_kernel, p, False), [(back_shape, f32), line] + msg_shapes, [vmem(full_shape)],
            )(members, static_scale, pack, pack_in, image, sums)
        halos = []
        for msg in msgs:
            near = inside(msg)
            far = across(msg)
            halos.append((near, far))
        grad, norms, partial_images, gots, rest = [], [], [], [], None
        for chunk in range(p.chunks):
            count = p.tiles(chunk)
            builds = first and chunk == 0
            args = [members if chunk else static_scale, back, *halos[chunk], scale_index if builds else kap]
            args += [rest] if chunk else []
            args += [] if first else [grads[0][chunk], step]
            outs = [((count, C, p.RG * SUB, LANES), f32), line]
            if chunk:
                outs += [((V, R, X), f32), ((V, R, X) if first else (p.mem - 1, S, R, X), bf16)]
            else:
                outs.append(((L, S, R, X), f32))
            if builds:
                outs.append(((L + p.ST, C, p.RE * SUB, LANES), f32))
            halo = vmem((2, count, C, 2 * SWEEPS * SUB, LANES))
            work = [halo, vmem((C, p.RE * SUB, LANES)), vmem((C, p.RE * SUB, LANES))]
            g, norm, *more = call(
                part(sweep_kernel, p, first, chunk), outs, work + [vmem((count, C, R * SUB, LANES))],
                cost=8 << 20,
            )(*args)
            grad.append(g)
            norms.append(norm)
            if builds:
                rest, kap = more
            elif chunk == 0:
                (rest,) = more
            else:
                partial_image, ship = more
                partial_images.append(partial_image)
                gots.append(jnp.stack([round_mem(ship if first else ship[shift - 1], shift) for shift in shifts]))
        grads.append(grad)
        if first:
            image, send = call(
                part(curvature_kernel, p, True), [(full_shape, f32), send_shape], [],
            )(*partial_images, *gots, *norms, pack, pack_in)
        else:
            final_image, send = call(
                part(curvature_kernel, p, False), [(own_shape, f32), send_shape], [],
            )(*partial_images, *gots, *norms, pack, image, step)
        sums = lax.all_to_all(send, ("mem", "row"), 0, 0)
    return call(
        part(final_kernel, p),
        [((K, L, R, X), f32), (own_shape, f32), (own_shape, f32)], [],
    )(sums, step, image, final_image, matrix, *grads[0], *grads[1])


def solution(mesh):
    placed = (
        P("mem", None, None, "row", None),
        P("mem", None, "row", None),
        P("mem", None, "row", None),
        P("mem", None, "row", None),
        P(None, "row", None),
    )
    return jax.shard_map(
        local,
        mesh=mesh,
        in_specs=placed,
        out_specs=(
            P("mem", None, "row", None),
            P("mem", None, "row", None),
            P("mem", None, "row", None),
        ),
        check_vma=False,
    )
```

```python
import functools
import math

import jax
import jax.numpy as jnp
from jax import lax
from jax.experimental import pallas as pl
from jax.experimental.pallas import tpu as pltpu
from jax.sharding import PartitionSpec as P


SWEEPS = 4
ITERS = 2
SUB = 8
LANES = 128
kappa_table = (0.06, 0.11, 0.17, 0.23)
huber_levels = (1.0, 0.5, 1.0, 2.0)
f32 = jnp.float32
bf16 = jnp.bfloat16


def table(index, values):
    result = jnp.full(index.shape, values[3], f32)
    for entry in range(3):
        result = jnp.where(index == entry, f32(values[entry]), result)
    return result


class Plan:
    def __init__(self, members, static_scale, mem, row):
        self.K, self.V, self.L, self.R, self.X = members.shape
        self.S = static_scale.shape[0]
        self.mem, self.row = mem, row
        self.devices = mem * row
        self.KT = -(-self.K // SUB)
        self.ST = -(-(self.S * self.L) // SUB)
        self.PM = self.L * self.KT
        self.PN = self.PM + self.ST
        self.chunks = self.L + 1
        self.C = self.X // LANES
        self.RE = self.R + 4 * SWEEPS
        self.RG = self.R + 2 * SWEEPS
        self.pads = self.K % SUB != 0 or (self.S * self.L) % SUB != 0
        self.ens = math.sqrt(0.7 / (self.K * mem - 1))
        self.stat = math.sqrt(0.3)

    def fields(self, chunk):
        if chunk == 0:
            return [(self.K + s, l) for s in range(self.S) for l in range(self.L)]
        return [(k, chunk - 1) for k in range(self.K)]

    def tiles(self, chunk):
        return self.KT if chunk else self.ST

    def inner(self, field, level):
        at = field if field < self.K else (field - self.K) * self.L + level
        return at // SUB, at % SUB

    def slot(self, field, level):
        if field < self.K:
            return level * self.KT + field // SUB, field % SUB
        at = (field - self.K) * self.L + level
        return self.PM + at // SUB, at % SUB


def strided(start, count):
    return pl.ds(start, count, stride=SUB)


def scatter(ref, tile, where, value):
    for c in range(value.shape[1] // LANES):
        ref[tile, c, where, :] = value[:, c * LANES : (c + 1) * LANES]


def gather(ref, tile, where):
    return jnp.concatenate([ref[tile, c, where, :] for c in range(ref.shape[1])], axis=1)


def onehot(p):
    source = lax.broadcasted_iota(jnp.int32, (p.X, p.X), 0)
    target = lax.broadcasted_iota(jnp.int32, (p.X, p.X), 1)
    return jnp.where(source == (target % LANES) * p.C + target // LANES, 1.0, 0.0).astype(bf16)


def product(block, matrix, back=False):
    dims = (((1,), (1 if back else 0,)), ((), ()))
    return lax.dot_general(block, matrix, dims, preferred_element_type=f32)


def pieces(block):
    first = block.astype(bf16)
    left = block - first.astype(f32)
    second = left.astype(bf16)
    return [first, second, (left - second.astype(f32)).astype(bf16)]


def products(blocks, matrix, back=False):
    parts = [pieces(block) if block.dtype == f32 else [block] for block in blocks]
    flat = [one for part in parts for one in part]
    whole = product(jnp.concatenate(flat, axis=0), matrix, back)
    out, at = [], 0
    for part in parts:
        rows = part[0].shape[0]
        cut = [whole[at + i * rows : at + (i + 1) * rows] for i in range(len(part))]
        out.append(cut[0] if len(cut) == 1 else cut[0] + (cut[1] + cut[2]))
        at += rows * len(part)
    return out


def folded(norm, curvature):
    lane = lax.broadcasted_iota(jnp.int32, norm.shape, 1)
    half = LANES // 2
    return jnp.where(lane < half, norm + pltpu.roll(norm, half, 1), curvature + pltpu.roll(curvature, half, 1))


def step_of(got):
    total = jnp.sum(got[...], axis=0)
    lane = lax.broadcasted_iota(jnp.int32, total.shape, 1)
    norm = jnp.sum(jnp.where(lane < LANES // 2, total, 0.0), axis=1, keepdims=True)
    curvature = jnp.sum(jnp.where(lane < LANES // 2, 0.0, total), axis=1, keepdims=True)
    return norm / (norm + curvature)


def load_kernel(p, obs, cls, obs_out, cls_out, sent, sems):
    pairs = ((obs, obs_out), (cls, cls_out))
    copies = [pltpu.make_async_copy(src, dst, sems.at[i]) for i, (src, dst) in enumerate(pairs)]
    for copy in copies:
        copy.start()
    for copy in copies:
        copy.wait()
    for s in range(p.S):
        for l in range(p.L):
            index = cls_out[s, l]
            threshold = table(index, huber_levels)
            clipped = jnp.where(index > 0, jnp.clip(-obs_out[s, l], -threshold, threshold), 0.0)
            sent[s, l] = clipped.astype(bf16)


def fetch_kernel(p, members, static_scale, scale_index, obs, cls, own, members_out, static_out, scale_out, pack,
                 own_out, matrix_out, raw, static_raw, scale_raw, sems):
    copies = [pltpu.make_async_copy(members.at[k], raw.at[k], sems.at[k]) for k in range(p.K)]
    rest = [
        pltpu.make_async_copy(static_scale, static_raw, sems.at[p.K]),
        pltpu.make_async_copy(scale_index, scale_raw, sems.at[p.K + 1]),
    ]
    for copy in copies + rest:
        copy.start()
    matrix_out[...] = onehot(p)
    matrix = matrix_out[...]
    rows = p.S * p.L * p.R
    shape = (p.S, p.L, p.R, p.X)
    flat = lambda x: x.reshape(rows, p.X)
    for copy in rest:
        copy.wait()
    scale = scale_raw[...].astype(f32).astype(bf16).reshape(p.L * p.R, p.X)
    blocks = [flat(own[...]), flat(obs[...]), flat(cls[...].astype(f32).astype(bf16)), flat(static_raw[...]), scale]
    blocks = products(blocks, matrix)
    own_out[...] = blocks[0].astype(bf16).reshape(shape)
    pack[0] = blocks[1].reshape(shape)
    pack[1] = blocks[2].reshape(shape)
    static_out[...] = blocks[3].reshape(shape)
    scale_out[...] = blocks[4].reshape(scale_out.shape)
    step = -(-p.K // 1)
    for k in range(0, p.K, step):
        some = min(step, p.K - k)
        for copy in copies[k : k + some]:
            copy.wait()
        block = raw[k : k + some].reshape(some * p.V * p.L * p.R, p.X)
        block = product(block, matrix)
        members_out[k : k + some] = block.reshape(some, p.V, p.L, p.R, p.X)


def back_kernel(p, first, *refs):
    if first:
        members, static_scale, scale_index, own, others, matrix, back, *msgs, sent = refs
    else:
        members, static_scale, pack, pack_in, image, got, back, step_out, *msgs, sent = refs
    me = lax.axis_index("mem")
    if p.pads:
        back[...] = jnp.zeros(back.shape, f32)
    if not first:
        step = step_of(got)
        step_out[...] = jnp.broadcast_to(step, step_out.shape)
    for shift in range(p.mem):
        base = lax.rem(me + (p.mem - shift), p.mem) * p.S
        if first and shift:
            block = product(others[shift - 1].reshape(p.S * p.L * p.R, p.X), matrix[...])
            block = block.reshape(p.S, p.L, p.R, p.X)
        for s in range(p.S):
            for l in range(p.L):
                if first:
                    rounded = block[s, l] if shift else own[s, l].astype(f32)
                else:
                    if shift == 0:
                        seen, index = pack[0, s, l], pack[1, s, l]
                    else:
                        seen, index = pack_in[shift - 1, 0, s, l], pack_in[shift - 1, 1, s, l]
                    threshold = table(index, huber_levels)
                    misfit = -(step * image[base + s, l]) - seen
                    clipped = jnp.where(index > 0, jnp.clip(misfit, -threshold, threshold), 0.0)
                    rounded = clipped.astype(bf16).astype(f32)
                sent[base + s, l] = rounded
                if shift == 0:
                    tile, lane = p.slot(p.K + s, l)
                    value = p.stat * static_scale[s, l] * rounded
                    scatter(back, tile, strided(lane, p.R), value)
                    msgs[0][s * p.L + l] = value.astype(bf16)
    if first:
        for l in range(p.L):
            msgs[0][len(p.fields(0)) + l] = scale_index[l].astype(bf16)
    for l in range(p.L):
        for k in range(p.K):
            value = members[k, 0, l] * sent[0, l]
            for v in range(1, p.V):
                value = value + members[k, v, l] * sent[v, l]
            value = p.ens * value
            tile, lane = p.slot(k, l)
            scatter(back, tile, strided(lane, p.R), value)
            msgs[l + 1][k] = value.astype(bf16)


def sideways(u, first_lane, last_lane):
    zero = jnp.zeros_like(u[0])
    before = jnp.where(first_lane, zero, pltpu.roll(u[-1], 1, 1))
    after = jnp.where(last_lane, zero, pltpu.roll(u[0], LANES - 1, 1))
    around = [before] + list(u) + [after]
    return [around[i] + around[i + 2] for i in range(len(u))]


def stencil(above, here, below, side):
    across = side(here)
    return [(above[c] + below[c]) + across[c] - 4.0 * here[c] for c in range(len(here))]


def sweep_kernel(p, first, chunk, *refs):
    refs = list(refs)
    source_of, back, near, far = refs[:4]
    refs = refs[4:]
    builds = first and chunk == 0
    if builds:
        scale_index, *refs = refs
    else:
        kap, *refs = refs
    if chunk:
        members, level = source_of, chunk - 1
        rest, *refs = refs
    else:
        static_scale = source_of
    if not first:
        before, step, *refs = refs
    grad, norm, *refs = refs
    if chunk:
        part, ship, *refs = refs
    else:
        rest, *refs = refs
    if builds:
        kap, *refs = refs
    ends, a, b, out = refs
    me, at = lax.axis_index("mem"), lax.axis_index("row")
    low_ok = jnp.where(at > 0, 1.0, 0.0).astype(f32)
    high_ok = jnp.where(at < p.row - 1, 1.0, 0.0).astype(f32)
    R, RE, W = p.R, p.RE, SWEEPS
    H = 2 * W
    fields = p.fields(chunk)
    count = p.tiles(chunk)
    odd = lax.rem(at, 2)
    if p.pads:
        ends[...] = jnp.zeros(ends.shape, f32)

    def edge(value, side):
        if R == H:
            return value
        return jnp.where(side == 0, value[R - H :], value[:H])

    for ref, side in ((near, 1 - odd), (far, odd)):
        for i, (field, l) in enumerate(fields):
            tile, lane = p.inner(field, l)
            scatter(ends.at[side], tile, strided(lane, H), edge(ref[i].astype(f32), side))
    if builds:
        for l in range(p.L):
            pieces_of = [(table(scale_index[l], kappa_table), H)]
            for ref, side in ((near, 1 - odd), (far, odd)):
                value = table(edge(ref[len(fields) + l].astype(f32), side), kappa_table)
                pieces_of.append((value * jnp.where(side == 0, low_ok, high_ok), side * (H + R)))
            for value, offset in pieces_of:
                start = offset * SUB if isinstance(offset, int) else pl.multiple_of(offset * SUB, SUB)
                for r in range(value.shape[0]):
                    scatter(kap, l, pl.ds(start + r * SUB, SUB), jnp.broadcast_to(value[r : r + 1], (SUB, p.X)))
                for j in range(p.ST * SUB):
                    if (j % p.L) == l:
                        scatter(kap, p.L + j // SUB, strided(start + j % SUB, value.shape[0]), value)
    lane = lax.broadcasted_iota(jnp.int32, (SUB, LANES), 1)
    first_lane, last_lane = lane == 0, lane == LANES - 1
    side = functools.partial(sideways, first_lane=first_lane, last_lane=last_lane)
    cols = range(p.C)

    def tiles(ref, r, *lead):
        return [ref[(*lead, c, pl.ds(r * SUB, SUB), slice(None))] for c in cols]

    def keep(value, ref, r, *lead):
        for c in cols:
            ref[(*lead, c, pl.ds(r * SUB, SUB), slice(None))] = value[c]

    if not first:
        step_tile = jnp.broadcast_to(step[0:1, 0:1], (SUB, LANES))

    def problem(t, total):
        which, whole = (level, t + level * p.KT) if chunk else (t + p.L, t + p.PM)
        source = None
        for sweep in range(W):
            target = (a, b)[sweep % 2]
            held = []
            for r in range(sweep, RE - sweep):
                if sweep:
                    u = tiles(source, r)
                elif r < H:
                    u = tiles(ends, r, 0, t)
                elif r < H + R:
                    u = tiles(back, r - H, whole)
                else:
                    u = tiles(ends, r - H - R, 1, t)
                factor = tiles(kap, r, which)
                w = [factor[c] * u[c] for c in cols]
                held = (held + [(u, w)])[-3:]
                if len(held) < 3:
                    continue
                (_, w0), (u1, w1), (_, w2) = held
                change = stencil(w0, w1, w2, side)
                value = [u1[c] + change[c] for c in cols]
                if sweep < W - 1:
                    keep(value, target, r - 1)
                    continue
                if not first:
                    earlier = tiles(before, r - 1 - W, t)
                    value = [value[c] - step_tile * earlier[c] for c in cols]
                if r - 1 < H:
                    value = [one * low_ok for one in value]
                elif r - 1 >= H + R:
                    value = [one * high_ok for one in value]
                else:
                    for one in value:
                        total = total + one * one
                keep(value, grad, r - 1 - W, t)
            source = target
        for sweep in range(W):
            target = (a, b)[sweep % 2]
            held = []
            for r in range(W + sweep, RE - W - sweep):
                u = tiles(source, r) if sweep else tiles(grad, r - W, t)
                held = (held + [u])[-3:]
                if len(held) < 3:
                    continue
                change = stencil(*held, side)
                factor = tiles(kap, r - 1, which)
                value = [held[1][c] + factor[c] * change[c] for c in cols]
                if sweep < W - 1:
                    keep(value, target, r - 1)
                else:
                    keep(value, out, r - 1 - H, t)
            source = target
        return total

    total = lax.fori_loop(0, count, problem, jnp.zeros((SUB, LANES), f32))
    norm[...] = jnp.sum(total, axis=0, keepdims=True)
    if chunk == 0:
        for s in range(p.S):
            for l in range(p.L):
                tile, j = p.inner(p.K + s, l)
                rest[l, s] = p.stat * static_scale[s, l] * gather(out, tile, strided(j, R))
        return
    sums = [None] * p.V
    for k in range(p.K):
        tile, j = p.inner(k, level)
        spread = gather(out, tile, strided(j, R)).astype(bf16).astype(f32)
        for v in range(p.V):
            term = members[k, v, level] * spread
            sums[v] = term if k == 0 else sums[v] + term
    for v in range(p.V):
        part[v] = p.ens * sums[v]
    for s in range(p.S):
        own = me * p.S + s
        part[own] = part[own] + rest[level, s]
    if first:
        for v in range(p.V):
            ship[v] = part[v].astype(bf16)
        return
    for shift in range(1, p.mem):
        base = lax.rem(me + shift, p.mem) * p.S
        for s in range(p.S):
            ship[shift - 1, s] = part[base + s].astype(bf16)


def curvature_kernel(p, first, *refs):
    parts, gots, norms = refs[: p.L], refs[p.L : 2 * p.L], refs[2 * p.L : 3 * p.L + 1]
    refs = refs[3 * p.L + 1 :]
    if first:
        pack, _, image, send = refs
    else:
        pack, image_before, step, image, send = refs
    me = lax.axis_index("mem")
    total = jnp.zeros((p.R, p.X), f32)
    for l in range(p.L):
        if first:
            for v in range(p.V):
                value = parts[l][v]
                for other in range(p.mem - 1):
                    value = value + gots[l][other, v].astype(f32)
                image[v, l] = value
        for s in range(p.S):
            own = me * p.S + s
            if first:
                value = image[own, l]
                misfit = -pack[0, s, l]
            else:
                value = parts[l][own]
                for other in range(p.mem - 1):
                    value = value + gots[l][other, s].astype(f32)
                image[s, l] = value
                misfit = -(step[0:1, 0:1] * image_before[own, l]) - pack[0, s, l]
            index = pack[1, s, l]
            threshold = table(index, huber_levels)
            weight = jnp.where(index > 0, threshold / jnp.maximum(jnp.abs(misfit), threshold), 0.0)
            total = total + weight * value * value
    total = jnp.sum(total, axis=0, keepdims=True)
    total = sum(total[:, i * LANES : (i + 1) * LANES] for i in range(p.X // LANES))
    norm = sum(one[...] for one in norms)
    send[...] = jnp.broadcast_to(folded(norm, total)[None], send.shape)


def natural_kernel(p, matrix_ref, *refs):
    grads, (members_out, static_out) = refs[: p.chunks], refs[p.chunks :]
    targets, blocks = [], []
    for chunk in range(p.chunks):
        for field, l in p.fields(chunk):
            tile, lane = p.inner(field, l)
            blocks.append(gather(grads[chunk], tile, strided(SWEEPS * SUB + lane, p.R)))
            targets.append((members_out, field, l) if field < p.K else (static_out, field - p.K, l))
    (whole,) = products([jnp.concatenate(blocks, axis=0)], matrix_ref[...], True)
    for i, (ref, index, l) in enumerate(targets):
        ref[index, l] = whole[i * p.R : (i + 1) * p.R]


def final_kernel(p, got, step, image0, image1, matrix_ref, members0, static0, members1, static1, *outs):
    control, static_control, increment = outs
    me = lax.axis_index("mem")
    second = step_of(got)
    first = step[0:1, 0:1]
    rows = [(s, l) for s in range(p.S) for l in range(p.L)]
    blocks = [-(first * image0[me * p.S + s, l]) - second * image1[s, l] for s, l in rows]
    (whole,) = products([jnp.concatenate(blocks, axis=0)], matrix_ref[...], True)
    for l in range(p.L):
        for k in range(p.K):
            control[k, l] = -(first * members0[k, l]) - second * members1[k, l]
        for s in range(p.S):
            static_control[s, l] = -(first * static0[s, l]) - second * static1[s, l]
    for i, (s, l) in enumerate(rows):
        increment[s, l] = whole[i * p.R : (i + 1) * p.R]


def call(kernel, outs, scratch, far=0, cost=0, grant=8):
    vmem = pl.BlockSpec(memory_space=pltpu.VMEM)
    anywhere = pl.BlockSpec(memory_space=pltpu.MemorySpace.HBM)

    def run(*args):
        return pl.pallas_call(
            kernel,
            out_shape=tuple(jax.ShapeDtypeStruct(shape, dtype) for shape, dtype in outs),
            in_specs=[anywhere] * far + [vmem] * (len(args) - far),
            out_specs=tuple(vmem for _ in outs),
            scratch_shapes=scratch,
            compiler_params=pltpu.CompilerParams(vmem_limit_bytes=grant << 20),
            cost_estimate=pl.CostEstimate(flops=cost, bytes_accessed=cost, transcendentals=0),
        )(*[pltpu.with_memory_space_constraint(x, pltpu.MemorySpace.HBM) for x in args[:far]], *args[far:])

    return run


def local(members, static_scale, observed, huber_class, scale_index):
    p = Plan(members, static_scale, lax.axis_size("mem"), lax.axis_size("row"))
    K, V, L, R, X, S, C = p.K, p.V, p.L, p.R, p.X, p.S, p.C
    assert R >= 2 * SWEEPS and p.row % 2 == 0

    def round_mem(block, shift):
        return lax.ppermute(block, "mem", [(i, (i + shift) % p.mem) for i in range(p.mem)])

    def inside(block):
        return lax.ppermute(block, "row", [(i, i ^ 1) for i in range(p.row)])

    def across(block):
        n, pairs = p.row, []
        for m in range(p.mem):
            pairs += [(m * n + i, m * n + (i + 1 if i % 2 else i - 1)) for i in range(1, n - 1)]
            other = m ^ 1 if p.mem % 2 == 0 else m
            pairs += [(m * n + i, other * n + i) for i in (0, n - 1)]
        return lax.ppermute(block, ("mem", "row"), pairs)

    vmem = lambda shape: pltpu.VMEM(shape, f32)
    part = functools.partial
    shifts = range(1, p.mem)
    own_shape = (S, L, R, X)
    full_shape = (V, L, R, X)
    back_shape = (p.PN, C, R * SUB, LANES)
    send_shape = ((p.devices, 1, LANES), f32)
    line = ((1, LANES), f32)

    obs, cls, own = call(
        part(load_kernel, p), [(own_shape, f32), (own_shape, jnp.int32), (own_shape, bf16)],
        [pltpu.SemaphoreType.DMA((2,))], far=2,
    )(observed, huber_class)
    others = jnp.stack([round_mem(own, shift) for shift in shifts])
    scratch = [pltpu.VMEM(x.shape, x.dtype) for x in (members, static_scale, scale_index)]
    members, static_scale, scale_index, pack, own, matrix = call(
        part(fetch_kernel, p),
        [(members.shape, f32), (own_shape, f32), ((L, R, X), f32), ((2,) + own_shape, f32), (own_shape, bf16), ((X, X), bf16)],
        scratch + [pltpu.SemaphoreType.DMA((K + 2,))], far=3, cost=4 << 20, grant=20,
    )(members, static_scale, scale_index, obs, cls, own)
    pack_in = jnp.stack([round_mem(pack, shift) for shift in shifts])

    grads, naturals, image, step, kap, sums = [], [], None, None, None, None
    for turn in range(ITERS):
        first = turn == 0
        sizes = [len(p.fields(chunk)) for chunk in range(p.chunks)]
        if first:
            sizes[0] += L
        msg_shapes = [((size, R, X), bf16) for size in sizes]
        if first:
            back, *msgs = call(
                part(back_kernel, p, True), [(back_shape, f32)] + msg_shapes, [vmem(full_shape)],
            )(members, static_scale, scale_index, own, others, matrix)
        else:
            back, step, *msgs = call(
                part(back_kernel, p, False), [(back_shape, f32), line] + msg_shapes, [vmem(full_shape)],
            )(members, static_scale, pack, pack_in, image, sums)
        halos = []
        for msg in msgs:
            near = inside(msg)
            far = across(msg)
            halos.append((near, far))
        grad, norms, partial_images, gots, rest = [], [], [], [], None
        for chunk in range(p.chunks):
            count = p.tiles(chunk)
            builds = first and chunk == 0
            args = [members if chunk else static_scale, back, *halos[chunk], scale_index if builds else kap]
            args += [rest] if chunk else []
            args += [] if first else [grads[0][chunk], step]
            outs = [((count, C, p.RG * SUB, LANES), f32), line]
            if chunk:
                outs += [((V, R, X), f32), ((V, R, X) if first else (p.mem - 1, S, R, X), bf16)]
            else:
                outs.append(((L, S, R, X), f32))
            if builds:
                outs.append(((L + p.ST, C, p.RE * SUB, LANES), f32))
            halo = vmem((2, count, C, 2 * SWEEPS * SUB, LANES))
            work = [halo, vmem((C, p.RE * SUB, LANES)), vmem((C, p.RE * SUB, LANES))]
            g, norm, *more = call(
                part(sweep_kernel, p, first, chunk), outs, work + [vmem((count, C, R * SUB, LANES))],
                cost=8 << 20,
            )(*args)
            grad.append(g)
            norms.append(norm)
            if builds:
                rest, kap = more
            elif chunk == 0:
                (rest,) = more
            else:
                partial_image, ship = more
                partial_images.append(partial_image)
                gots.append(jnp.stack([round_mem(ship if first else ship[shift - 1], shift) for shift in shifts]))
        grads.append(grad)
        naturals += call(
            part(natural_kernel, p), [((K, L, R, X), f32), (own_shape, f32)], [], cost=4 << 20,
        )(matrix, *grad)
        if first:
            image, send = call(
                part(curvature_kernel, p, True), [(full_shape, f32), send_shape], [],
            )(*partial_images, *gots, *norms, pack, pack_in)
        else:
            final_image, send = call(
                part(curvature_kernel, p, False), [(own_shape, f32), send_shape], [],
            )(*partial_images, *gots, *norms, pack, image, step)
        sums = lax.all_to_all(send, ("mem", "row"), 0, 0)
    return call(
        part(final_kernel, p),
        [((K, L, R, X), f32), (own_shape, f32), (own_shape, f32)], [],
    )(sums, step, image, final_image, matrix, *naturals)


def solution(mesh):
    placed = (
        P("mem", None, None, "row", None),
        P("mem", None, "row", None),
        P("mem", None, "row", None),
        P("mem", None, "row", None),
        P(None, "row", None),
    )
    return jax.shard_map(
        local,
        mesh=mesh,
        in_specs=placed,
        out_specs=(
            P("mem", None, "row", None),
            P("mem", None, "row", None),
            P("mem", None, "row", None),
        ),
        check_vma=False,
    )
```
